32 devices in a mesh: comp: 4 (over z), lat: 8 (over y, x, core).
Axes of the slice: x: 2, y: 2, z: 4, core: 2. Of those that a mesh axis runs over, the one named last changes fastest.
Arguments:
- spectrum: float32 [1152, 16, 2048], P('comp', 'lat'), may hold values from 0.1 to 2
- courant_lat: float32 [1152], P('comp'), may hold values from -0.45 to 0.45
- courant_lon: float32 [1152], P('comp'), may hold values from -0.45 to 0.45
- sea_mask: int32 [16, 2048], P('lat'), may hold values from 0 to 1, as said below
- strength: float32 [1152], replicated, may hold values from 0.02 to 0.2
- quad_shift: int32 [4, 2], replicated, may hold values from -4 to 4
Outputs:
- spectrum_next: float32 [1152, 16, 2048], P('comp', 'lat')
The draws below stay inside these ranges and needn't reach their ends.
Inputs may be any that keep to these rules, and one draw needn't show every extreme that they name: `quad_shift`: column 0 offsets frequency, column 1 offsets direction. `sea_mask`: each aligned block of 2 rows holds at most 3072 sea points, and some block holds exactly 3072.
All inputs are finite; a program needn't handle non-finite values.
Results may differ from the reference program's by a relative error of at most 0.00002.
Values sent between devices are 32-bit elements; how exact they have to be, the bound alone decides.
No kernel may reach another device: no remote copies, remote signals or barrier semaphores. Data moves between devices by JAX's collectives and lax.ppermute only.
A program may use at most 64 MiB of HBM per device.

```python
import math
import jax
import jax.numpy as jnp
from jax import lax

NF = 36
ND = 32
NQ = 4
LAT_DEV = 2
LON = 2048
NC = 1152
LAT = 16


def draw_sea_mask(key, part):
    blocks = LAT // LAT_DEV
    points = LAT_DEV * LON
    most = 3 * points // 4
    key_counts = jax.random.fold_in(key, 11)
    key_top = jax.random.fold_in(key, 12)
    key_place = jax.random.fold_in(key, 13)
    counts = jax.random.randint(key_counts, (blocks,), most // 2, most + 1)
    top_block = jax.random.randint(key_top, (), 0, blocks)
    counts = jnp.where(jnp.arange(blocks) == top_block, most, counts)
    block_keys = jax.random.split(key_place, blocks)
    ranks = jax.vmap(lambda one: jax.random.permutation(one, points))(block_keys)
    marks = (ranks < counts[:, None]).astype(jnp.int32)
    return marks.reshape(LAT, LON)


def with_ends(array, stream_key, low, largest):
    spot = [jax.random.randint(jax.random.fold_in(stream_key, axis), (), 0, length) for axis, length in enumerate(array.shape)]
    main_axis = array.shape.index(max(array.shape))
    neighbour = spot[:main_axis] + [(spot[main_axis] + 1) % array.shape[main_axis]] + spot[main_axis + 1:]
    return array.at[tuple(spot)].set(low).at[tuple(neighbour)].set(largest)


def shard_levels(own_key, shape, cuts, smallest, largest):
    def one(position, blocks):
        draws = jax.random.uniform(jax.random.fold_in(jax.random.fold_in(own_key, 6), position), (blocks,), jnp.float32, smallest / len(cuts), largest / len(cuts))
        return jnp.repeat(jnp.exp(draws), shape[position] // blocks).reshape((-1,) + (1,) * (len(shape) - position - 1))

    loudness = one(*cuts[0])
    for cut in cuts[1:]:
        loudness = loudness * one(*cut)
    return loudness


def setup_inputs(seed: int = 0) -> dict:
    keys = jax.random.split(jax.random.key(seed), 7)
    spectrum = jnp.clip(0.1 + 1.9 * jax.random.uniform(keys[0], (NC, LAT, LON), jnp.float32) ** shard_levels(keys[0], (NC, LAT, LON), ((0, 4), (1, 8)), -0.2, 0.2), 0.1, 2.0)
    courant_lat = jnp.clip(jax.random.uniform(keys[1], (NC,), jnp.float32, -0.45, 0.45) * shard_levels(keys[1], (NC,), ((0, 4),), -0.4, 0.0), -0.45, 0.45)
    courant_lon = jnp.clip(jax.random.uniform(keys[2], (NC,), jnp.float32, -0.45, 0.45) * shard_levels(keys[2], (NC,), ((0, 4),), -0.4, 0.0), -0.45, 0.45)
    sea_mask = draw_sea_mask(jax.random.fold_in(keys[6], 71), 0)
    strength = jnp.clip(jnp.exp(jax.random.uniform(keys[4], (NC,), jnp.float32, math.log(0.02), math.log(0.2))), 0.02, 0.2)
    quad_shift = with_ends(jax.random.randint(keys[5], (NQ, 2), -4, 5), jax.random.fold_in(keys[5], 1), -4, 4).astype(jnp.int32)
    return {"spectrum": spectrum, "courant_lat": courant_lat, "courant_lon": courant_lon, "sea_mask": sea_mask, "strength": strength, "quad_shift": quad_shift}


reach = 4


def upwind(field, along_lat, along_lon, maskf):
    padded = jnp.pad(field, ((0, 0), (1, 1), (0, 0)))
    south = padded[:, :-2, :]
    north = padded[:, 2:, :]
    west = jnp.roll(field, 1, axis=2)
    east = jnp.roll(field, -1, axis=2)
    plus_a = jnp.maximum(along_lat, 0.0)
    minus_a = jnp.minimum(along_lat, 0.0)
    plus_b = jnp.maximum(along_lon, 0.0)
    minus_b = jnp.minimum(along_lon, 0.0)
    moved = field - plus_a * (field - south) - minus_a * (north - field)
    moved = moved - plus_b * (field - west) - minus_b * (east - field)
    return moved * maskf


def interact(energy, strength, quad_shift):
    rest = energy.shape[1:]
    grid = energy.reshape((NF, ND) + rest)
    widths = ((reach, reach),) + ((0, 0),) * (grid.ndim - 1)
    padded = jnp.pad(grid, widths)
    total = jnp.zeros(grid.shape, jnp.float32)
    for index in range(NQ):
        offset_f = quad_shift[index, 0].astype(jnp.int32)
        offset_d = quad_shift[index, 1].astype(jnp.int32)
        partner = lax.dynamic_slice_in_dim(padded, reach + offset_f, NF, 0)
        partner = jnp.roll(partner, -offset_d, axis=1)
        total = total + partner * (partner - grid)
    coeff = strength.reshape((NF, ND) + (1,) * len(rest))
    return (coeff * grid * total).reshape(energy.shape)


def reference(spectrum, courant_lat, courant_lon, sea_mask, strength, quad_shift):
    maskf = sea_mask.astype(jnp.float32)[None]
    along_lat = courant_lat[:, None, None]
    along_lon = courant_lon[:, None, None]
    field = upwind(spectrum, along_lat, along_lon, maskf)
    field = upwind(field, along_lat, along_lon, maskf)
    rows = jnp.transpose(field, (1, 0, 2))
    updated = lax.map(lambda row: row + interact(row, strength, quad_shift), rows)
    return jnp.transpose(updated, (1, 0, 2))
```

```python
import jax
import jax.numpy as jnp
from jax import lax
from jax.sharding import PartitionSpec as P
from jax.experimental import pallas as pl
from jax.experimental.pallas import tpu as pltpu

NF = 36
ND = 32
NQ = 4


reach = 4


def extended(cells, sides, width):
    for axis, dim in sides:
        count = lax.axis_size(axis)
        ends = count - 1
        head = lax.slice_in_dim(cells, 0, width, axis=dim)
        tail = lax.slice_in_dim(cells, cells.shape[dim] - width, cells.shape[dim], axis=dim)
        cells = jnp.concatenate(
            [
                lax.ppermute(tail, axis, [(i, (i + 1) % count) for i in range(ends)]),
                cells,
                lax.ppermute(head, axis, [((i + 1) % count, i) for i in range(ends)]),
            ],
            axis=dim,
        )
    return cells


def upwind(field, along_lat, along_lon, maskf):
    padded = extended(field, (("lat", 1),), 1)
    south = padded[:, :-2, :]
    north = padded[:, 2:, :]
    west = jnp.roll(field, 1, axis=2)
    east = jnp.roll(field, -1, axis=2)
    plus_a = jnp.maximum(along_lat, 0.0)
    minus_a = jnp.minimum(along_lat, 0.0)
    plus_b = jnp.maximum(along_lon, 0.0)
    minus_b = jnp.minimum(along_lon, 0.0)
    moved = field - plus_a * (field - south) - minus_a * (north - field)
    moved = moved - plus_b * (field - west) - minus_b * (east - field)
    return moved * maskf


def interact(energy, strength, quad_shift):
    rest = energy.shape[1:]
    grid = energy.reshape((NF, ND) + rest)
    widths = ((reach, reach),) + ((0, 0),) * (grid.ndim - 1)
    padded = jnp.pad(grid, widths)
    total = jnp.zeros(grid.shape, jnp.float32)
    for index in range(NQ):
        offset_f = quad_shift[index, 0]
        offset_d = quad_shift[index, 1]
        partner = lax.dynamic_slice_in_dim(padded, reach + offset_f, NF, 0)
        partner = jnp.roll(partner, -offset_d, axis=1)
        total = total + partner * (partner - grid)
    coeff = strength.reshape((NF, ND) + (1,) * len(rest))
    return (coeff * grid * total).reshape(energy.shape)


def gathered_plan(spectrum, courant_lat, courant_lon, sea_mask, strength, quad_shift):
    maskf = sea_mask.astype(jnp.float32)[None]
    along_lat = courant_lat[:, None, None]
    along_lon = courant_lon[:, None, None]
    field = upwind(spectrum, along_lat, along_lon, maskf)
    field = upwind(field, along_lat, along_lon, maskf)
    comp_dev, lat_dev, lon_count = field.shape
    point_count = lat_dev * lon_count
    flat = field.reshape(comp_dev, point_count)
    sea_most = 3 * point_count // 4
    land_first = 1 - sea_mask.reshape(point_count)
    ordering = jnp.argsort(land_first, stable=True)
    chosen = ordering[:sea_most]
    packed = jnp.take(flat, chosen, axis=1)
    spectra = lax.all_to_all(packed, "comp", split_axis=1, concat_axis=0, tiled=True)
    updated = spectra + interact(spectra, strength, quad_shift)
    returned = lax.all_to_all(updated, "comp", split_axis=0, concat_axis=1, tiled=True)
    result = jnp.zeros((comp_dev, point_count), jnp.float32).at[:, chosen].set(returned)
    return result.reshape(comp_dev, lat_dev, lon_count)


LANES = 128
SMEM = pltpu.SMEM
VMEM = pltpu.VMEM
ANY = pl.ANY
STEP = 16


def tiled(cells):
    comp_dev, lat_dev, lon_count = cells.shape
    blocks = lon_count // LANES
    cells = cells.reshape(comp_dev, lat_dev, blocks, LANES).transpose(0, 2, 1, 3)
    return cells.reshape(comp_dev, blocks * lat_dev, LANES)


def untiled(cells, lat_dev):
    comp_dev, rows, _ = cells.shape
    blocks = rows // lat_dev
    cells = cells.reshape(comp_dev, blocks, lat_dev, LANES).transpose(0, 2, 1, 3)
    return cells.reshape(comp_dev, lat_dev, blocks * LANES)


def chunk_block(freqs):
    per = ND // STEP
    first = freqs[0]
    stride = freqs[1] - freqs[0] if len(freqs) > 1 else 0
    return lambda g: ((first + (g // per) * stride) * per + g % per, 0, 0)


def cost(flops, count):
    return pl.CostEstimate(flops=flops, bytes_accessed=count, transcendentals=0)


def pack_message(own, mate, along_lat, place, freqs, mate_whole):
    rows = own.shape[1]
    per = ND // STEP
    steps = len(freqs) * per
    where_own = chunk_block(freqs)
    here = lambda g: (g, 0, 0)

    def kernel(a_ref, place_ref, own_ref, mate_ref, out_ref):
        block = where_own(pl.program_id(0))[0]
        odd = place_ref[0] > 0

        def one(i, carry):
            from_own = (a_ref[block * STEP + i] > 0) == odd
            out_ref[i] = jnp.where(from_own, own_ref[i], mate_ref[i])
            return carry

        lax.fori_loop(0, STEP, one, 0, unroll=4)

    shape = (STEP, rows, LANES)
    return pl.pallas_call(
        kernel,
        out_shape=jax.ShapeDtypeStruct((len(freqs) * ND, rows, LANES), jnp.float32),
        grid=(steps,),
        in_specs=[
            pl.BlockSpec(memory_space=SMEM),
            pl.BlockSpec(memory_space=SMEM),
            pl.BlockSpec(shape, where_own),
            pl.BlockSpec(shape, where_own if mate_whole else here),
        ],
        out_specs=pl.BlockSpec(shape, here),
        cost_estimate=cost(0, 3 * len(freqs) * ND * rows * LANES * 4),
        name="pack_message",
    )(along_lat, place, own, mate)


def propagate(own, mate, side, relay, along_lat, along_lon, place, masks, freqs, mate_whole):
    rows = own.shape[1]
    per = ND // STEP
    steps = len(freqs) * per
    where_own = chunk_block(freqs)
    here = lambda g: (g, 0, 0)
    outs = len(freqs)

    def kernel(a_ref, b_ref, place_ref, mask_ref, own_ref, mate_ref, side_ref, relay_ref, *out_refs):
        step_id = pl.program_id(0)
        block = where_own(step_id)[0]
        odd = place_ref[0] > 0
        relayed = place_ref[1] > 0
        sub = lax.broadcasted_iota(jnp.int32, (rows, LANES), 0) & 1
        lane = lax.broadcasted_iota(jnp.int32, (rows, LANES), 1)
        own_mask = mask_ref[0]

        def swap(x):
            return jnp.where(sub == 0, pltpu.roll(x, rows - 1, 0), pltpu.roll(x, 1, 0))

        def west(x):
            turned = pltpu.roll(x, 1, 1)
            return jnp.where(lane == 0, pltpu.roll(turned, 2, 0), turned)

        def east(x):
            turned = pltpu.roll(x, LANES - 1, 1)
            return jnp.where(lane == LANES - 1, pltpu.roll(turned, rows - 2, 0), turned)

        def moved(x, before, beside, a, b, mask):
            return (x - a * (x - before) - b * (x - beside)) * mask

        def one(i, carry):
            a = a_ref[block * STEP + i]
            b = b_ref[block * STEP + i]
            south = a > 0
            near = south == odd
            a = jnp.abs(a)

            def run(shift, size):
                x = own_ref[i]
                far = jnp.where(relayed, relay_ref[i], side_ref[i])
                halo = jnp.where(near, mate_ref[i], far)
                halo_mask = jnp.where(south, mask_ref[1], mask_ref[2])
                cross = sub == jnp.where(south, 0, 1)
                halo_back = swap(halo)
                first = moved(x, jnp.where(cross, halo_back, swap(x)), shift(x), a, size, own_mask)
                halo_first = moved(halo, halo_back, shift(halo), a, size, halo_mask)
                second = moved(first, jnp.where(cross, swap(halo_first), swap(first)), shift(first), a, size, own_mask)
                if outs == 1:
                    out_refs[0][i] = second
                else:
                    for which in range(outs):
                        @pl.when(step_id // per == which)
                        def _():
                            out_refs[which][i] = second

            @pl.when(b > 0)
            def _():
                run(west, b)

            @pl.when(b <= 0)
            def _():
                run(east, -b)

            return carry

        lax.fori_loop(0, STEP, one, 0)

    shape = (STEP, rows, LANES)
    out_specs = [
        pl.BlockSpec(shape, lambda g, which=which: (jnp.clip(g - which * per, 0, per - 1), 0, 0))
        for which in range(outs)
    ]
    return pl.pallas_call(
        kernel,
        out_shape=[jax.ShapeDtypeStruct((ND, rows, LANES), jnp.float32)] * outs,
        grid=(steps,),
        in_specs=[
            pl.BlockSpec(memory_space=SMEM),
            pl.BlockSpec(memory_space=SMEM),
            pl.BlockSpec(memory_space=SMEM),
            pl.BlockSpec((3, rows, LANES), lambda g: (0, 0, 0)),
            pl.BlockSpec(shape, where_own),
            pl.BlockSpec(shape, where_own if mate_whole else here),
            pl.BlockSpec(shape, here),
            pl.BlockSpec(shape, here),
        ],
        out_specs=out_specs,
        cost_estimate=cost(40 * len(freqs) * ND * rows * LANES, 5 * len(freqs) * ND * rows * LANES * 4),
        name="propagate",
    )(along_lat, along_lon, place, masks, own, mate, side, relay)


def quadruplets(window, strength, quad_shift, local, start, stride, count, into):
    rows = window[0].shape[1]
    used = sorted({start + i * stride + p + reach for i in range(count) for p in range(-reach, reach + 1)})
    per = 2
    half = ND // per

    def kernel(strength_ref, shift_ref, *refs):
        sources = refs[: len(used)]
        out_ref = refs[-3]
        held, sems = refs[-2], refs[-1]
        g = pl.program_id(0)
        f = start + (g // per) * stride
        d0 = (g % per) * half

        @pl.when(g == 0)
        def _():
            copies = [
                pltpu.make_async_copy(sources[n], held.at[pl.ds(w * ND, ND)], sems.at[n])
                for n, w in enumerate(used)
            ]
            for one in copies:
                one.start()
            for one in copies:
                one.wait()

        def one(i, carry):
            d = d0 + i
            energy = held[(f + reach) * ND + d]
            total = jnp.zeros_like(energy)
            for q in range(NQ):
                turned = lax.rem(d + shift_ref[q, 1] + ND, ND)
                partner = held[(f + reach + shift_ref[q, 0]) * ND + turned]
                total = total + partner * (partner - energy)
            out_ref[i] = energy + strength_ref[f * ND + d] * energy * total
            return carry

        lax.fori_loop(0, half, one, 0, unroll=4)

    in_specs = [pl.BlockSpec(memory_space=SMEM)] * 2 + [pl.BlockSpec(memory_space=ANY)] * len(used)
    operands = [strength, quad_shift] + [window[w] for w in used]
    aliases = {}
    if into is not None:
        aliases = {len(operands): 0}
        in_specs = in_specs + [pl.BlockSpec(memory_space=ANY)]
        operands = operands + [into]
    return pl.pallas_call(
        kernel,
        out_shape=jax.ShapeDtypeStruct((local * ND, rows, LANES), jnp.float32),
        grid=(count * per,),
        in_specs=in_specs,
        out_specs=pl.BlockSpec((half, rows, LANES), lambda g: ((start + (g // per) * stride) * per + g % per, 0, 0)),
        scratch_shapes=[
            VMEM(((local + 2 * reach) * ND, rows, LANES), jnp.float32),
            pltpu.SemaphoreType.DMA((len(used),)),
        ],
        input_output_aliases=aliases,
        cost_estimate=cost(15 * count * ND * rows * LANES, (len(used) + count) * ND * rows * LANES * 4),
        name="quadruplets",
    )(*operands)


def halo_plan(spectrum, courant_lat, courant_lon, sea_mask, strength, quad_shift):
    comp_dev, lat_dev, _ = spectrum.shape
    local = comp_dev // ND
    lat_count = lax.axis_size("lat")
    comp_count = lax.axis_size("comp")
    at = lax.axis_index("lat")
    strength = lax.dynamic_slice_in_dim(strength, lax.axis_index("comp") * comp_dev, comp_dev)
    mates = [(i, i ^ 1) for i in range(lat_count)]
    sides = [(i, i + 1) for i in range(1, lat_count, 4)] + [(i + 1, i) for i in range(1, lat_count, 4)]
    relays = [(i - 2, i + 1) for i in range(3, lat_count - 1, 4)] + [(i + 3, i) for i in range(3, lat_count - 1, 4)]
    place = jnp.stack([at % 2, jnp.where((at % 4 == 0) | (at % 4 == 3), 1, 0)]).astype(jnp.int32)
    up = [(i, i + 1) for i in range(lat_count - 1)]
    down = [(i + 1, i) for i in range(lat_count - 1)]
    z_up = [(i, i + 1) for i in range(comp_count - 1)]
    z_down = [(i + 1, i) for i in range(comp_count - 1)]

    own = tiled(spectrum)
    rows = own.shape[1]
    maskf = tiled(sea_mask.astype(jnp.float32)[None])
    masks = jnp.concatenate([maskf, lax.ppermute(maskf, "lat", up), lax.ppermute(maskf, "lat", down)])

    pairs = [(c, local - 1 - c) for c in range(reach)]
    middle = list(range(reach, local - reach))
    chunks = [list(pair) for pair in pairs] + ([middle] if middle else [])
    head = jnp.concatenate([own[f * ND:(f + 1) * ND] for f in chunks[0]])
    mate_head = lax.ppermute(head, "lat", mates)
    mate = lax.ppermute(own, "lat", mates)
    sides_in = []
    for n, freqs in enumerate(chunks):
        message = pack_message(own, mate if n else mate_head, courant_lat, place, freqs, n > 0)
        sides_in.append(lax.ppermute(message, "lat", sides))
    relays_in = [lax.ppermute(side, "lat", relays) for side in sides_in]
    window = [None] * (local + 2 * reach)
    for n, freqs in enumerate(chunks):
        parts = propagate(
            own, mate if n else mate_head, sides_in[n], relays_in[n], courant_lat, courant_lon, place, masks, freqs, n > 0
        )
        for f, part in zip(freqs, parts):
            window[reach + f] = part
        if n < reach:
            low, high = parts
            window[reach - 1 - n] = lax.ppermute(high, "comp", z_up)
            window[reach + local + n] = lax.ppermute(low, "comp", z_down)
    inner = quadruplets(window, strength, quad_shift, local, 1, 1, local - 2, None)
    result = quadruplets(window, strength, quad_shift, local, 0, local - 1, 2, inner)
    return untiled(result, lat_dev)


def per_device(spectrum, courant_lat, courant_lon, sea_mask, strength, quad_shift):
    comp_dev, lat_dev, lon_count = spectrum.shape
    whole_freqs = comp_dev % ND == 0 and comp_dev // ND >= 2 * reach and comp_dev // ND - 2 * reach <= 2
    square = lax.axis_size("lat") % 4 == 0
    if whole_freqs and square and lat_dev == 2 and lon_count % LANES == 0:
        return halo_plan(spectrum, courant_lat, courant_lon, sea_mask, strength, quad_shift)
    return gathered_plan(spectrum, courant_lat, courant_lon, sea_mask, strength, quad_shift)


def solution(mesh):
    return jax.shard_map(
        per_device,
        mesh=mesh,
        in_specs=(P("comp", "lat", None), P("comp"), P("comp"), P("lat", None), P(), P()),
        out_specs=P("comp", "lat", None),
        check_vma=False,
    )
```

```python
import jax
import jax.numpy as jnp
from jax import lax
from jax.sharding import PartitionSpec as P
from jax.experimental import pallas as pl
from jax.experimental.pallas import tpu as pltpu

NF = 36
ND = 32
NQ = 4


reach = 4


def extended(cells, sides, width):
    for axis, dim in sides:
        count = lax.axis_size(axis)
        ends = count - 1
        head = lax.slice_in_dim(cells, 0, width, axis=dim)
        tail = lax.slice_in_dim(cells, cells.shape[dim] - width, cells.shape[dim], axis=dim)
        cells = jnp.concatenate(
            [
                lax.ppermute(tail, axis, [(i, (i + 1) % count) for i in range(ends)]),
                cells,
                lax.ppermute(head, axis, [((i + 1) % count, i) for i in range(ends)]),
            ],
            axis=dim,
        )
    return cells


def upwind(field, along_lat, along_lon, maskf):
    padded = extended(field, (("lat", 1),), 1)
    south = padded[:, :-2, :]
    north = padded[:, 2:, :]
    west = jnp.roll(field, 1, axis=2)
    east = jnp.roll(field, -1, axis=2)
    plus_a = jnp.maximum(along_lat, 0.0)
    minus_a = jnp.minimum(along_lat, 0.0)
    plus_b = jnp.maximum(along_lon, 0.0)
    minus_b = jnp.minimum(along_lon, 0.0)
    moved = field - plus_a * (field - south) - minus_a * (north - field)
    moved = moved - plus_b * (field - west) - minus_b * (east - field)
    return moved * maskf


def interact(energy, strength, quad_shift):
    rest = energy.shape[1:]
    grid = energy.reshape((NF, ND) + rest)
    widths = ((reach, reach),) + ((0, 0),) * (grid.ndim - 1)
    padded = jnp.pad(grid, widths)
    total = jnp.zeros(grid.shape, jnp.float32)
    for index in range(NQ):
        offset_f = quad_shift[index, 0]
        offset_d = quad_shift[index, 1]
        partner = lax.dynamic_slice_in_dim(padded, reach + offset_f, NF, 0)
        partner = jnp.roll(partner, -offset_d, axis=1)
        total = total + partner * (partner - grid)
    coeff = strength.reshape((NF, ND) + (1,) * len(rest))
    return (coeff * grid * total).reshape(energy.shape)


def gathered_plan(spectrum, courant_lat, courant_lon, sea_mask, strength, quad_shift):
    maskf = sea_mask.astype(jnp.float32)[None]
    along_lat = courant_lat[:, None, None]
    along_lon = courant_lon[:, None, None]
    field = upwind(spectrum, along_lat, along_lon, maskf)
    field = upwind(field, along_lat, along_lon, maskf)
    comp_dev, lat_dev, lon_count = field.shape
    point_count = lat_dev * lon_count
    flat = field.reshape(comp_dev, point_count)
    sea_most = 3 * point_count // 4
    land_first = 1 - sea_mask.reshape(point_count)
    ordering = jnp.argsort(land_first, stable=True)
    chosen = ordering[:sea_most]
    packed = jnp.take(flat, chosen, axis=1)
    spectra = lax.all_to_all(packed, "comp", split_axis=1, concat_axis=0, tiled=True)
    updated = spectra + interact(spectra, strength, quad_shift)
    returned = lax.all_to_all(updated, "comp", split_axis=0, concat_axis=1, tiled=True)
    result = jnp.zeros((comp_dev, point_count), jnp.float32).at[:, chosen].set(returned)
    return result.reshape(comp_dev, lat_dev, lon_count)


LANES = 128
PAIR = 2


def vmem(shape):
    return pltpu.VMEM(shape, jnp.float32)


def near_core(cells):
    return pltpu.with_memory_space_constraint(cells, pltpu.VMEM)


def whole(space):
    return pl.BlockSpec(memory_space=space)


def limits(mib):
    return pltpu.CompilerParams(vmem_limit_bytes=mib * 2**20)


def cost(flops, count):
    return pl.CostEstimate(flops=flops, bytes_accessed=count, transcendentals=0)


def tiled(cells):
    comp_dev, lat_dev, lon_count = cells.shape
    blocks = lon_count // LANES
    cells = cells.reshape(comp_dev, lat_dev, blocks, LANES).transpose(0, 2, 1, 3)
    return cells.reshape(comp_dev, blocks * lat_dev, LANES)


def untiled(cells, lat_dev):
    comp_dev, rows, _ = cells.shape
    blocks = rows // lat_dev
    cells = cells.reshape(comp_dev, blocks, lat_dev, LANES).transpose(0, 2, 1, 3)
    return cells.reshape(comp_dev, lat_dev, blocks * LANES)


def load(own, chunks):
    spots = [(c, n, f) for c, freqs in enumerate(chunks) for n, f in enumerate(freqs)]
    rows = own.shape[1]

    def kernel(own_ref, *refs):
        sems = refs[-1]
        copies = [
            pltpu.make_async_copy(own_ref.at[pl.ds(f * ND, ND)], refs[c].at[pl.ds(n * ND, ND)], sems.at[m])
            for m, (c, n, f) in enumerate(spots)
        ]
        for one in copies:
            one.start()
        for one in copies:
            one.wait()

    return pl.pallas_call(
        kernel,
        out_shape=[vmem((len(freqs) * ND, rows, LANES)) for freqs in chunks],
        in_specs=[whole(pltpu.HBM)],
        out_specs=[whole(pltpu.VMEM)] * len(chunks),
        scratch_shapes=[pltpu.SemaphoreType.DMA((len(spots),))],
        compiler_params=limits(8),
        cost_estimate=cost(0, 2 * len(spots) * ND * rows * LANES * 4),
        name="load",
    )(pltpu.with_memory_space_constraint(own, pltpu.HBM))


def pack_message(own, mate, along_lat, place, freqs):
    rows = own.shape[1]

    def kernel(a_ref, place_ref, own_ref, mate_ref, out_ref):
        odd = place_ref[0] > 0
        for n, f in enumerate(freqs):
            def one(i, carry):
                k = f * ND + i
                j = n * ND + i
                from_own = (a_ref[k] > 0) == odd
                out_ref[j] = jnp.where(from_own, own_ref[j], mate_ref[j])
                return carry

            lax.fori_loop(0, ND, one, 0, unroll=4)

    return pl.pallas_call(
        kernel,
        out_shape=vmem((len(freqs) * ND, rows, LANES)),
        in_specs=[whole(pltpu.SMEM)] * 2 + [whole(pltpu.VMEM)] * 2,
        out_specs=whole(pltpu.VMEM),
        compiler_params=limits(8),
        cost_estimate=cost(0, 3 * len(freqs) * ND * rows * LANES * 4),
        name="pack_message",
    )(along_lat, place, near_core(own), near_core(mate))


def propagate(own, mate, side, relay, along_lat, along_lon, place, masks, freqs):
    rows = own.shape[1]
    half = rows // PAIR

    def kernel(a_ref, b_ref, place_ref, mask_ref, own_ref, mate_ref, side_ref, relay_ref, *out_refs):
        odd = place_ref[0] > 0
        relayed = place_ref[1] > 0
        lane = lax.broadcasted_iota(jnp.int32, (half, LANES), 1)

        def run(far_ref):
            for n, f in enumerate(freqs):
                def one(i, carry):
                    k = f * ND + i
                    j = n * ND + i
                    a = a_ref[k]
                    b = b_ref[k]
                    south = a > 0
                    near = south == odd
                    west = b > 0
                    fore = jnp.where(south, 0, 1)
                    back = 1 - fore
                    turn = jnp.where(west, 1, LANES - 1)
                    edge = lane == jnp.where(west, 0, LANES - 1)
                    a = jnp.abs(a)
                    b = jnp.abs(b)

                    def row(ref, at, which):
                        return ref[at, pl.ds(which, half, stride=PAIR), :]

                    def beside(x):
                        turned = pltpu.roll(x, turn, 1)
                        over = jnp.where(west, pltpu.roll(turned, 1, 0), pltpu.roll(turned, half - 1, 0))
                        return jnp.where(edge, over, turned)

                    def moved(x, before, mask):
                        return (x - a * (x - before) - b * (x - beside(x))) * mask

                    x0 = jnp.where(near, row(mate_ref, j, fore), row(far_ref, j, fore))
                    x1 = jnp.where(near, row(mate_ref, j, back), row(far_ref, j, back))
                    x2 = row(own_ref, j, fore)
                    x3 = row(own_ref, j, back)
                    y1 = moved(x1, x0, mask_ref[2 + fore])
                    y2 = moved(x2, x1, mask_ref[fore])
                    y3 = moved(x3, x2, mask_ref[back])
                    z2 = moved(y2, y1, mask_ref[fore])
                    z3 = moved(y3, y2, mask_ref[back])
                    out_refs[n][i, pl.ds(fore, half, stride=PAIR), :] = z2
                    out_refs[n][i, pl.ds(back, half, stride=PAIR), :] = z3
                    return carry

                lax.fori_loop(0, ND, one, 0, unroll=2)

        @pl.when(relayed)
        def _():
            run(relay_ref)

        @pl.when(jnp.logical_not(relayed))
        def _():
            run(side_ref)

    operands = [along_lat, along_lon, place] + [near_core(x) for x in (masks, own, mate, side, relay)]
    in_specs = [whole(pltpu.SMEM)] * 3 + [whole(pltpu.VMEM)] * 5
    return pl.pallas_call(
        kernel,
        out_shape=[vmem((ND, rows, LANES))] * len(freqs),
        in_specs=in_specs,
        out_specs=[whole(pltpu.VMEM)] * len(freqs),
        compiler_params=limits(8),
        cost_estimate=cost(40 * len(freqs) * ND * rows * LANES, 5 * len(freqs) * ND * rows * LANES * 4),
        name="propagate",
    )(*operands)


def quadruplets(window, parts, places, local, strength, shifts, first, freqs, into):
    rows = parts[0].shape[1]
    count = len(parts)

    def kernel(strength_ref, shift_ref, first_ref, *refs):
        part_refs = refs[:count]
        held_ref, out_ref, done, sems, part_sems = refs[-5:]
        arrivals = [
            pltpu.make_async_copy(part_refs[n], held_ref.at[pl.ds(place * ND, ND)], part_sems.at[n])
            for n, place in enumerate(places)
        ]
        for one in arrivals:
            one.start()
        for one in arrivals:
            one.wait()
        base = first_ref[0]
        copies = []
        for n, f in enumerate(freqs):
            def one(d, carry):
                energy = held_ref[(f + reach) * ND + d]
                total = jnp.zeros_like(energy)
                for q in range(NQ):
                    turned = lax.rem(d + shift_ref[1, q] + ND, ND)
                    partner = held_ref[(f + reach + shift_ref[0, q]) * ND + turned]
                    total = total + partner * (partner - energy)
                done[n * ND + d] = energy + strength_ref[base + f * ND + d] * energy * total
                return carry

            lax.fori_loop(0, ND, one, 0, unroll=4)
            copies.append(
                pltpu.make_async_copy(done.at[pl.ds(n * ND, ND)], out_ref.at[pl.ds(f * ND, ND)], sems.at[n])
            )
            copies[-1].start()
        for one in copies:
            one.wait()

    operands = [strength, shifts, first] + parts
    in_specs = [whole(pltpu.SMEM)] * 3 + [whole(pl.ANY)] * count
    aliases = {}
    if window is not None:
        aliases = {len(operands): 0, len(operands) + 1: 1}
        operands += [near_core(window), into]
        in_specs += [whole(pltpu.VMEM), whole(pl.ANY)]
    return pl.pallas_call(
        kernel,
        out_shape=[
            vmem(((local + 2 * reach) * ND, rows, LANES)),
            jax.ShapeDtypeStruct((local * ND, rows, LANES), jnp.float32),
        ],
        in_specs=in_specs,
        out_specs=[whole(pltpu.VMEM), whole(pl.ANY)],
        scratch_shapes=[
            pltpu.VMEM((len(freqs) * ND, rows, LANES), jnp.float32),
            pltpu.SemaphoreType.DMA((len(freqs),)),
            pltpu.SemaphoreType.DMA((count,)),
        ],
        input_output_aliases=aliases,
        compiler_params=limits(8),
        cost_estimate=cost(15 * len(freqs) * ND * rows * LANES, 6 * len(freqs) * ND * rows * LANES * 4),
        name="quadruplets",
    )(*operands)


def halo_plan(spectrum, courant_lat, courant_lon, sea_mask, strength, quad_shift):
    comp_dev, lat_dev, _ = spectrum.shape
    local = comp_dev // ND
    lat_count = lax.axis_size("lat")
    comp_count = lax.axis_size("comp")
    at = lax.axis_index("lat")
    first = (lax.axis_index("comp") * comp_dev)[None].astype(jnp.int32)
    mates = [(i, i ^ 1) for i in range(lat_count)]
    sides = [(i, i + 1) for i in range(1, lat_count, 4)] + [(i + 1, i) for i in range(1, lat_count, 4)]
    relays = [(i - 2, i + 1) for i in range(3, lat_count - 1, 4)] + [(i + 3, i) for i in range(3, lat_count - 1, 4)]
    place = jnp.stack([at % 2, jnp.where((at % 4 == 0) | (at % 4 == 3), 1, 0)]).astype(jnp.int32)
    up = [(i, i + 1) for i in range(lat_count - 1)]
    down = [(i + 1, i) for i in range(lat_count - 1)]
    z_up = [(i, i + 1) for i in range(comp_count - 1)]
    z_down = [(i + 1, i) for i in range(comp_count - 1)]

    own = tiled(spectrum)
    rows = own.shape[1]
    maskf = sea_mask.astype(jnp.float32).reshape(lat_dev, rows // lat_dev, LANES)

    pairs = [(c, local - 1 - c) for c in range(reach)]
    middle = list(range(reach, local - reach))
    chunks = [list(pair) for pair in pairs] + ([middle] if middle else [])
    owns = load(own, chunks[:1]) + load(own, chunks[1:])
    mask_south = lax.ppermute(maskf[1:], "lat", up)
    mask_north = lax.ppermute(maskf[:1], "lat", down)
    masks = jnp.concatenate([maskf, mask_south, mask_north])
    mates_in = [lax.ppermute(part, "lat", mates) for part in owns]
    sides_in = [
        lax.ppermute(pack_message(owns[n], mates_in[n], courant_lat, place, freqs), "lat", sides)
        for n, freqs in enumerate(chunks)
    ]
    relays_in = [lax.ppermute(side, "lat", relays) for side in sides_in]
    parts = []
    places = []
    last = []
    for n, freqs in enumerate(chunks):
        made = propagate(
            owns[n], mates_in[n], sides_in[n], relays_in[n], courant_lat, courant_lon, place, masks, freqs
        )
        parts += made
        places += [reach + f for f in freqs]
        if n < reach:
            low, high = made
            last = [lax.ppermute(high, "comp", z_up), lax.ppermute(low, "comp", z_down)]
            last_places = [reach - 1 - n, reach + local + n]
            if n < reach - 1:
                parts += last
                places += last_places
    shifts = quad_shift.T
    window, inner = quadruplets(
        None, parts, places, local, strength, shifts, first, list(range(1, local - 1)), None
    )
    window, result = quadruplets(
        window, last, last_places, local, strength, shifts, first, [0, local - 1], inner
    )
    return untiled(result, lat_dev)


def fits(comp_dev, lat_count, lat_dev, lon_count):
    local, left = divmod(comp_dev, ND)
    return left == 0 and 0 < local - 2 * reach <= 1 and lat_count % 4 == 0 and lat_dev == 2 and lon_count % LANES == 0


def per_device(spectrum, courant_lat, courant_lon, sea_mask, strength, quad_shift):
    comp_dev, lat_dev, lon_count = spectrum.shape
    if fits(comp_dev, lax.axis_size("lat"), lat_dev, lon_count):
        return halo_plan(spectrum, courant_lat, courant_lon, sea_mask, strength, quad_shift)
    return gathered_plan(spectrum, courant_lat, courant_lon, sea_mask, strength, quad_shift)


def solution(mesh):
    return jax.shard_map(
        per_device,
        mesh=mesh,
        in_specs=(P("comp", "lat", None), P("comp"), P("comp"), P("lat", None), P(), P()),
        out_specs=P("comp", "lat", None),
        check_vma=False,
    )
```

```python
import jax
import jax.numpy as jnp
from jax import lax
from jax.sharding import PartitionSpec as P
from jax.experimental import pallas as pl
from jax.experimental.pallas import tpu as pltpu

NF = 36
ND = 32
NQ = 4


reach = 4


def extended(cells, sides, width):
    for axis, dim in sides:
        count = lax.axis_size(axis)
        ends = count - 1
        head = lax.slice_in_dim(cells, 0, width, axis=dim)
        tail = lax.slice_in_dim(cells, cells.shape[dim] - width, cells.shape[dim], axis=dim)
        cells = jnp.concatenate(
            [
                lax.ppermute(tail, axis, [(i, (i + 1) % count) for i in range(ends)]),
                cells,
                lax.ppermute(head, axis, [((i + 1) % count, i) for i in range(ends)]),
            ],
            axis=dim,
        )
    return cells


def upwind(field, along_lat, along_lon, maskf):
    padded = extended(field, (("lat", 1),), 1)
    south = padded[:, :-2, :]
    north = padded[:, 2:, :]
    west = jnp.roll(field, 1, axis=2)
    east = jnp.roll(field, -1, axis=2)
    plus_a = jnp.maximum(along_lat, 0.0)
    minus_a = jnp.minimum(along_lat, 0.0)
    plus_b = jnp.maximum(along_lon, 0.0)
    minus_b = jnp.minimum(along_lon, 0.0)
    moved = field - plus_a * (field - south) - minus_a * (north - field)
    moved = moved - plus_b * (field - west) - minus_b * (east - field)
    return moved * maskf


def interact(energy, strength, quad_shift):
    rest = energy.shape[1:]
    grid = energy.reshape((NF, ND) + rest)
    widths = ((reach, reach),) + ((0, 0),) * (grid.ndim - 1)
    padded = jnp.pad(grid, widths)
    total = jnp.zeros(grid.shape, jnp.float32)
    for index in range(NQ):
        offset_f = quad_shift[index, 0]
        offset_d = quad_shift[index, 1]
        partner = lax.dynamic_slice_in_dim(padded, reach + offset_f, NF, 0)
        partner = jnp.roll(partner, -offset_d, axis=1)
        total = total + partner * (partner - grid)
    coeff = strength.reshape((NF, ND) + (1,) * len(rest))
    return (coeff * grid * total).reshape(energy.shape)


def gathered_plan(spectrum, courant_lat, courant_lon, sea_mask, strength, quad_shift):
    maskf = sea_mask.astype(jnp.float32)[None]
    along_lat = courant_lat[:, None, None]
    along_lon = courant_lon[:, None, None]
    field = upwind(spectrum, along_lat, along_lon, maskf)
    field = upwind(field, along_lat, along_lon, maskf)
    comp_dev, lat_dev, lon_count = field.shape
    point_count = lat_dev * lon_count
    flat = field.reshape(comp_dev, point_count)
    sea_most = 3 * point_count // 4
    land_first = 1 - sea_mask.reshape(point_count)
    ordering = jnp.argsort(land_first, stable=True)
    chosen = ordering[:sea_most]
    packed = jnp.take(flat, chosen, axis=1)
    spectra = lax.all_to_all(packed, "comp", split_axis=1, concat_axis=0, tiled=True)
    updated = spectra + interact(spectra, strength, quad_shift)
    returned = lax.all_to_all(updated, "comp", split_axis=0, concat_axis=1, tiled=True)
    result = jnp.zeros((comp_dev, point_count), jnp.float32).at[:, chosen].set(returned)
    return result.reshape(comp_dev, lat_dev, lon_count)


LANES = 128
PAIR = 2


def vmem(shape):
    return pltpu.VMEM(shape, jnp.float32)


def near_core(cells):
    return pltpu.with_memory_space_constraint(cells, pltpu.VMEM)


def far_from_core(cells):
    return pltpu.with_memory_space_constraint(cells, pltpu.HBM)


def whole(space):
    return pl.BlockSpec(memory_space=space)


def limits(mib):
    return pltpu.CompilerParams(vmem_limit_bytes=mib * 2**20)


def cost(flops, count):
    return pl.CostEstimate(flops=flops, bytes_accessed=count, transcendentals=0)


def tiled(cells):
    comp_dev, lat_dev, lon_count = cells.shape
    blocks = lon_count // LANES
    cells = cells.reshape(comp_dev, lat_dev, blocks, LANES).transpose(0, 2, 1, 3)
    return cells.reshape(comp_dev, blocks * lat_dev, LANES)


def untiled(cells, lat_dev):
    comp_dev, rows, _ = cells.shape
    blocks = rows // lat_dev
    cells = cells.reshape(comp_dev, blocks, lat_dev, LANES).transpose(0, 2, 1, 3)
    return cells.reshape(comp_dev, lat_dev, blocks * LANES)


def load(own, chunks, extra=None):
    spots = [(c, n, f) for c, freqs in enumerate(chunks) for n, f in enumerate(freqs)]
    rows = own.shape[1]
    ends = [len(freqs) * ND for freqs in chunks]
    sizes = list(ends)
    operands = [own]
    if extra is not None:
        sizes[0] += 1
        operands.append(extra)

    def kernel(own_ref, *refs):
        sems = refs[-1]
        out_refs = refs[len(operands) - 1:-1]
        copies = [
            pltpu.make_async_copy(own_ref.at[pl.ds(f * ND, ND)], out_refs[c].at[pl.ds(n * ND, ND)], sems.at[m])
            for m, (c, n, f) in enumerate(spots)
        ]
        for one in copies:
            one.start()
        if extra is not None:
            out_refs[0][ends[0]] = refs[0][0]
        for one in copies:
            one.wait()

    return pl.pallas_call(
        kernel,
        out_shape=[vmem((size, rows, LANES)) for size in sizes],
        in_specs=[whole(pltpu.HBM)] + [whole(pltpu.VMEM)] * (len(operands) - 1),
        out_specs=[whole(pltpu.VMEM)] * len(chunks),
        scratch_shapes=[pltpu.SemaphoreType.DMA((len(spots),))],
        compiler_params=limits(8),
        cost_estimate=cost(0, 2 * len(spots) * ND * rows * LANES * 4),
        name="load",
    )(far_from_core(own), *operands[1:])


def pack_first(own, mate, along_lat, place, freqs):
    rows = own.shape[1]
    size = len(freqs) * ND

    def kernel(a_ref, place_ref, own_ref, mate_ref, out_ref):
        odd = place_ref[0] > 0
        for n, f in enumerate(freqs):
            def one(i, carry):
                j = n * ND + i
                from_own = (a_ref[f * ND + i] > 0) == odd
                out_ref[j] = jnp.where(from_own, own_ref[j], mate_ref[j])
                return carry

            lax.fori_loop(0, ND, one, 0, unroll=8)
        out_ref[size] = own_ref[size]
        out_ref[size + 1] = mate_ref[size]

    return pl.pallas_call(
        kernel,
        out_shape=vmem((size + 2, rows, LANES)),
        in_specs=[whole(pltpu.SMEM)] * 2 + [whole(pltpu.VMEM)] * 2,
        out_specs=whole(pltpu.VMEM),
        compiler_params=limits(8),
        cost_estimate=cost(0, 3 * size * rows * LANES * 4),
        name="pack_first",
    )(along_lat, place, near_core(own), near_core(mate))


def pack_message(own, other, along_lat, place, freqs):
    rows = own.shape[1]

    def kernel(a_ref, place_ref, own_ref, other_ref, out_ref, held_ref, sems):
        odd = place_ref[0] > 0
        copies = [
            pltpu.make_async_copy(own_ref.at[pl.ds(f * ND, ND)], held_ref.at[pl.ds(n * ND, ND)], sems.at[n])
            for n, f in enumerate(freqs)
        ]
        for one in copies:
            one.start()
        for n, f in enumerate(freqs):
            copies[n].wait()

            def one(i, carry):
                j = n * ND + i
                from_own = (a_ref[f * ND + i] > 0) == odd
                out_ref[j] = jnp.where(from_own, held_ref[j], other_ref[j])
                return carry

            lax.fori_loop(0, ND, one, 0, unroll=8)

    shape = (len(freqs) * ND, rows, LANES)
    return pl.pallas_call(
        kernel,
        out_shape=vmem(shape),
        in_specs=[whole(pltpu.SMEM)] * 2 + [whole(pltpu.HBM), whole(pltpu.VMEM)],
        out_specs=whole(pltpu.VMEM),
        scratch_shapes=[vmem(shape), pltpu.SemaphoreType.DMA((len(freqs),))],
        compiler_params=limits(8),
        cost_estimate=cost(0, 3 * len(freqs) * ND * rows * LANES * 4),
        name="pack_message",
    )(along_lat, place, far_from_core(own), near_core(other))


def propagate(own, mate, side, hand, along_lat, along_lon, place, masks, freqs):
    rows = own.shape[1]
    half = rows // PAIR
    size = len(freqs) * ND

    def kernel(a_ref, b_ref, place_ref, mask_ref, own_hbm, mate_hbm, side_ref, hand_ref, *refs):
        out_refs = refs[:len(freqs)]
        own_ref, mate_ref, done_ref, sems, out_sems = refs[len(freqs):]
        odd = place_ref[0] > 0
        handed = place_ref[1] > 0
        lane = lax.broadcasted_iota(jnp.int32, (half, LANES), 1)
        arrivals = [
            [
                pltpu.make_async_copy(src.at[pl.ds(f * ND, ND)], dst.at[pl.ds(n * ND, ND)], sems.at[n, m])
                for m, (src, dst) in enumerate(((own_hbm, own_ref), (mate_hbm, mate_ref)))
            ]
            for n, f in enumerate(freqs)
        ]
        for pair in arrivals:
            for one in pair:
                one.start()
        leaving = [
            pltpu.make_async_copy(done_ref.at[pl.ds(n * ND, ND)], out_refs[n], out_sems.at[n])
            for n in range(len(freqs))
        ]

        def run(far_ref, n, f):
            def one(i, carry):
                k = f * ND + i
                j = n * ND + i
                a = a_ref[k]
                b = b_ref[k]
                south = a > 0
                near = south == odd
                west = b > 0
                fore = jnp.where(south, 0, 1)
                back = 1 - fore
                turn = jnp.where(west, 1, LANES - 1)
                edge = lane == jnp.where(west, 0, LANES - 1)
                a = jnp.abs(a)
                b = jnp.abs(b)

                def row(ref, at, which):
                    return ref[at, pl.ds(which, half, stride=PAIR), :]

                def beside(x):
                    turned = pltpu.roll(x, turn, 1)
                    over = jnp.where(west, pltpu.roll(turned, 1, 0), pltpu.roll(turned, half - 1, 0))
                    return jnp.where(edge, over, turned)

                def moved(x, before, mask):
                    return (x - a * (x - before) - b * (x - beside(x))) * mask

                fore_mask = row(mask_ref, 0, fore)
                back_mask = row(mask_ref, 0, back)
                x0 = jnp.where(near, row(mate_ref, j, fore), row(far_ref, j, fore))
                x1 = jnp.where(near, row(mate_ref, j, back), row(far_ref, j, back))
                x2 = row(own_ref, j, fore)
                x3 = row(own_ref, j, back)
                y1 = moved(x1, x0, row(mask_ref, jnp.where(near, 1, 2), back))
                y2 = moved(x2, x1, fore_mask)
                y3 = moved(x3, x2, back_mask)
                done_ref[j, pl.ds(fore, half, stride=PAIR), :] = moved(y2, y1, fore_mask)
                done_ref[j, pl.ds(back, half, stride=PAIR), :] = moved(y3, y2, back_mask)
                return carry

            lax.fori_loop(0, ND, one, 0, unroll=4)

        for n, f in enumerate(freqs):
            for one in arrivals[n]:
                one.wait()

            @pl.when(handed)
            def _():
                run(hand_ref, n, f)

            @pl.when(jnp.logical_not(handed))
            def _():
                run(side_ref, n, f)

            leaving[n].start()
        for one in leaving:
            one.wait()

    return pl.pallas_call(
        kernel,
        out_shape=[jax.ShapeDtypeStruct((ND, rows, LANES), jnp.float32)] * len(freqs),
        in_specs=[whole(pltpu.SMEM)] * 3 + [whole(pltpu.VMEM)] + [whole(pltpu.HBM)] * 2 + [whole(pltpu.VMEM)] * 2,
        out_specs=[whole(pltpu.HBM)] * len(freqs),
        scratch_shapes=[vmem((size, rows, LANES))] * 3
        + [pltpu.SemaphoreType.DMA((len(freqs), 2)), pltpu.SemaphoreType.DMA((len(freqs),))],
        compiler_params=limits(8),
        cost_estimate=cost(40 * size * rows * LANES, 5 * size * rows * LANES * 4),
        name="propagate",
    )(
        along_lat, along_lon, place, near_core(masks),
        far_from_core(own), far_from_core(mate), near_core(side), near_core(hand),
    )


def quadruplets(window, parts, places, local, strength, shifts, first, freqs, into):
    rows = parts[0].shape[1]
    count = len(parts)

    def kernel(strength_ref, shift_ref, first_ref, *refs):
        part_refs = refs[:count]
        held_ref, out_ref, done, sems, part_sems = refs[-5:]
        arrivals = [
            pltpu.make_async_copy(part_refs[n], held_ref.at[pl.ds(place * ND, ND)], part_sems.at[n])
            for n, place in enumerate(places)
        ]
        for one in arrivals:
            one.start()
        for one in arrivals:
            one.wait()
        base = first_ref[0]
        copies = []
        for n, f in enumerate(freqs):
            def one(d, carry):
                energy = held_ref[(f + reach) * ND + d]
                total = jnp.zeros_like(energy)
                for q in range(NQ):
                    turned = lax.rem(d + shift_ref[1, q] + ND, ND)
                    partner = held_ref[(f + reach + shift_ref[0, q]) * ND + turned]
                    total = total + partner * (partner - energy)
                done[n * ND + d] = energy + strength_ref[base + f * ND + d] * energy * total
                return carry

            lax.fori_loop(0, ND, one, 0, unroll=4)
            copies.append(
                pltpu.make_async_copy(done.at[pl.ds(n * ND, ND)], out_ref.at[pl.ds(f * ND, ND)], sems.at[n])
            )
            copies[-1].start()
        for one in copies:
            one.wait()

    operands = [strength, shifts, first] + parts
    in_specs = [whole(pltpu.SMEM)] * 3 + [whole(pl.ANY)] * count
    aliases = {}
    if window is not None:
        aliases = {len(operands): 0, len(operands) + 1: 1}
        operands += [near_core(window), into]
        in_specs += [whole(pltpu.VMEM), whole(pl.ANY)]
    return pl.pallas_call(
        kernel,
        out_shape=[
            vmem(((local + 2 * reach) * ND, rows, LANES)),
            jax.ShapeDtypeStruct((local * ND, rows, LANES), jnp.float32),
        ],
        in_specs=in_specs,
        out_specs=[whole(pltpu.VMEM), whole(pl.ANY)],
        scratch_shapes=[
            pltpu.VMEM((len(freqs) * ND, rows, LANES), jnp.float32),
            pltpu.SemaphoreType.DMA((len(freqs),)),
            pltpu.SemaphoreType.DMA((count,)),
        ],
        input_output_aliases=aliases,
        compiler_params=limits(8),
        cost_estimate=cost(15 * len(freqs) * ND * rows * LANES, 6 * len(freqs) * ND * rows * LANES * 4),
        name="quadruplets",
    )(*operands)


def halo_plan(spectrum, courant_lat, courant_lon, sea_mask, strength, quad_shift):
    comp_dev, lat_dev, _ = spectrum.shape
    local = comp_dev // ND
    lat_count = lax.axis_size("lat")
    comp_count = lax.axis_size("comp")
    at = lax.axis_index("lat")
    first = (lax.axis_index("comp") * comp_dev)[None].astype(jnp.int32)
    mates = [(i, i ^ 1) for i in range(lat_count)]
    corners = range(3, lat_count - 1, 4)
    sides = [(i, i + 1) for i in range(1, lat_count, 4)] + [(i + 1, i) for i in range(1, lat_count, 4)]
    relays = [(i - 2, i + 1) for i in corners] + [(i + 3, i) for i in corners]
    aheads = [(i, i + 3) for i in corners] + [(i + 1, i - 2) for i in corners]
    hands = [(i + 2, i + 1) for i in corners] + [(i - 1, i) for i in corners]
    handed = (at % 4 == 0) | (at % 4 == 3)
    place = jnp.stack([at % 2, jnp.where(handed, 1, 0)]).astype(jnp.int32)
    z_up = [(i, i + 1) for i in range(comp_count - 1)]
    z_down = [(i + 1, i) for i in range(comp_count - 1)]

    own = tiled(spectrum)
    mask = tiled(sea_mask.astype(jnp.float32)[None])

    pairs = [(c, local - 1 - c) for c in range(reach)]
    middle = list(range(reach, local - reach))
    chunks = [list(pair) for pair in pairs] + ([middle] if middle else [])
    (head,) = load(own, chunks[:1], mask)
    mate_head = lax.ppermute(head, "lat", mates)
    ahead = [None] + [lax.ppermute(part, "lat", aheads) for part in load(own, chunks[1:])]
    mate = lax.ppermute(own, "lat", mates)
    sides_in = [lax.ppermute(pack_first(head, mate_head, courant_lat, place, chunks[0]), "lat", sides)]
    hands_in = [lax.ppermute(sides_in[0], "lat", relays)]
    for n, freqs in enumerate(chunks):
        if n:
            message = pack_message(own, ahead[n], courant_lat, place, freqs)
            sides_in.append(lax.ppermute(message, "lat", sides))
            hands_in.append(lax.ppermute(sides_in[n], "lat", hands))
    size = len(chunks[0]) * ND
    masks = jnp.concatenate([
        mask, mate_head[size:], jnp.where(handed, hands_in[0][size + 1:], sides_in[0][size:size + 1])
    ])
    parts = []
    places = []
    last = []
    for n, freqs in enumerate(chunks):
        made = propagate(
            own, mate, sides_in[n], hands_in[n], courant_lat, courant_lon, place, masks, freqs
        )
        parts += made
        places += [reach + f for f in freqs]
        if n < reach:
            low, high = made
            last = [lax.ppermute(high, "comp", z_up), lax.ppermute(low, "comp", z_down)]
            last_places = [reach - 1 - n, reach + local + n]
            if n < reach - 1:
                parts += last
                places += last_places
    shifts = quad_shift.T
    window, inner = quadruplets(
        None, parts, places, local, strength, shifts, first, list(range(1, local - 1)), None
    )
    window, result = quadruplets(
        window, last, last_places, local, strength, shifts, first, [0, local - 1], inner
    )
    return untiled(result, lat_dev)


def fits(comp_dev, lat_count, lat_dev, lon_count):
    local, left = divmod(comp_dev, ND)
    return left == 0 and 0 < local - 2 * reach <= 1 and lat_count % 4 == 0 and lat_dev == 2 and lon_count % LANES == 0


def per_device(spectrum, courant_lat, courant_lon, sea_mask, strength, quad_shift):
    comp_dev, lat_dev, lon_count = spectrum.shape
    if fits(comp_dev, lax.axis_size("lat"), lat_dev, lon_count):
        return halo_plan(spectrum, courant_lat, courant_lon, sea_mask, strength, quad_shift)
    return gathered_plan(spectrum, courant_lat, courant_lon, sea_mask, strength, quad_shift)


def solution(mesh):
    return jax.shard_map(
        per_device,
        mesh=mesh,
        in_specs=(P("comp", "lat", None), P("comp"), P("comp"), P("lat", None), P(), P()),
        out_specs=P("comp", "lat", None),
        check_vma=False,
    )
```

```python
import jax
import jax.numpy as jnp
from jax import lax
from jax.sharding import PartitionSpec as P
from jax.experimental import pallas as pl
from jax.experimental.pallas import tpu as pltpu

NF = 36
ND = 32
NQ = 4


reach = 4


def extended(cells, sides, width):
    for axis, dim in sides:
        count = lax.axis_size(axis)
        ends = count - 1
        head = lax.slice_in_dim(cells, 0, width, axis=dim)
        tail = lax.slice_in_dim(cells, cells.shape[dim] - width, cells.shape[dim], axis=dim)
        cells = jnp.concatenate(
            [
                lax.ppermute(tail, axis, [(i, (i + 1) % count) for i in range(ends)]),
                cells,
                lax.ppermute(head, axis, [((i + 1) % count, i) for i in range(ends)]),
            ],
            axis=dim,
        )
    return cells


def upwind(field, along_lat, along_lon, maskf):
    padded = extended(field, (("lat", 1),), 1)
    south = padded[:, :-2, :]
    north = padded[:, 2:, :]
    west = jnp.roll(field, 1, axis=2)
    east = jnp.roll(field, -1, axis=2)
    plus_a = jnp.maximum(along_lat, 0.0)
    minus_a = jnp.minimum(along_lat, 0.0)
    plus_b = jnp.maximum(along_lon, 0.0)
    minus_b = jnp.minimum(along_lon, 0.0)
    moved = field - plus_a * (field - south) - minus_a * (north - field)
    moved = moved - plus_b * (field - west) - minus_b * (east - field)
    return moved * maskf


def interact(energy, strength, quad_shift):
    rest = energy.shape[1:]
    grid = energy.reshape((NF, ND) + rest)
    widths = ((reach, reach),) + ((0, 0),) * (grid.ndim - 1)
    padded = jnp.pad(grid, widths)
    total = jnp.zeros(grid.shape, jnp.float32)
    for index in range(NQ):
        offset_f = quad_shift[index, 0]
        offset_d = quad_shift[index, 1]
        partner = lax.dynamic_slice_in_dim(padded, reach + offset_f, NF, 0)
        partner = jnp.roll(partner, -offset_d, axis=1)
        total = total + partner * (partner - grid)
    coeff = strength.reshape((NF, ND) + (1,) * len(rest))
    return (coeff * grid * total).reshape(energy.shape)


def gathered_plan(spectrum, courant_lat, courant_lon, sea_mask, strength, quad_shift):
    maskf = sea_mask.astype(jnp.float32)[None]
    along_lat = courant_lat[:, None, None]
    along_lon = courant_lon[:, None, None]
    field = upwind(spectrum, along_lat, along_lon, maskf)
    field = upwind(field, along_lat, along_lon, maskf)
    comp_dev, lat_dev, lon_count = field.shape
    point_count = lat_dev * lon_count
    flat = field.reshape(comp_dev, point_count)
    sea_most = 3 * point_count // 4
    land_first = 1 - sea_mask.reshape(point_count)
    ordering = jnp.argsort(land_first, stable=True)
    chosen = ordering[:sea_most]
    packed = jnp.take(flat, chosen, axis=1)
    spectra = lax.all_to_all(packed, "comp", split_axis=1, concat_axis=0, tiled=True)
    updated = spectra + interact(spectra, strength, quad_shift)
    returned = lax.all_to_all(updated, "comp", split_axis=0, concat_axis=1, tiled=True)
    result = jnp.zeros((comp_dev, point_count), jnp.float32).at[:, chosen].set(returned)
    return result.reshape(comp_dev, lat_dev, lon_count)


LANES = 128
PAIR = 2


def vmem(shape):
    return pltpu.VMEM(shape, jnp.float32)


def near_core(cells):
    return pltpu.with_memory_space_constraint(cells, pltpu.VMEM)


def far_from_core(cells):
    return pltpu.with_memory_space_constraint(cells, pltpu.HBM)


def whole(space):
    return pl.BlockSpec(memory_space=space)


def limits(mib):
    return pltpu.CompilerParams(vmem_limit_bytes=mib * 2**20)


def cost(flops, count):
    return pl.CostEstimate(flops=flops, bytes_accessed=count, transcendentals=0)


def tiled(cells):
    comp_dev, lat_dev, lon_count = cells.shape
    blocks = lon_count // LANES
    cells = cells.reshape(comp_dev, lat_dev, blocks, LANES).transpose(0, 2, 1, 3)
    return cells.reshape(comp_dev, blocks * lat_dev, LANES)


def untiled(cells, lat_dev):
    comp_dev, rows, _ = cells.shape
    blocks = rows // lat_dev
    cells = cells.reshape(comp_dev, blocks, lat_dev, LANES).transpose(0, 2, 1, 3)
    return cells.reshape(comp_dev, lat_dev, blocks * LANES)


def load(own, chunks, extra=None):
    spots = [(c, n, f) for c, freqs in enumerate(chunks) for n, f in enumerate(freqs)]
    rows = own.shape[1]
    ends = [len(freqs) * ND for freqs in chunks]
    sizes = list(ends)
    operands = [own]
    if extra is not None:
        sizes[0] += 1
        operands.append(extra)

    def kernel(own_ref, *refs):
        sems = refs[-1]
        out_refs = refs[len(operands) - 1:-1]
        copies = [
            pltpu.make_async_copy(own_ref.at[pl.ds(f * ND, ND)], out_refs[c].at[pl.ds(n * ND, ND)], sems.at[m])
            for m, (c, n, f) in enumerate(spots)
        ]
        for one in copies:
            one.start()
        if extra is not None:
            out_refs[0][ends[0]] = refs[0][0].astype(jnp.float32)
        for one in copies:
            one.wait()

    return pl.pallas_call(
        kernel,
        out_shape=[vmem((size, rows, LANES)) for size in sizes],
        in_specs=[whole(pltpu.HBM)] + [whole(pltpu.VMEM)] * (len(operands) - 1),
        out_specs=[whole(pltpu.VMEM)] * len(chunks),
        scratch_shapes=[pltpu.SemaphoreType.DMA((len(spots),))],
        compiler_params=limits(8),
        cost_estimate=cost(0, 2 * len(spots) * ND * rows * LANES * 4),
        name="load",
    )(far_from_core(own), *operands[1:])


def pack_first(own, mate, along_lat, place, freqs):
    rows = own.shape[1]
    size = len(freqs) * ND

    def kernel(a_ref, place_ref, own_ref, mate_ref, out_ref):
        odd = place_ref[0] > 0
        for n, f in enumerate(freqs):
            def one(i, carry):
                j = n * ND + i
                from_own = (a_ref[f * ND + i] > 0) == odd
                out_ref[j] = jnp.where(from_own, own_ref[j], mate_ref[j])
                return carry

            lax.fori_loop(0, ND, one, 0, unroll=8)
        out_ref[size] = own_ref[size]
        out_ref[size + 1] = mate_ref[size]

    return pl.pallas_call(
        kernel,
        out_shape=vmem((size + 2, rows, LANES)),
        in_specs=[whole(pltpu.SMEM)] * 2 + [whole(pltpu.VMEM)] * 2,
        out_specs=whole(pltpu.VMEM),
        compiler_params=limits(8),
        cost_estimate=cost(0, 3 * size * rows * LANES * 4),
        name="pack_first",
    )(along_lat, place, near_core(own), near_core(mate))


def pack_message(own, other, along_lat, place, freqs):
    rows = own.shape[1]

    def kernel(a_ref, place_ref, own_ref, other_ref, out_ref, held_ref, sems):
        odd = place_ref[0] > 0
        copies = [
            pltpu.make_async_copy(own_ref.at[pl.ds(f * ND, ND)], held_ref.at[pl.ds(n * ND, ND)], sems.at[n])
            for n, f in enumerate(freqs)
        ]
        for one in copies:
            one.start()
        for n, f in enumerate(freqs):
            copies[n].wait()

            def one(i, carry):
                j = n * ND + i
                from_own = (a_ref[f * ND + i] > 0) == odd
                out_ref[j] = jnp.where(from_own, held_ref[j], other_ref[j])
                return carry

            lax.fori_loop(0, ND, one, 0, unroll=8)

    shape = (len(freqs) * ND, rows, LANES)
    return pl.pallas_call(
        kernel,
        out_shape=vmem(shape),
        in_specs=[whole(pltpu.SMEM)] * 2 + [whole(pltpu.HBM), whole(pltpu.VMEM)],
        out_specs=whole(pltpu.VMEM),
        scratch_shapes=[vmem(shape), pltpu.SemaphoreType.DMA((len(freqs),))],
        compiler_params=limits(8),
        cost_estimate=cost(0, 3 * len(freqs) * ND * rows * LANES * 4),
        name="pack_message",
    )(along_lat, place, far_from_core(own), near_core(other))


def propagate(own, mate, side, hand, along_lat, along_lon, place, masks, freqs, picked=False, skip=0):
    rows = own.shape[1]
    half = rows // PAIR
    size = len(freqs) * ND

    def kernel(a_ref, b_ref, place_ref, mask_ref, own_hbm, mate_hbm, side_ref, hand_ref, *refs):
        out_refs = refs[:len(freqs)]
        own_ref, mate_ref, done_ref, sems, out_sems = refs[len(freqs):]
        odd = place_ref[0] > 0
        handed = place_ref[1] > 0
        lane = lax.broadcasted_iota(jnp.int32, (half, LANES), 1)
        arrivals = [
            [
                pltpu.make_async_copy(
                    src.at[pl.ds((n if picked else f) * ND, ND)], dst.at[pl.ds(n * ND, ND)], sems.at[n, m]
                )
                for m, (src, dst) in enumerate(((own_hbm, own_ref), (mate_hbm, mate_ref)))
            ]
            for n, f in enumerate(freqs)
        ]
        for pair in arrivals:
            for one in pair:
                one.start()
        leaving = [
            pltpu.make_async_copy(done_ref.at[pl.ds(n * ND, ND)], out_refs[n], out_sems.at[n])
            for n in range(len(freqs))
        ]

        def run(far_ref, n, f):
            def one(i, carry):
                k = f * ND + i
                j = n * ND + i
                a = a_ref[k]
                b = b_ref[k]
                south = a > 0
                near = south == odd
                west = b > 0
                fore = jnp.where(south, 0, 1)
                back = 1 - fore
                turn = jnp.where(west, 1, LANES - 1)
                edge = lane == jnp.where(west, 0, LANES - 1)
                a = jnp.abs(a)
                b = jnp.abs(b)

                def row(ref, at, which):
                    return ref[at, pl.ds(which, half, stride=PAIR), :]

                def beside(x):
                    turned = pltpu.roll(x, turn, 1)
                    over = jnp.where(west, pltpu.roll(turned, 1, 0), pltpu.roll(turned, half - 1, 0))
                    return jnp.where(edge, over, turned)

                def moved(x, before, mask):
                    return (x - a * (x - before) - b * (x - beside(x))) * mask

                fore_mask = row(mask_ref, 0, fore)
                back_mask = row(mask_ref, 0, back)
                x0 = jnp.where(near, row(mate_ref, j, fore), row(far_ref, skip * ND + j, fore))
                x1 = jnp.where(near, row(mate_ref, j, back), row(far_ref, skip * ND + j, back))
                x2 = row(own_ref, j, fore)
                x3 = row(own_ref, j, back)
                y1 = moved(x1, x0, row(mask_ref, jnp.where(near, 1, 2), back))
                y2 = moved(x2, x1, fore_mask)
                y3 = moved(x3, x2, back_mask)
                done_ref[j, pl.ds(fore, half, stride=PAIR), :] = moved(y2, y1, fore_mask)
                done_ref[j, pl.ds(back, half, stride=PAIR), :] = moved(y3, y2, back_mask)
                return carry

            lax.fori_loop(0, ND, one, 0, unroll=4)

        for n, f in enumerate(freqs):
            for one in arrivals[n]:
                one.wait()

            @pl.when(handed)
            def _():
                run(hand_ref, n, f)

            @pl.when(jnp.logical_not(handed))
            def _():
                run(side_ref, n, f)

            leaving[n].start()
        for one in leaving:
            one.wait()

    return pl.pallas_call(
        kernel,
        out_shape=[jax.ShapeDtypeStruct((ND, rows, LANES), jnp.float32)] * len(freqs),
        in_specs=[whole(pltpu.SMEM)] * 3 + [whole(pltpu.VMEM)] + [whole(pl.ANY if picked else pltpu.HBM), whole(pl.ANY)]
        + [whole(pltpu.VMEM)] * 2,
        out_specs=[whole(pltpu.HBM)] * len(freqs),
        scratch_shapes=[vmem((size, rows, LANES))] * 3
        + [pltpu.SemaphoreType.DMA((len(freqs), 2)), pltpu.SemaphoreType.DMA((len(freqs),))],
        compiler_params=limits(8),
        cost_estimate=cost(40 * size * rows * LANES, 5 * size * rows * LANES * 4),
        name="propagate",
    )(
        along_lat, along_lon, place, near_core(masks),
        own if picked else far_from_core(own), mate, near_core(side), near_core(hand),
    )


def quadruplets(window, parts, places, local, strength, shifts, first, freqs, into):
    rows = parts[0].shape[1]
    count = len(parts)

    def kernel(strength_ref, shift_ref, first_ref, *refs):
        part_refs = refs[:count]
        held_ref, out_ref, done, sems, part_sems = refs[-5:]
        arrivals = [
            pltpu.make_async_copy(part_refs[n], held_ref.at[pl.ds(place * ND, ND)], part_sems.at[n])
            for n, place in enumerate(places)
        ]
        for one in arrivals:
            one.start()
        for one in arrivals:
            one.wait()
        base = first_ref[0]
        copies = []
        for n, f in enumerate(freqs):
            def one(d, carry):
                energy = held_ref[(f + reach) * ND + d]
                total = jnp.zeros_like(energy)
                for q in range(NQ):
                    turned = lax.rem(d + shift_ref[1, q] + ND, ND)
                    partner = held_ref[(f + reach + shift_ref[0, q]) * ND + turned]
                    total = total + partner * (partner - energy)
                done[n * ND + d] = energy + strength_ref[base + f * ND + d] * energy * total
                return carry

            lax.fori_loop(0, ND, one, 0, unroll=4)
            copies.append(
                pltpu.make_async_copy(done.at[pl.ds(n * ND, ND)], out_ref.at[pl.ds(f * ND, ND)], sems.at[n])
            )
            copies[-1].start()
        for one in copies:
            one.wait()

    operands = [strength, shifts, first] + parts
    in_specs = [whole(pltpu.SMEM)] * 3 + [whole(pl.ANY)] * count
    aliases = {}
    if window is not None:
        aliases = {len(operands): 0, len(operands) + 1: 1}
        operands += [near_core(window), into]
        in_specs += [whole(pltpu.VMEM), whole(pl.ANY)]
    return pl.pallas_call(
        kernel,
        out_shape=[
            vmem(((local + 2 * reach) * ND, rows, LANES)),
            jax.ShapeDtypeStruct((local * ND, rows, LANES), jnp.float32),
        ],
        in_specs=in_specs,
        out_specs=[whole(pltpu.VMEM), whole(pl.ANY)],
        scratch_shapes=[
            pltpu.VMEM((len(freqs) * ND, rows, LANES), jnp.float32),
            pltpu.SemaphoreType.DMA((len(freqs),)),
            pltpu.SemaphoreType.DMA((count,)),
        ],
        input_output_aliases=aliases,
        compiler_params=limits(8),
        cost_estimate=cost(15 * len(freqs) * ND * rows * LANES, 6 * len(freqs) * ND * rows * LANES * 4),
        name="quadruplets",
    )(*operands)


def halo_plan(spectrum, courant_lat, courant_lon, sea_mask, strength, quad_shift):
    comp_dev, lat_dev, _ = spectrum.shape
    local = comp_dev // ND
    lat_count = lax.axis_size("lat")
    comp_count = lax.axis_size("comp")
    at = lax.axis_index("lat")
    first = (lax.axis_index("comp") * comp_dev)[None].astype(jnp.int32)
    mates = [(i, i ^ 1) for i in range(lat_count)]
    corners = range(3, lat_count - 1, 4)
    sides = [(i, i + 1) for i in range(1, lat_count, 4)] + [(i + 1, i) for i in range(1, lat_count, 4)]
    relays = [(i - 2, i + 1) for i in corners] + [(i + 3, i) for i in corners]
    aheads = [(i, i + 3) for i in corners] + [(i + 1, i - 2) for i in corners]
    hands = [(i + 2, i + 1) for i in corners] + [(i - 1, i) for i in corners]
    handed = (at % 4 == 0) | (at % 4 == 3)
    place = jnp.stack([at % 2, jnp.where(handed, 1, 0)]).astype(jnp.int32)
    z_up = [(i, i + 1) for i in range(comp_count - 1)]
    z_down = [(i + 1, i) for i in range(comp_count - 1)]

    own = tiled(spectrum)
    mask = tiled(sea_mask[None])

    chunks = [[c, local - 1 - c] for c in range(reach)]
    middle = list(range(reach, local - reach))
    lots = chunks[:-1] + [chunks[-1] + middle]
    head, part = load(own, lots[:2], mask)
    mate_head = lax.ppermute(head, "lat", mates)
    ahead = [None, lax.ppermute(part, "lat", aheads)]
    sides_in = [lax.ppermute(pack_first(head, mate_head, courant_lat, place, chunks[0]), "lat", sides)]
    rest = load(own, lots[2:])
    ahead += [lax.ppermute(part, "lat", aheads) for part in rest]
    mate = lax.ppermute(own, "lat", mates)
    hands_in = [lax.ppermute(sides_in[0], "lat", relays)]
    for n, freqs in enumerate(lots):
        if n:
            message = pack_message(own, ahead[n], courant_lat, place, freqs)
            sides_in.append(lax.ppermute(message, "lat", sides))
            hands_in.append(lax.ppermute(sides_in[n], "lat", hands))
    size = len(chunks[0]) * ND
    masks = jnp.concatenate([
        head[size:], mate_head[size:], jnp.where(handed, hands_in[0][size + 1:], sides_in[0][size:size + 1])
    ])
    parts = []
    places = []
    last = []
    for n, freqs in enumerate(chunks):
        low, high = propagate(
            own if n else head, mate if n else mate_head, sides_in[n], hands_in[n],
            courant_lat, courant_lon, place, masks, freqs, picked=n == 0,
        )
        parts += [low, high]
        places += [reach + f for f in freqs]
        last = [lax.ppermute(high, "comp", z_up), lax.ppermute(low, "comp", z_down)]
        last_places = [reach - 1 - n, reach + local + n]
        if n < reach - 1:
            parts += last
            places += last_places
    parts += propagate(
        own, mate, sides_in[-1], hands_in[-1], courant_lat, courant_lon, place, masks, middle, skip=len(chunks[-1])
    )
    places += [reach + f for f in middle]
    shifts = quad_shift.T
    window, inner = quadruplets(
        None, parts, places, local, strength, shifts, first, list(range(1, local - 1)), None
    )
    window, result = quadruplets(
        window, last, last_places, local, strength, shifts, first, [0, local - 1], inner
    )
    return untiled(result, lat_dev)


def fits(comp_dev, lat_count, lat_dev, lon_count):
    local, left = divmod(comp_dev, ND)
    return left == 0 and 0 < local - 2 * reach <= 1 and lat_count % 4 == 0 and lat_dev == 2 and lon_count % LANES == 0


def per_device(spectrum, courant_lat, courant_lon, sea_mask, strength, quad_shift):
    comp_dev, lat_dev, lon_count = spectrum.shape
    if fits(comp_dev, lax.axis_size("lat"), lat_dev, lon_count):
        return halo_plan(spectrum, courant_lat, courant_lon, sea_mask, strength, quad_shift)
    return gathered_plan(spectrum, courant_lat, courant_lon, sea_mask, strength, quad_shift)


def solution(mesh):
    return jax.shard_map(
        per_device,
        mesh=mesh,
        in_specs=(P("comp", "lat", None), P("comp"), P("comp"), P("lat", None), P(), P()),
        out_specs=P("comp", "lat", None),
        check_vma=False,
    )
```

```python
import jax
import jax.numpy as jnp
from jax import lax
from jax.sharding import PartitionSpec as P
from jax.experimental import pallas as pl
from jax.experimental.pallas import tpu as pltpu

NF = 36
ND = 32
NQ = 4


reach = 4


def extended(cells, sides, width):
    for axis, dim in sides:
        count = lax.axis_size(axis)
        ends = count - 1
        head = lax.slice_in_dim(cells, 0, width, axis=dim)
        tail = lax.slice_in_dim(cells, cells.shape[dim] - width, cells.shape[dim], axis=dim)
        cells = jnp.concatenate(
            [
                lax.ppermute(tail, axis, [(i, (i + 1) % count) for i in range(ends)]),
                cells,
                lax.ppermute(head, axis, [((i + 1) % count, i) for i in range(ends)]),
            ],
            axis=dim,
        )
    return cells


def upwind(field, along_lat, along_lon, maskf):
    padded = extended(field, (("lat", 1),), 1)
    south = padded[:, :-2, :]
    north = padded[:, 2:, :]
    west = jnp.roll(field, 1, axis=2)
    east = jnp.roll(field, -1, axis=2)
    plus_a = jnp.maximum(along_lat, 0.0)
    minus_a = jnp.minimum(along_lat, 0.0)
    plus_b = jnp.maximum(along_lon, 0.0)
    minus_b = jnp.minimum(along_lon, 0.0)
    moved = field - plus_a * (field - south) - minus_a * (north - field)
    moved = moved - plus_b * (field - west) - minus_b * (east - field)
    return moved * maskf


def interact(energy, strength, quad_shift):
    rest = energy.shape[1:]
    grid = energy.reshape((NF, ND) + rest)
    widths = ((reach, reach),) + ((0, 0),) * (grid.ndim - 1)
    padded = jnp.pad(grid, widths)
    total = jnp.zeros(grid.shape, jnp.float32)
    for index in range(NQ):
        offset_f = quad_shift[index, 0]
        offset_d = quad_shift[index, 1]
        partner = lax.dynamic_slice_in_dim(padded, reach + offset_f, NF, 0)
        partner = jnp.roll(partner, -offset_d, axis=1)
        total = total + partner * (partner - grid)
    coeff = strength.reshape((NF, ND) + (1,) * len(rest))
    return (coeff * grid * total).reshape(energy.shape)


def gathered_plan(spectrum, courant_lat, courant_lon, sea_mask, strength, quad_shift):
    maskf = sea_mask.astype(jnp.float32)[None]
    along_lat = courant_lat[:, None, None]
    along_lon = courant_lon[:, None, None]
    field = upwind(spectrum, along_lat, along_lon, maskf)
    field = upwind(field, along_lat, along_lon, maskf)
    comp_dev, lat_dev, lon_count = field.shape
    point_count = lat_dev * lon_count
    flat = field.reshape(comp_dev, point_count)
    sea_most = 3 * point_count // 4
    land_first = 1 - sea_mask.reshape(point_count)
    ordering = jnp.argsort(land_first, stable=True)
    chosen = ordering[:sea_most]
    packed = jnp.take(flat, chosen, axis=1)
    spectra = lax.all_to_all(packed, "comp", split_axis=1, concat_axis=0, tiled=True)
    updated = spectra + interact(spectra, strength, quad_shift)
    returned = lax.all_to_all(updated, "comp", split_axis=0, concat_axis=1, tiled=True)
    result = jnp.zeros((comp_dev, point_count), jnp.float32).at[:, chosen].set(returned)
    return result.reshape(comp_dev, lat_dev, lon_count)


LANES = 128
PAIR = 2


def vmem(shape):
    return pltpu.VMEM(shape, jnp.float32)


def near_core(cells):
    return pltpu.with_memory_space_constraint(cells, pltpu.VMEM)


def far_from_core(cells):
    return pltpu.with_memory_space_constraint(cells, pltpu.HBM)


def whole(space):
    return pl.BlockSpec(memory_space=space)


def limits(mib):
    return pltpu.CompilerParams(vmem_limit_bytes=mib * 2**20)


def cost(flops, count):
    return pl.CostEstimate(flops=flops, bytes_accessed=count, transcendentals=0)


def tiled(cells):
    comp_dev, lat_dev, lon_count = cells.shape
    blocks = lon_count // LANES
    cells = cells.reshape(comp_dev, lat_dev, blocks, LANES).transpose(0, 2, 1, 3)
    return cells.reshape(comp_dev, blocks * lat_dev, LANES)


def untiled(cells, lat_dev):
    comp_dev, rows, _ = cells.shape
    blocks = rows // lat_dev
    cells = cells.reshape(comp_dev, blocks, lat_dev, LANES).transpose(0, 2, 1, 3)
    return cells.reshape(comp_dev, lat_dev, blocks * LANES)


def load(own, chunks, extra=None):
    spots = [(c, n, f) for c, freqs in enumerate(chunks) for n, f in enumerate(freqs)]
    rows = own.shape[1]
    ends = [len(freqs) * ND for freqs in chunks]
    sizes = list(ends)
    operands = [own]
    if extra is not None:
        sizes[0] += 1
        sizes.append(1)
        operands.append(extra)

    def kernel(own_ref, *refs):
        sems = refs[-1]
        out_refs = refs[len(operands) - 1:-1]
        copies = [
            pltpu.make_async_copy(own_ref.at[pl.ds(f * ND, ND)], out_refs[c].at[pl.ds(n * ND, ND)], sems.at[m])
            for m, (c, n, f) in enumerate(spots)
        ]
        for one in copies:
            one.start()
        if extra is not None:
            maskf = refs[0][0].astype(jnp.float32)
            out_refs[0][ends[0]] = maskf
            out_refs[-1][0] = maskf
        for one in copies:
            one.wait()

    return pl.pallas_call(
        kernel,
        out_shape=[vmem((size, rows, LANES)) for size in sizes],
        in_specs=[whole(pltpu.HBM)] + [whole(pltpu.VMEM)] * (len(operands) - 1),
        out_specs=[whole(pltpu.VMEM)] * len(sizes),
        scratch_shapes=[pltpu.SemaphoreType.DMA((len(spots),))],
        compiler_params=limits(8),
        cost_estimate=cost(0, 2 * len(spots) * ND * rows * LANES * 4),
        name="load",
    )(far_from_core(own), *operands[1:])


def pack_message(own, other, along_lat, place, freqs):
    rows = own.shape[1]

    def kernel(a_ref, place_ref, own_ref, other_ref, out_ref, held_ref, sems):
        odd = place_ref[0] > 0
        copies = [
            pltpu.make_async_copy(own_ref.at[pl.ds(f * ND, ND)], held_ref.at[pl.ds(n * ND, ND)], sems.at[n])
            for n, f in enumerate(freqs)
        ]
        for one in copies:
            one.start()
        for n, f in enumerate(freqs):
            copies[n].wait()

            def one(i, carry):
                j = n * ND + i
                from_own = (a_ref[f * ND + i] > 0) == odd
                out_ref[j] = jnp.where(from_own, held_ref[j], other_ref[j])
                return carry

            lax.fori_loop(0, ND, one, 0, unroll=8)

    shape = (len(freqs) * ND, rows, LANES)
    return pl.pallas_call(
        kernel,
        out_shape=vmem(shape),
        in_specs=[whole(pltpu.SMEM)] * 2 + [whole(pltpu.HBM), whole(pltpu.VMEM)],
        out_specs=whole(pltpu.VMEM),
        scratch_shapes=[vmem(shape), pltpu.SemaphoreType.DMA((len(freqs),))],
        compiler_params=limits(8),
        cost_estimate=cost(0, 3 * len(freqs) * ND * rows * LANES * 4),
        name="pack_message",
    )(along_lat, place, far_from_core(own), near_core(other))


def propagate(own, mate, side, hand, along_lat, along_lon, place, masks, freqs, skip=0):
    rows = own.shape[1]
    half = rows // PAIR
    size = len(freqs) * ND

    def kernel(a_ref, b_ref, place_ref, mask_ref, own_hbm, mate_hbm, side_ref, hand_ref, *refs):
        out_refs = refs[:len(freqs)]
        own_ref, mate_ref, done_ref, sems, out_sems = refs[len(freqs):]
        odd = place_ref[0] > 0
        handed = place_ref[1] > 0
        lane = lax.broadcasted_iota(jnp.int32, (half, LANES), 1)
        arrivals = [
            [
                pltpu.make_async_copy(
                    src.at[pl.ds(f * ND, ND)], dst.at[pl.ds(n * ND, ND)], sems.at[n, m]
                )
                for m, (src, dst) in enumerate(((own_hbm, own_ref), (mate_hbm, mate_ref)))
            ]
            for n, f in enumerate(freqs)
        ]
        for pair in arrivals:
            for one in pair:
                one.start()
        leaving = [
            pltpu.make_async_copy(done_ref.at[pl.ds(n * ND, ND)], out_refs[n], out_sems.at[n])
            for n in range(len(freqs))
        ]

        def run(far_ref, n, f):
            def one(i, carry):
                k = f * ND + i
                j = n * ND + i
                a = a_ref[k]
                b = b_ref[k]
                south = a > 0
                near = south == odd
                west = b > 0
                fore = jnp.where(south, 0, 1)
                back = 1 - fore
                turn = jnp.where(west, 1, LANES - 1)
                edge = lane == jnp.where(west, 0, LANES - 1)
                a = jnp.abs(a)
                b = jnp.abs(b)

                def row(ref, at, which):
                    return ref[at, pl.ds(which, half, stride=PAIR), :]

                def beside(x):
                    turned = pltpu.roll(x, turn, 1)
                    over = jnp.where(west, pltpu.roll(turned, 1, 0), pltpu.roll(turned, half - 1, 0))
                    return jnp.where(edge, over, turned)

                def moved(x, before, mask):
                    return (x - a * (x - before) - b * (x - beside(x))) * mask

                fore_mask = row(mask_ref, 0, fore)
                back_mask = row(mask_ref, 0, back)
                x0 = jnp.where(near, row(mate_ref, j, fore), row(far_ref, skip * ND + j, fore))
                x1 = jnp.where(near, row(mate_ref, j, back), row(far_ref, skip * ND + j, back))
                x2 = row(own_ref, j, fore)
                x3 = row(own_ref, j, back)
                y1 = moved(x1, x0, row(mask_ref, jnp.where(near, 1, 2), back))
                y2 = moved(x2, x1, fore_mask)
                y3 = moved(x3, x2, back_mask)
                done_ref[j, pl.ds(fore, half, stride=PAIR), :] = moved(y2, y1, fore_mask)
                done_ref[j, pl.ds(back, half, stride=PAIR), :] = moved(y3, y2, back_mask)
                return carry

            lax.fori_loop(0, ND, one, 0, unroll=4)

        for n, f in enumerate(freqs):
            for one in arrivals[n]:
                one.wait()

            @pl.when(handed)
            def _():
                run(hand_ref, n, f)

            @pl.when(jnp.logical_not(handed))
            def _():
                run(side_ref, n, f)

            leaving[n].start()
        for one in leaving:
            one.wait()

    return pl.pallas_call(
        kernel,
        out_shape=[jax.ShapeDtypeStruct((ND, rows, LANES), jnp.float32)] * len(freqs),
        in_specs=[whole(pltpu.SMEM)] * 3 + [whole(pltpu.VMEM)] + [whole(pltpu.HBM), whole(pl.ANY)]
        + [whole(pltpu.VMEM)] * 2,
        out_specs=[whole(pltpu.HBM)] * len(freqs),
        scratch_shapes=[vmem((size, rows, LANES))] * 3
        + [pltpu.SemaphoreType.DMA((len(freqs), 2)), pltpu.SemaphoreType.DMA((len(freqs),))],
        compiler_params=limits(8),
        cost_estimate=cost(40 * size * rows * LANES, 5 * size * rows * LANES * 4),
        name="propagate",
    )(
        along_lat, along_lon, place, near_core(masks),
        far_from_core(own), mate, near_core(side), near_core(hand),
    )


def quadruplets(window, parts, places, local, strength, shifts, first, freqs, into):
    rows = parts[0].shape[1]
    count = len(parts)

    def kernel(strength_ref, shift_ref, first_ref, *refs):
        part_refs = refs[:count]
        held_ref, out_ref, done, sems, part_sems = refs[-5:]
        arrivals = [
            pltpu.make_async_copy(part_refs[n], held_ref.at[pl.ds(place * ND, ND)], part_sems.at[n])
            for n, place in enumerate(places)
        ]
        for one in arrivals:
            one.start()
        for one in arrivals:
            one.wait()
        base = first_ref[0]
        copies = []
        for n, f in enumerate(freqs):
            def one(d, carry):
                energy = held_ref[(f + reach) * ND + d]
                total = jnp.zeros_like(energy)
                for q in range(NQ):
                    turned = lax.rem(d + shift_ref[1, q] + ND, ND)
                    partner = held_ref[(f + reach + shift_ref[0, q]) * ND + turned]
                    total = total + partner * (partner - energy)
                done[n * ND + d] = energy + strength_ref[base + f * ND + d] * energy * total
                return carry

            lax.fori_loop(0, ND, one, 0, unroll=4)
            copies.append(
                pltpu.make_async_copy(done.at[pl.ds(n * ND, ND)], out_ref.at[pl.ds(f * ND, ND)], sems.at[n])
            )
            copies[-1].start()
        for one in copies:
            one.wait()

    operands = [strength, shifts, first] + parts
    in_specs = [whole(pltpu.SMEM)] * 3 + [whole(pl.ANY)] * count
    aliases = {}
    if window is not None:
        aliases = {len(operands): 0, len(operands) + 1: 1}
        operands += [near_core(window), into]
        in_specs += [whole(pltpu.VMEM), whole(pl.ANY)]
    return pl.pallas_call(
        kernel,
        out_shape=[
            vmem(((local + 2 * reach) * ND, rows, LANES)),
            jax.ShapeDtypeStruct((local * ND, rows, LANES), jnp.float32),
        ],
        in_specs=in_specs,
        out_specs=[whole(pltpu.VMEM), whole(pl.ANY)],
        scratch_shapes=[
            pltpu.VMEM((len(freqs) * ND, rows, LANES), jnp.float32),
            pltpu.SemaphoreType.DMA((len(freqs),)),
            pltpu.SemaphoreType.DMA((count,)),
        ],
        input_output_aliases=aliases,
        compiler_params=limits(8),
        cost_estimate=cost(15 * len(freqs) * ND * rows * LANES, 6 * len(freqs) * ND * rows * LANES * 4),
        name="quadruplets",
    )(*operands)


def halo_plan(spectrum, courant_lat, courant_lon, sea_mask, strength, quad_shift):
    comp_dev, lat_dev, _ = spectrum.shape
    local = comp_dev // ND
    lat_count = lax.axis_size("lat")
    comp_count = lax.axis_size("comp")
    at = lax.axis_index("lat")
    first = (lax.axis_index("comp") * comp_dev)[None].astype(jnp.int32)
    mates = [(i, i ^ 1) for i in range(lat_count)]
    corners = range(3, lat_count - 1, 4)
    sides = [(i, i + 1) for i in range(1, lat_count, 4)] + [(i + 1, i) for i in range(1, lat_count, 4)]
    diagonals = [(i, i + 1) for i in corners] + [(i + 1, i) for i in corners]
    aheads = [(i, i + 3) for i in corners] + [(i + 1, i - 2) for i in corners]
    hands = [(i + 2, i + 1) for i in corners] + [(i - 1, i) for i in corners]
    handed = (at % 4 == 0) | (at % 4 == 3)
    place = jnp.stack([at % 2, jnp.where(handed, 1, 0)]).astype(jnp.int32)
    z_up = [(i, i + 1) for i in range(comp_count - 1)]
    z_down = [(i + 1, i) for i in range(comp_count - 1)]

    own = tiled(spectrum)
    mask = tiled(sea_mask[None])

    chunks = [[c, local - 1 - c] for c in range(reach)]
    middle = list(range(reach, local - reach))
    lots = chunks[:-1] + [chunks[-1] + middle]
    head, part, maskf = load(own, lots[:2], mask)
    hands_in = [lax.ppermute(head, "lat", diagonals)]
    sides_in = [lax.ppermute(head, "lat", sides)]
    ahead = [None, lax.ppermute(part, "lat", aheads)]
    rest = load(own, lots[2:])
    ahead += [lax.ppermute(part, "lat", aheads) for part in rest]
    mate_mask = lax.ppermute(maskf, "lat", mates)
    mate = lax.ppermute(own, "lat", mates)
    for n, freqs in enumerate(lots):
        if n:
            message = pack_message(own, ahead[n], courant_lat, place, freqs)
            sides_in.append(lax.ppermute(message, "lat", sides))
            hands_in.append(lax.ppermute(sides_in[n], "lat", hands))
    size = len(chunks[0]) * ND
    masks = jnp.concatenate([maskf, mate_mask, jnp.where(handed, hands_in[0][size:], sides_in[0][size:])])
    parts = []
    places = []
    last = []
    for n, freqs in enumerate(chunks):
        low, high = propagate(
            own, far_from_core(mate) if n else mate, sides_in[n], hands_in[n],
            courant_lat, courant_lon, place, masks, freqs,
        )
        parts += [low, high]
        places += [reach + f for f in freqs]
        last = [lax.ppermute(high, "comp", z_up), lax.ppermute(low, "comp", z_down)]
        last_places = [reach - 1 - n, reach + local + n]
        if n < reach - 1:
            parts += last
            places += last_places
    parts += propagate(
        own, far_from_core(mate), sides_in[-1], hands_in[-1],
        courant_lat, courant_lon, place, masks, middle, skip=len(chunks[-1]),
    )
    places += [reach + f for f in middle]
    shifts = quad_shift.T
    window, inner = quadruplets(
        None, parts, places, local, strength, shifts, first, list(range(1, local - 1)), None
    )
    window, result = quadruplets(
        window, last, last_places, local, strength, shifts, first, [0, local - 1], inner
    )
    return untiled(result, lat_dev)


def fits(comp_dev, lat_count, lat_dev, lon_count):
    local, left = divmod(comp_dev, ND)
    return left == 0 and 0 < local - 2 * reach <= 1 and lat_count % 4 == 0 and lat_dev == 2 and lon_count % LANES == 0


def per_device(spectrum, courant_lat, courant_lon, sea_mask, strength, quad_shift):
    comp_dev, lat_dev, lon_count = spectrum.shape
    if fits(comp_dev, lax.axis_size("lat"), lat_dev, lon_count):
        return halo_plan(spectrum, courant_lat, courant_lon, sea_mask, strength, quad_shift)
    return gathered_plan(spectrum, courant_lat, courant_lon, sea_mask, strength, quad_shift)


def solution(mesh):
    return jax.shard_map(
        per_device,
        mesh=mesh,
        in_specs=(P("comp", "lat", None), P("comp"), P("comp"), P("lat", None), P(), P()),
        out_specs=P("comp", "lat", None),
        check_vma=False,
    )
```

```python
import jax
import jax.numpy as jnp
from jax import lax
from jax.sharding import PartitionSpec as P
from jax.experimental import pallas as pl
from jax.experimental.pallas import tpu as pltpu

NF = 36
ND = 32
NQ = 4


reach = 4


def extended(cells, sides, width):
    for axis, dim in sides:
        count = lax.axis_size(axis)
        ends = count - 1
        head = lax.slice_in_dim(cells, 0, width, axis=dim)
        tail = lax.slice_in_dim(cells, cells.shape[dim] - width, cells.shape[dim], axis=dim)
        cells = jnp.concatenate(
            [
                lax.ppermute(tail, axis, [(i, (i + 1) % count) for i in range(ends)]),
                cells,
                lax.ppermute(head, axis, [((i + 1) % count, i) for i in range(ends)]),
            ],
            axis=dim,
        )
    return cells


def upwind(field, along_lat, along_lon, maskf):
    padded = extended(field, (("lat", 1),), 1)
    south = padded[:, :-2, :]
    north = padded[:, 2:, :]
    west = jnp.roll(field, 1, axis=2)
    east = jnp.roll(field, -1, axis=2)
    plus_a = jnp.maximum(along_lat, 0.0)
    minus_a = jnp.minimum(along_lat, 0.0)
    plus_b = jnp.maximum(along_lon, 0.0)
    minus_b = jnp.minimum(along_lon, 0.0)
    moved = field - plus_a * (field - south) - minus_a * (north - field)
    moved = moved - plus_b * (field - west) - minus_b * (east - field)
    return moved * maskf


def interact(energy, strength, quad_shift):
    rest = energy.shape[1:]
    grid = energy.reshape((NF, ND) + rest)
    widths = ((reach, reach),) + ((0, 0),) * (grid.ndim - 1)
    padded = jnp.pad(grid, widths)
    total = jnp.zeros(grid.shape, jnp.float32)
    for index in range(NQ):
        offset_f = quad_shift[index, 0]
        offset_d = quad_shift[index, 1]
        partner = lax.dynamic_slice_in_dim(padded, reach + offset_f, NF, 0)
        partner = jnp.roll(partner, -offset_d, axis=1)
        total = total + partner * (partner - grid)
    coeff = strength.reshape((NF, ND) + (1,) * len(rest))
    return (coeff * grid * total).reshape(energy.shape)


def gathered_plan(spectrum, courant_lat, courant_lon, sea_mask, strength, quad_shift):
    maskf = sea_mask.astype(jnp.float32)[None]
    along_lat = courant_lat[:, None, None]
    along_lon = courant_lon[:, None, None]
    field = upwind(spectrum, along_lat, along_lon, maskf)
    field = upwind(field, along_lat, along_lon, maskf)
    comp_dev, lat_dev, lon_count = field.shape
    point_count = lat_dev * lon_count
    flat = field.reshape(comp_dev, point_count)
    sea_most = 3 * point_count // 4
    land_first = 1 - sea_mask.reshape(point_count)
    ordering = jnp.argsort(land_first, stable=True)
    chosen = ordering[:sea_most]
    packed = jnp.take(flat, chosen, axis=1)
    spectra = lax.all_to_all(packed, "comp", split_axis=1, concat_axis=0, tiled=True)
    updated = spectra + interact(spectra, strength, quad_shift)
    returned = lax.all_to_all(updated, "comp", split_axis=0, concat_axis=1, tiled=True)
    result = jnp.zeros((comp_dev, point_count), jnp.float32).at[:, chosen].set(returned)
    return result.reshape(comp_dev, lat_dev, lon_count)


LANES = 128
PAIR = 2
GROUP = 4
CUTS = (0, 3, 8, 13, 16)


def vmem(shape):
    return pltpu.VMEM(shape, jnp.float32)


def near_core(cells):
    return pltpu.with_memory_space_constraint(cells, pltpu.VMEM)


def far_from_core(cells):
    return pltpu.with_memory_space_constraint(cells, pltpu.HBM)


def whole(space):
    return pl.BlockSpec(memory_space=space)


def limits(mib):
    return pltpu.CompilerParams(vmem_limit_bytes=mib * 2**20)


def cost(flops, count):
    return pl.CostEstimate(flops=flops, bytes_accessed=count, transcendentals=0)


def tiled(cells):
    comp_dev, lat_dev, lon_count = cells.shape
    blocks = lon_count // LANES
    cells = cells.reshape(comp_dev, lat_dev, blocks, LANES).transpose(0, 2, 1, 3)
    return cells.reshape(comp_dev, blocks * lat_dev, LANES)


def untiled(cells, lat_dev):
    comp_dev, rows, _ = cells.shape
    blocks = rows // lat_dev
    cells = cells.reshape(comp_dev, blocks, lat_dev, LANES).transpose(0, 2, 1, 3)
    return cells.reshape(comp_dev, lat_dev, blocks * LANES)


def total(spans):
    return sum(length for _, length in spans)


def laid(spans):
    at = 0
    for start, length in spans:
        yield at, start, length
        at += length


def load(own, chunks, extra=None):
    spots = [(c, at, start, length) for c, spans in enumerate(chunks) for at, start, length in laid(spans)]
    rows = own.shape[1]
    ends = [total(spans) for spans in chunks]
    sizes = list(ends)
    operands = [own]
    if extra is not None:
        sizes[0] += 1
        sizes.append(1)
        operands.append(extra)

    def kernel(own_ref, *refs):
        sems = refs[-1]
        out_refs = refs[len(operands) - 1:-1]
        copies = [
            pltpu.make_async_copy(own_ref.at[pl.ds(start, length)], out_refs[c].at[pl.ds(at, length)], sems.at[m])
            for m, (c, at, start, length) in enumerate(spots)
        ]
        for one in copies:
            one.start()
        if extra is not None:
            maskf = refs[0][0].astype(jnp.float32)
            out_refs[0][ends[0]] = maskf
            out_refs[-1][0] = maskf
        for one in copies:
            one.wait()

    return pl.pallas_call(
        kernel,
        out_shape=[vmem((size, rows, LANES)) for size in sizes],
        in_specs=[whole(pltpu.HBM)] + [whole(pltpu.VMEM)] * (len(operands) - 1),
        out_specs=[whole(pltpu.VMEM)] * len(sizes),
        scratch_shapes=[pltpu.SemaphoreType.DMA((len(spots),))],
        compiler_params=limits(8),
        cost_estimate=cost(0, 2 * sum(ends) * rows * LANES * 4),
        name="load",
    )(far_from_core(own), *operands[1:])


def pack_message(own, other, along_lat, place, spans):
    rows = own.shape[1]

    def kernel(a_ref, place_ref, own_ref, other_ref, out_ref, held_ref, sems):
        odd = place_ref[0] > 0
        copies = [
            pltpu.make_async_copy(own_ref.at[pl.ds(start, length)], held_ref.at[pl.ds(at, length)], sems.at[n])
            for n, (at, start, length) in enumerate(laid(spans))
        ]
        for one in copies:
            one.start()
        for n, (at, start, length) in enumerate(laid(spans)):
            copies[n].wait()

            def one(i, carry):
                from_own = (a_ref[start + i] > 0) == odd
                out_ref[at + i] = jnp.where(from_own, held_ref[at + i], other_ref[at + i])
                return carry

            lax.fori_loop(0, length, one, 0, unroll=8)

    shape = (total(spans), rows, LANES)
    return pl.pallas_call(
        kernel,
        out_shape=vmem(shape),
        in_specs=[whole(pltpu.SMEM)] * 2 + [whole(pltpu.HBM), whole(pltpu.VMEM)],
        out_specs=whole(pltpu.VMEM),
        scratch_shapes=[vmem(shape), pltpu.SemaphoreType.DMA((len(spans),))],
        compiler_params=limits(8),
        cost_estimate=cost(0, 3 * total(spans) * rows * LANES * 4),
        name="pack_message",
    )(along_lat, place, far_from_core(own), near_core(other))


def propagate(own, mate, side, hand, along_lat, along_lon, place, masks, spans, skip=0):
    rows = own.shape[1]
    half = rows // PAIR
    size = total(spans)
    count = len(spans)

    def kernel(a_ref, b_ref, place_ref, mask_ref, own_hbm, mate_hbm, side_ref, hand_ref, *refs):
        out_refs = refs[:count]
        own_ref, mate_ref, done_ref, sems, out_sems = refs[count:]
        odd = place_ref[0] > 0
        handed = place_ref[1] > 0
        lane = lax.broadcasted_iota(jnp.int32, (half, LANES), 1)
        sub = lax.broadcasted_iota(jnp.int32, (8, LANES), 0)
        arrivals = [
            [
                pltpu.make_async_copy(src.at[pl.ds(start, length)], dst.at[pl.ds(at, length)], sems.at[n, m])
                for m, (src, dst) in enumerate(((own_hbm, own_ref), (mate_hbm, mate_ref)))
            ]
            for n, (at, start, length) in enumerate(laid(spans))
        ]
        for pair in arrivals:
            for one in pair:
                one.start()
        leaving = [
            pltpu.make_async_copy(done_ref.at[pl.ds(at, length)], out_refs[n], out_sems.at[n])
            for n, (at, start, length) in enumerate(laid(spans))
        ]

        def run(far_ref, at, start, length):
            def row(ref, spot, which):
                return ref[spot, pl.ds(which, half, stride=PAIR), :]

            def prepare(i):
                k = start + i
                j = at + i
                a = a_ref[k]
                b = b_ref[k]
                south = a > 0
                near = south == odd
                west = b > 0
                fore = jnp.where(south, 0, 1)
                back = 1 - fore
                far = skip + j
                return dict(
                    j=j,
                    a=jnp.abs(a),
                    b=jnp.abs(b),
                    west=west,
                    fore=fore,
                    back=back,
                    turn=jnp.where(west, 1, LANES - 1),
                    step=jnp.where(west, 1, 7),
                    first=sub == jnp.where(west, 0, 7),
                    edge=lane == jnp.where(west, 0, LANES - 1),
                    fore_mask=row(mask_ref, 0, fore),
                    back_mask=row(mask_ref, 0, back),
                    halo_mask=row(mask_ref, jnp.where(near, 1, 2), back),
                    x=[
                        jnp.where(near, row(mate_ref, j, fore), row(far_ref, far, fore)),
                        jnp.where(near, row(mate_ref, j, back), row(far_ref, far, back)),
                        row(own_ref, j, fore),
                        row(own_ref, j, back),
                    ],
                )

            def beside(c, x):
                turned = pltpu.roll(x, c["turn"], 1)
                rolled = [pltpu.roll(turned[8 * t:8 * t + 8], c["step"], 0) for t in range(half // 8)]
                over = [
                    jnp.where(c["first"], jnp.where(c["west"], rolled[t - 1], rolled[(t + 1) % len(rolled)]), rolled[t])
                    for t in range(len(rolled))
                ]
                return jnp.where(c["edge"], jnp.concatenate(over, 0), turned)

            def moved(c, x, before, mask):
                return (x - c["a"] * (x - before) - c["b"] * (x - beside(c, x))) * mask

            def some(group, carry):
                comps = [prepare(group * GROUP + u) for u in range(GROUP)]
                y1 = [moved(c, c["x"][1], c["x"][0], c["halo_mask"]) for c in comps]
                y2 = [moved(c, c["x"][2], c["x"][1], c["fore_mask"]) for c in comps]
                y3 = [moved(c, c["x"][3], c["x"][2], c["back_mask"]) for c in comps]
                z2 = [moved(c, v, u, c["fore_mask"]) for c, v, u in zip(comps, y2, y1)]
                z3 = [moved(c, v, u, c["back_mask"]) for c, v, u in zip(comps, y3, y2)]
                for c, v, u in zip(comps, z2, z3):
                    done_ref[c["j"], pl.ds(c["fore"], half, stride=PAIR), :] = v
                    done_ref[c["j"], pl.ds(c["back"], half, stride=PAIR), :] = u
                return carry

            lax.fori_loop(0, length // GROUP, some, 0)

        for n, span in enumerate(laid(spans)):
            for one in arrivals[n]:
                one.wait()

            @pl.when(handed)
            def _():
                run(hand_ref, *span)

            @pl.when(jnp.logical_not(handed))
            def _():
                run(side_ref, *span)

            leaving[n].start()
        for one in leaving:
            one.wait()

    return pl.pallas_call(
        kernel,
        out_shape=[jax.ShapeDtypeStruct((length, rows, LANES), jnp.float32) for _, length in spans],
        in_specs=[whole(pltpu.SMEM)] * 3 + [whole(pltpu.VMEM)] + [whole(pltpu.HBM), whole(pl.ANY)]
        + [whole(pltpu.VMEM)] * 2,
        out_specs=[whole(pltpu.HBM)] * count,
        scratch_shapes=[vmem((size, rows, LANES))] * 3
        + [pltpu.SemaphoreType.DMA((count, 2)), pltpu.SemaphoreType.DMA((count,))],
        compiler_params=limits(8),
        cost_estimate=cost(40 * size * rows * LANES, 5 * size * rows * LANES * 4),
        name="propagate",
    )(
        along_lat, along_lon, place, near_core(masks),
        far_from_core(own), mate, near_core(side), near_core(hand),
    )


def quadruplets(window, parts, places, local, strength, shifts, first, freqs, into):
    rows = parts[0].shape[1]
    count = len(parts)

    def kernel(strength_ref, shift_ref, first_ref, *refs):
        part_refs = refs[:count]
        held_ref, out_ref, done, sems, part_sems = refs[-5:]
        arrivals = [
            pltpu.make_async_copy(part_refs[n], held_ref.at[pl.ds(place, parts[n].shape[0])], part_sems.at[n])
            for n, place in enumerate(places)
        ]
        for one in arrivals:
            one.start()
        for one in arrivals:
            one.wait()
        base = first_ref[0]
        turns = [shift_ref[1, q] for q in range(NQ)]
        copies = []
        for n, f in enumerate(freqs):
            bases = [(f + reach + shift_ref[0, q]) * ND for q in range(NQ)]

            def some(group, carry):
                made = []
                for u in range(GROUP):
                    d = group * GROUP + u
                    energy = held_ref[(f + reach) * ND + d]
                    summed = jnp.zeros_like(energy)
                    for q in range(NQ):
                        partner = held_ref[bases[q] + jnp.bitwise_and(d + turns[q], ND - 1)]
                        summed = summed + partner * (partner - energy)
                    made.append(energy + strength_ref[base + f * ND + d] * energy * summed)
                for u, one in enumerate(made):
                    done[n * ND + group * GROUP + u] = one
                return carry

            lax.fori_loop(0, ND // GROUP, some, 0)
            copies.append(
                pltpu.make_async_copy(done.at[pl.ds(n * ND, ND)], out_ref.at[pl.ds(f * ND, ND)], sems.at[n])
            )
            copies[-1].start()
        for one in copies:
            one.wait()

    operands = [strength, shifts, first] + parts
    in_specs = [whole(pltpu.SMEM)] * 3 + [whole(pl.ANY)] * count
    aliases = {}
    if window is not None:
        aliases = {len(operands): 0, len(operands) + 1: 1}
        operands += [near_core(window), into]
        in_specs += [whole(pltpu.VMEM), whole(pl.ANY)]
    return pl.pallas_call(
        kernel,
        out_shape=[
            vmem(((local + 2 * reach) * ND, rows, LANES)),
            jax.ShapeDtypeStruct((local * ND, rows, LANES), jnp.float32),
        ],
        in_specs=in_specs,
        out_specs=[whole(pltpu.VMEM), whole(pl.ANY)],
        scratch_shapes=[
            pltpu.VMEM((len(freqs) * ND, rows, LANES), jnp.float32),
            pltpu.SemaphoreType.DMA((len(freqs),)),
            pltpu.SemaphoreType.DMA((count,)),
        ],
        input_output_aliases=aliases,
        compiler_params=limits(8),
        cost_estimate=cost(15 * len(freqs) * ND * rows * LANES, 6 * len(freqs) * ND * rows * LANES * 4),
        name="quadruplets",
    )(*operands)


def halo_plan(spectrum, courant_lat, courant_lon, sea_mask, strength, quad_shift):
    comp_dev, lat_dev, _ = spectrum.shape
    local = comp_dev // ND
    lat_count = lax.axis_size("lat")
    comp_count = lax.axis_size("comp")
    at = lax.axis_index("lat")
    first = (lax.axis_index("comp") * comp_dev)[None].astype(jnp.int32)
    mates = [(i, i ^ 1) for i in range(lat_count)]
    corners = range(3, lat_count - 1, 4)
    sides = [(i, i + 1) for i in range(1, lat_count, 4)] + [(i + 1, i) for i in range(1, lat_count, 4)]
    diagonals = [(i, i + 1) for i in corners] + [(i + 1, i) for i in corners]
    aheads = [(i, i + 3) for i in corners] + [(i + 1, i - 2) for i in corners]
    hands = [(i + 2, i + 1) for i in corners] + [(i - 1, i) for i in corners]
    handed = (at % 4 == 0) | (at % 4 == 3)
    place = jnp.stack([at % 2, jnp.where(handed, 1, 0)]).astype(jnp.int32)
    z_up = [(i, i + 1) for i in range(comp_count - 1)]
    z_down = [(i + 1, i) for i in range(comp_count - 1)]

    own = tiled(spectrum)
    mask = tiled(sea_mask[None])

    edge = reach * ND
    cuts = [edge * cut // 16 for cut in CUTS]
    chunks = [[(low, high - low), (comp_dev - high, high - low)] for low, high in zip(cuts, cuts[1:])]
    middle = [(edge, comp_dev - 2 * edge)]
    lots = chunks[:-1] + [chunks[-1] + middle]
    head, part, maskf = load(own, lots[:2], mask)
    hands_in = [lax.ppermute(head, "lat", diagonals)]
    sides_in = [lax.ppermute(head, "lat", sides)]
    ahead = [None, lax.ppermute(part, "lat", aheads)]
    rest = load(own, lots[2:])
    ahead += [lax.ppermute(part, "lat", aheads) for part in rest]
    mate_mask = lax.ppermute(maskf, "lat", mates)
    mate = lax.ppermute(own, "lat", mates)
    for n, spans in enumerate(lots):
        if n:
            message = pack_message(own, ahead[n], courant_lat, place, spans)
            sides_in.append(lax.ppermute(message, "lat", sides))
            hands_in.append(lax.ppermute(sides_in[n], "lat", hands))
    size = total(chunks[0])
    masks = jnp.concatenate([maskf, mate_mask, jnp.where(handed, hands_in[0][size:], sides_in[0][size:])])
    parts = []
    places = []
    last = []
    for n, spans in enumerate(chunks):
        low, high = propagate(
            own, far_from_core(mate) if n else mate, sides_in[n], hands_in[n],
            courant_lat, courant_lon, place, masks, spans,
        )
        parts += [low, high]
        places += [edge + start for start, _ in spans]
        last = [lax.ppermute(high, "comp", z_up), lax.ppermute(low, "comp", z_down)]
        last_places = [edge + spans[1][0] - comp_dev, edge + comp_dev + spans[0][0]]
        if n < len(chunks) - 1:
            parts += last
            places += last_places
    parts += propagate(
        own, far_from_core(mate), sides_in[-1], hands_in[-1],
        courant_lat, courant_lon, place, masks, middle, skip=total(chunks[-1]),
    )
    places += [edge + start for start, _ in middle]
    shifts = quad_shift.T
    window, inner = quadruplets(
        None, parts, places, local, strength, shifts, first, list(range(1, local - 1)), None
    )
    window, result = quadruplets(
        window, last, last_places, local, strength, shifts, first, [0, local - 1], inner
    )
    return untiled(result, lat_dev)


def fits(comp_dev, lat_count, lat_dev, lon_count):
    local, left = divmod(comp_dev, ND)
    return left == 0 and 0 < local - 2 * reach <= 1 and lat_count % 4 == 0 and lat_dev == 2 and lon_count % LANES == 0


def per_device(spectrum, courant_lat, courant_lon, sea_mask, strength, quad_shift):
    comp_dev, lat_dev, lon_count = spectrum.shape
    if fits(comp_dev, lax.axis_size("lat"), lat_dev, lon_count):
        return halo_plan(spectrum, courant_lat, courant_lon, sea_mask, strength, quad_shift)
    return gathered_plan(spectrum, courant_lat, courant_lon, sea_mask, strength, quad_shift)


def solution(mesh):
    return jax.shard_map(
        per_device,
        mesh=mesh,
        in_specs=(P("comp", "lat", None), P("comp"), P("comp"), P("lat", None), P(), P()),
        out_specs=P("comp", "lat", None),
        check_vma=False,
    )
```

```python
import jax
import jax.numpy as jnp
from jax import lax
from jax.sharding import PartitionSpec as P
from jax.experimental import pallas as pl
from jax.experimental.pallas import tpu as pltpu

NF = 36
ND = 32
NQ = 4


reach = 4


def extended(cells, sides, width):
    for axis, dim in sides:
        count = lax.axis_size(axis)
        ends = count - 1
        head = lax.slice_in_dim(cells, 0, width, axis=dim)
        tail = lax.slice_in_dim(cells, cells.shape[dim] - width, cells.shape[dim], axis=dim)
        cells = jnp.concatenate(
            [
                lax.ppermute(tail, axis, [(i, (i + 1) % count) for i in range(ends)]),
                cells,
                lax.ppermute(head, axis, [((i + 1) % count, i) for i in range(ends)]),
            ],
            axis=dim,
        )
    return cells


def upwind(field, along_lat, along_lon, maskf):
    padded = extended(field, (("lat", 1),), 1)
    south = padded[:, :-2, :]
    north = padded[:, 2:, :]
    west = jnp.roll(field, 1, axis=2)
    east = jnp.roll(field, -1, axis=2)
    plus_a = jnp.maximum(along_lat, 0.0)
    minus_a = jnp.minimum(along_lat, 0.0)
    plus_b = jnp.maximum(along_lon, 0.0)
    minus_b = jnp.minimum(along_lon, 0.0)
    moved = field - plus_a * (field - south) - minus_a * (north - field)
    moved = moved - plus_b * (field - west) - minus_b * (east - field)
    return moved * maskf


def interact(energy, strength, quad_shift):
    rest = energy.shape[1:]
    grid = energy.reshape((NF, ND) + rest)
    widths = ((reach, reach),) + ((0, 0),) * (grid.ndim - 1)
    padded = jnp.pad(grid, widths)
    total = jnp.zeros(grid.shape, jnp.float32)
    for index in range(NQ):
        offset_f = quad_shift[index, 0]
        offset_d = quad_shift[index, 1]
        partner = lax.dynamic_slice_in_dim(padded, reach + offset_f, NF, 0)
        partner = jnp.roll(partner, -offset_d, axis=1)
        total = total + partner * (partner - grid)
    coeff = strength.reshape((NF, ND) + (1,) * len(rest))
    return (coeff * grid * total).reshape(energy.shape)


def gathered_plan(spectrum, courant_lat, courant_lon, sea_mask, strength, quad_shift):
    maskf = sea_mask.astype(jnp.float32)[None]
    along_lat = courant_lat[:, None, None]
    along_lon = courant_lon[:, None, None]
    field = upwind(spectrum, along_lat, along_lon, maskf)
    field = upwind(field, along_lat, along_lon, maskf)
    comp_dev, lat_dev, lon_count = field.shape
    point_count = lat_dev * lon_count
    flat = field.reshape(comp_dev, point_count)
    sea_most = 3 * point_count // 4
    land_first = 1 - sea_mask.reshape(point_count)
    ordering = jnp.argsort(land_first, stable=True)
    chosen = ordering[:sea_most]
    packed = jnp.take(flat, chosen, axis=1)
    spectra = lax.all_to_all(packed, "comp", split_axis=1, concat_axis=0, tiled=True)
    updated = spectra + interact(spectra, strength, quad_shift)
    returned = lax.all_to_all(updated, "comp", split_axis=0, concat_axis=1, tiled=True)
    result = jnp.zeros((comp_dev, point_count), jnp.float32).at[:, chosen].set(returned)
    return result.reshape(comp_dev, lat_dev, lon_count)


LANES = 128
PAIR = 2
GROUP = 4
CUTS = (0, 3, 8, 13, 16)


def vmem(shape):
    return pltpu.VMEM(shape, jnp.float32)


def near_core(cells):
    return pltpu.with_memory_space_constraint(cells, pltpu.VMEM)


def far_from_core(cells):
    return pltpu.with_memory_space_constraint(cells, pltpu.HBM)


def whole(space):
    return pl.BlockSpec(memory_space=space)


def limits(mib):
    return pltpu.CompilerParams(vmem_limit_bytes=mib * 2**20)


def cost(flops, count):
    return pl.CostEstimate(flops=flops, bytes_accessed=count, transcendentals=0)


def tiled(cells):
    comp_dev, lat_dev, lon_count = cells.shape
    blocks = lon_count // LANES
    cells = cells.reshape(comp_dev, lat_dev, blocks, LANES).transpose(0, 2, 1, 3)
    return cells.reshape(comp_dev, blocks * lat_dev, LANES)


def untiled(cells, lat_dev):
    comp_dev, rows, _ = cells.shape
    blocks = rows // lat_dev
    cells = cells.reshape(comp_dev, blocks, lat_dev, LANES).transpose(0, 2, 1, 3)
    return cells.reshape(comp_dev, lat_dev, blocks * LANES)


def total(spans):
    return sum(length for _, length in spans)


def laid(spans):
    at = 0
    for start, length in spans:
        yield at, start, length
        at += length


def load(own, chunks, extra=None):
    spots = [(c, at, start, length) for c, spans in enumerate(chunks) for at, start, length in laid(spans)]
    rows = own.shape[1]
    ends = [total(spans) for spans in chunks]
    sizes = list(ends)
    operands = [own]
    if extra is not None:
        sizes[0] += 1
        sizes.append(1)
        operands.append(extra)

    def kernel(own_ref, *refs):
        sems = refs[-1]
        out_refs = refs[len(operands) - 1:-1]
        copies = [
            pltpu.make_async_copy(own_ref.at[pl.ds(start, length)], out_refs[c].at[pl.ds(at, length)], sems.at[m])
            for m, (c, at, start, length) in enumerate(spots)
        ]
        for one in copies:
            one.start()
        if extra is not None:
            maskf = refs[0][0].astype(jnp.float32)
            out_refs[0][ends[0]] = maskf
            out_refs[-1][0] = maskf
        for one in copies:
            one.wait()

    return pl.pallas_call(
        kernel,
        out_shape=[vmem((size, rows, LANES)) for size in sizes],
        in_specs=[whole(pltpu.HBM)] + [whole(pltpu.VMEM)] * (len(operands) - 1),
        out_specs=[whole(pltpu.VMEM)] * len(sizes),
        scratch_shapes=[pltpu.SemaphoreType.DMA((len(spots),))],
        compiler_params=limits(8),
        cost_estimate=cost(0, 2 * sum(ends) * rows * LANES * 4),
        name="load",
    )(far_from_core(own), *operands[1:])


def pack_first(own, mate, along_lat, place, spans):
    rows = own.shape[1]
    size = total(spans)

    def kernel(a_ref, place_ref, own_ref, mate_ref, out_ref):
        odd = place_ref[0] > 0
        for at, start, length in laid(spans):
            def one(i, carry):
                from_own = (a_ref[start + i] > 0) == odd
                out_ref[at + i] = jnp.where(from_own, own_ref[at + i], mate_ref[at + i])
                return carry

            lax.fori_loop(0, length, one, 0, unroll=8)
        out_ref[size] = own_ref[size]
        out_ref[size + 1] = mate_ref[size]

    return pl.pallas_call(
        kernel,
        out_shape=vmem((size + 2, rows, LANES)),
        in_specs=[whole(pltpu.SMEM)] * 2 + [whole(pltpu.VMEM)] * 2,
        out_specs=whole(pltpu.VMEM),
        compiler_params=limits(8),
        cost_estimate=cost(0, 3 * size * rows * LANES * 4),
        name="pack_first",
    )(along_lat, place, near_core(own), near_core(mate))


def pack_message(own, other, along_lat, place, spans):
    rows = own.shape[1]

    def kernel(a_ref, place_ref, own_ref, other_ref, out_ref, held_ref, sems):
        odd = place_ref[0] > 0
        copies = [
            pltpu.make_async_copy(own_ref.at[pl.ds(start, length)], held_ref.at[pl.ds(at, length)], sems.at[n])
            for n, (at, start, length) in enumerate(laid(spans))
        ]
        for one in copies:
            one.start()
        for n, (at, start, length) in enumerate(laid(spans)):
            copies[n].wait()

            def one(i, carry):
                from_own = (a_ref[start + i] > 0) == odd
                out_ref[at + i] = jnp.where(from_own, held_ref[at + i], other_ref[at + i])
                return carry

            lax.fori_loop(0, length, one, 0, unroll=8)

    shape = (total(spans), rows, LANES)
    return pl.pallas_call(
        kernel,
        out_shape=vmem(shape),
        in_specs=[whole(pltpu.SMEM)] * 2 + [whole(pltpu.HBM), whole(pltpu.VMEM)],
        out_specs=whole(pltpu.VMEM),
        scratch_shapes=[vmem(shape), pltpu.SemaphoreType.DMA((len(spans),))],
        compiler_params=limits(8),
        cost_estimate=cost(0, 3 * total(spans) * rows * LANES * 4),
        name="pack_message",
    )(along_lat, place, far_from_core(own), near_core(other))


def propagate(own, mate, side, hand, along_lat, along_lon, place, masks, spans, skip=0):
    rows = own.shape[1]
    half = rows // PAIR
    size = total(spans)
    count = len(spans)

    def kernel(a_ref, b_ref, place_ref, mask_ref, own_hbm, mate_hbm, side_ref, hand_ref, *refs):
        out_refs = refs[:count]
        own_ref, mate_ref, done_ref, sems, out_sems = refs[count:]
        odd = place_ref[0] > 0
        handed = place_ref[1] > 0
        lane = lax.broadcasted_iota(jnp.int32, (half, LANES), 1)
        sub = lax.broadcasted_iota(jnp.int32, (8, LANES), 0)
        arrivals = [
            [
                pltpu.make_async_copy(src.at[pl.ds(start, length)], dst.at[pl.ds(at, length)], sems.at[n, m])
                for m, (src, dst) in enumerate(((own_hbm, own_ref), (mate_hbm, mate_ref)))
            ]
            for n, (at, start, length) in enumerate(laid(spans))
        ]
        for pair in arrivals:
            for one in pair:
                one.start()
        leaving = [
            pltpu.make_async_copy(done_ref.at[pl.ds(at, length)], out_refs[n], out_sems.at[n])
            for n, (at, start, length) in enumerate(laid(spans))
        ]

        def run(far_ref, at, start, length):
            def row(ref, spot, which):
                return ref[spot, pl.ds(which, half, stride=PAIR), :]

            def prepare(i):
                k = start + i
                j = at + i
                a = a_ref[k]
                b = b_ref[k]
                south = a > 0
                near = south == odd
                west = b > 0
                fore = jnp.where(south, 0, 1)
                back = 1 - fore
                far = skip + j
                return dict(
                    j=j,
                    a=jnp.abs(a),
                    b=jnp.abs(b),
                    west=west,
                    fore=fore,
                    back=back,
                    turn=jnp.where(west, 1, LANES - 1),
                    step=jnp.where(west, 1, 7),
                    first=sub == jnp.where(west, 0, 7),
                    edge=lane == jnp.where(west, 0, LANES - 1),
                    fore_mask=row(mask_ref, 0, fore),
                    back_mask=row(mask_ref, 0, back),
                    halo_mask=row(mask_ref, jnp.where(near, 1, 2), back),
                    x=[
                        jnp.where(near, row(mate_ref, j, fore), row(far_ref, far, fore)),
                        jnp.where(near, row(mate_ref, j, back), row(far_ref, far, back)),
                        row(own_ref, j, fore),
                        row(own_ref, j, back),
                    ],
                )

            def beside(c, x):
                turned = pltpu.roll(x, c["turn"], 1)
                rolled = [pltpu.roll(turned[8 * t:8 * t + 8], c["step"], 0) for t in range(half // 8)]
                over = [
                    jnp.where(c["first"], jnp.where(c["west"], rolled[t - 1], rolled[(t + 1) % len(rolled)]), rolled[t])
                    for t in range(len(rolled))
                ]
                return jnp.where(c["edge"], jnp.concatenate(over, 0), turned)

            def moved(c, x, before, mask):
                return (x - c["a"] * (x - before) - c["b"] * (x - beside(c, x))) * mask

            def some(group, carry):
                comps = [prepare(group * GROUP + u) for u in range(GROUP)]
                y1 = [moved(c, c["x"][1], c["x"][0], c["halo_mask"]) for c in comps]
                y2 = [moved(c, c["x"][2], c["x"][1], c["fore_mask"]) for c in comps]
                y3 = [moved(c, c["x"][3], c["x"][2], c["back_mask"]) for c in comps]
                z2 = [moved(c, v, u, c["fore_mask"]) for c, v, u in zip(comps, y2, y1)]
                z3 = [moved(c, v, u, c["back_mask"]) for c, v, u in zip(comps, y3, y2)]
                for c, v, u in zip(comps, z2, z3):
                    done_ref[c["j"], pl.ds(c["fore"], half, stride=PAIR), :] = v
                    done_ref[c["j"], pl.ds(c["back"], half, stride=PAIR), :] = u
                return carry

            lax.fori_loop(0, length // GROUP, some, 0)

        for n, span in enumerate(laid(spans)):
            for one in arrivals[n]:
                one.wait()

            @pl.when(handed)
            def _():
                run(hand_ref, *span)

            @pl.when(jnp.logical_not(handed))
            def _():
                run(side_ref, *span)

            leaving[n].start()
        for one in leaving:
            one.wait()

    return pl.pallas_call(
        kernel,
        out_shape=[jax.ShapeDtypeStruct((length, rows, LANES), jnp.float32) for _, length in spans],
        in_specs=[whole(pltpu.SMEM)] * 3 + [whole(pltpu.VMEM)] + [whole(pltpu.HBM), whole(pl.ANY)]
        + [whole(pltpu.VMEM)] * 2,
        out_specs=[whole(pltpu.HBM)] * count,
        scratch_shapes=[vmem((size, rows, LANES))] * 3
        + [pltpu.SemaphoreType.DMA((count, 2)), pltpu.SemaphoreType.DMA((count,))],
        compiler_params=limits(8),
        cost_estimate=cost(40 * size * rows * LANES, 5 * size * rows * LANES * 4),
        name="propagate",
    )(
        along_lat, along_lon, place, near_core(masks),
        far_from_core(own), mate, near_core(side), near_core(hand),
    )


def quadruplets(window, parts, places, local, strength, shifts, first, freqs, into):
    rows = parts[0].shape[1]
    count = len(parts)

    def kernel(strength_ref, shift_ref, first_ref, *refs):
        part_refs = refs[:count]
        held_ref, out_ref, done, sems, part_sems = refs[-5:]
        arrivals = [
            pltpu.make_async_copy(part_refs[n], held_ref.at[pl.ds(place, parts[n].shape[0])], part_sems.at[n])
            for n, place in enumerate(places)
        ]
        for one in arrivals:
            one.start()
        for one in arrivals:
            one.wait()
        base = first_ref[0]
        turns = [shift_ref[1, q] for q in range(NQ)]
        copies = []
        for n, f in enumerate(freqs):
            bases = [(f + reach + shift_ref[0, q]) * ND for q in range(NQ)]

            def some(group, carry):
                made = []
                for u in range(GROUP):
                    d = group * GROUP + u
                    energy = held_ref[(f + reach) * ND + d]
                    summed = jnp.zeros_like(energy)
                    for q in range(NQ):
                        partner = held_ref[bases[q] + jnp.bitwise_and(d + turns[q], ND - 1)]
                        summed = summed + partner * (partner - energy)
                    made.append(energy + strength_ref[base + f * ND + d] * energy * summed)
                for u, one in enumerate(made):
                    done[n * ND + group * GROUP + u] = one
                return carry

            lax.fori_loop(0, ND // GROUP, some, 0)
            copies.append(
                pltpu.make_async_copy(done.at[pl.ds(n * ND, ND)], out_ref.at[pl.ds(f * ND, ND)], sems.at[n])
            )
            copies[-1].start()
        for one in copies:
            one.wait()

    operands = [strength, shifts, first] + parts
    in_specs = [whole(pltpu.SMEM)] * 3 + [whole(pl.ANY)] * count
    aliases = {}
    if window is not None:
        aliases = {len(operands): 0, len(operands) + 1: 1}
        operands += [near_core(window), into]
        in_specs += [whole(pltpu.VMEM), whole(pl.ANY)]
    return pl.pallas_call(
        kernel,
        out_shape=[
            vmem(((local + 2 * reach) * ND, rows, LANES)),
            jax.ShapeDtypeStruct((local * ND, rows, LANES), jnp.float32),
        ],
        in_specs=in_specs,
        out_specs=[whole(pltpu.VMEM), whole(pl.ANY)],
        scratch_shapes=[
            pltpu.VMEM((len(freqs) * ND, rows, LANES), jnp.float32),
            pltpu.SemaphoreType.DMA((len(freqs),)),
            pltpu.SemaphoreType.DMA((count,)),
        ],
        input_output_aliases=aliases,
        compiler_params=limits(8),
        cost_estimate=cost(15 * len(freqs) * ND * rows * LANES, 6 * len(freqs) * ND * rows * LANES * 4),
        name="quadruplets",
    )(*operands)


def halo_plan(spectrum, courant_lat, courant_lon, sea_mask, strength, quad_shift):
    comp_dev, lat_dev, _ = spectrum.shape
    local = comp_dev // ND
    lat_count = lax.axis_size("lat")
    comp_count = lax.axis_size("comp")
    at = lax.axis_index("lat")
    first = (lax.axis_index("comp") * comp_dev)[None].astype(jnp.int32)
    mates = [(i, i ^ 1) for i in range(lat_count)]
    corners = range(3, lat_count - 1, 4)
    sides = [(i, i + 1) for i in range(1, lat_count, 4)] + [(i + 1, i) for i in range(1, lat_count, 4)]
    relays = [(i - 2, i + 1) for i in corners] + [(i + 3, i) for i in corners]
    aheads = [(i, i + 3) for i in corners] + [(i + 1, i - 2) for i in corners]
    hands = [(i + 2, i + 1) for i in corners] + [(i - 1, i) for i in corners]
    handed = (at % 4 == 0) | (at % 4 == 3)
    place = jnp.stack([at % 2, jnp.where(handed, 1, 0)]).astype(jnp.int32)
    z_up = [(i, i + 1) for i in range(comp_count - 1)]
    z_down = [(i + 1, i) for i in range(comp_count - 1)]

    own = tiled(spectrum)
    mask = tiled(sea_mask[None])

    edge = reach * ND
    cuts = [edge * cut // 16 for cut in CUTS]
    chunks = [[(low, high - low), (comp_dev - high, high - low)] for low, high in zip(cuts, cuts[1:])]
    middle = [(edge, comp_dev - 2 * edge)]
    lots = chunks[:-1] + [chunks[-1] + middle]
    head, part, maskf = load(own, lots[:2], mask)
    mate_head = lax.ppermute(head, "lat", mates)
    ahead = [None, lax.ppermute(part, "lat", aheads)]
    sides_in = [lax.ppermute(pack_first(head, mate_head, courant_lat, place, chunks[0]), "lat", sides)]
    hands_in = [lax.ppermute(sides_in[0], "lat", relays)]
    rest = load(own, lots[2:])
    ahead += [lax.ppermute(part, "lat", aheads) for part in rest]
    mate = lax.ppermute(own, "lat", mates)
    for n, spans in enumerate(lots):
        if n:
            message = pack_message(own, ahead[n], courant_lat, place, spans)
            sides_in.append(lax.ppermute(message, "lat", sides))
            hands_in.append(lax.ppermute(sides_in[n], "lat", hands))
    size = total(chunks[0])
    far_mask = jnp.where(handed, hands_in[0][size + 1:], sides_in[0][size:size + 1])
    masks = jnp.concatenate([maskf, mate_head[size:], far_mask])
    parts = []
    places = []
    last = []
    for n, spans in enumerate(chunks):
        low, high = propagate(
            own, far_from_core(mate) if n else mate, sides_in[n], hands_in[n],
            courant_lat, courant_lon, place, masks, spans,
        )
        parts += [low, high]
        places += [edge + start for start, _ in spans]
        last = [lax.ppermute(high, "comp", z_up), lax.ppermute(low, "comp", z_down)]
        last_places = [edge + spans[1][0] - comp_dev, edge + comp_dev + spans[0][0]]
        if n < len(chunks) - 1:
            parts += last
            places += last_places
    parts += propagate(
        own, far_from_core(mate), sides_in[-1], hands_in[-1],
        courant_lat, courant_lon, place, masks, middle, skip=total(chunks[-1]),
    )
    places += [edge + start for start, _ in middle]
    shifts = quad_shift.T
    window, inner = quadruplets(
        None, parts, places, local, strength, shifts, first, list(range(1, local - 1)), None
    )
    window, result = quadruplets(
        window, last, last_places, local, strength, shifts, first, [0, local - 1], inner
    )
    return untiled(result, lat_dev)


def fits(comp_dev, lat_count, lat_dev, lon_count):
    local, left = divmod(comp_dev, ND)
    return left == 0 and 0 < local - 2 * reach <= 1 and lat_count % 4 == 0 and lat_dev == 2 and lon_count % LANES == 0


def per_device(spectrum, courant_lat, courant_lon, sea_mask, strength, quad_shift):
    comp_dev, lat_dev, lon_count = spectrum.shape
    if fits(comp_dev, lax.axis_size("lat"), lat_dev, lon_count):
        return halo_plan(spectrum, courant_lat, courant_lon, sea_mask, strength, quad_shift)
    return gathered_plan(spectrum, courant_lat, courant_lon, sea_mask, strength, quad_shift)


def solution(mesh):
    return jax.shard_map(
        per_device,
        mesh=mesh,
        in_specs=(P("comp", "lat", None), P("comp"), P("comp"), P("lat", None), P(), P()),
        out_specs=P("comp", "lat", None),
        check_vma=False,
    )
```

```python
import jax
import jax.numpy as jnp
from jax import lax
from jax.sharding import PartitionSpec as P
from jax.experimental import pallas as pl
from jax.experimental.pallas import tpu as pltpu

NF = 36
ND = 32
NQ = 4


reach = 4


def extended(cells, sides, width):
    for axis, dim in sides:
        count = lax.axis_size(axis)
        ends = count - 1
        head = lax.slice_in_dim(cells, 0, width, axis=dim)
        tail = lax.slice_in_dim(cells, cells.shape[dim] - width, cells.shape[dim], axis=dim)
        cells = jnp.concatenate(
            [
                lax.ppermute(tail, axis, [(i, (i + 1) % count) for i in range(ends)]),
                cells,
                lax.ppermute(head, axis, [((i + 1) % count, i) for i in range(ends)]),
            ],
            axis=dim,
        )
    return cells


def upwind(field, along_lat, along_lon, maskf):
    padded = extended(field, (("lat", 1),), 1)
    south = padded[:, :-2, :]
    north = padded[:, 2:, :]
    west = jnp.roll(field, 1, axis=2)
    east = jnp.roll(field, -1, axis=2)
    plus_a = jnp.maximum(along_lat, 0.0)
    minus_a = jnp.minimum(along_lat, 0.0)
    plus_b = jnp.maximum(along_lon, 0.0)
    minus_b = jnp.minimum(along_lon, 0.0)
    moved = field - plus_a * (field - south) - minus_a * (north - field)
    moved = moved - plus_b * (field - west) - minus_b * (east - field)
    return moved * maskf


def interact(energy, strength, quad_shift):
    rest = energy.shape[1:]
    grid = energy.reshape((NF, ND) + rest)
    widths = ((reach, reach),) + ((0, 0),) * (grid.ndim - 1)
    padded = jnp.pad(grid, widths)
    total = jnp.zeros(grid.shape, jnp.float32)
    for index in range(NQ):
        offset_f = quad_shift[index, 0]
        offset_d = quad_shift[index, 1]
        partner = lax.dynamic_slice_in_dim(padded, reach + offset_f, NF, 0)
        partner = jnp.roll(partner, -offset_d, axis=1)
        total = total + partner * (partner - grid)
    coeff = strength.reshape((NF, ND) + (1,) * len(rest))
    return (coeff * grid * total).reshape(energy.shape)


def gathered_plan(spectrum, courant_lat, courant_lon, sea_mask, strength, quad_shift):
    maskf = sea_mask.astype(jnp.float32)[None]
    along_lat = courant_lat[:, None, None]
    along_lon = courant_lon[:, None, None]
    field = upwind(spectrum, along_lat, along_lon, maskf)
    field = upwind(field, along_lat, along_lon, maskf)
    comp_dev, lat_dev, lon_count = field.shape
    point_count = lat_dev * lon_count
    flat = field.reshape(comp_dev, point_count)
    sea_most = 3 * point_count // 4
    land_first = 1 - sea_mask.reshape(point_count)
    ordering = jnp.argsort(land_first, stable=True)
    chosen = ordering[:sea_most]
    packed = jnp.take(flat, chosen, axis=1)
    spectra = lax.all_to_all(packed, "comp", split_axis=1, concat_axis=0, tiled=True)
    updated = spectra + interact(spectra, strength, quad_shift)
    returned = lax.all_to_all(updated, "comp", split_axis=0, concat_axis=1, tiled=True)
    result = jnp.zeros((comp_dev, point_count), jnp.float32).at[:, chosen].set(returned)
    return result.reshape(comp_dev, lat_dev, lon_count)


LANES = 128
PAIR = 2
GROUP = 4
CUTS = (0, 4, 11, 16)


def vmem(shape):
    return pltpu.VMEM(shape, jnp.float32)


def near_core(cells):
    return pltpu.with_memory_space_constraint(cells, pltpu.VMEM)


def far_from_core(cells):
    return pltpu.with_memory_space_constraint(cells, pltpu.HBM)


def whole(space):
    return pl.BlockSpec(memory_space=space)


def limits(mib):
    return pltpu.CompilerParams(vmem_limit_bytes=mib * 2**20)


def cost(flops, count):
    return pl.CostEstimate(flops=flops, bytes_accessed=count, transcendentals=0)


def tiled(cells):
    comp_dev, lat_dev, lon_count = cells.shape
    blocks = lon_count // LANES
    cells = cells.reshape(comp_dev, lat_dev, blocks, LANES).transpose(0, 2, 1, 3)
    return cells.reshape(comp_dev, blocks * lat_dev, LANES)


def untiled(cells, lat_dev):
    comp_dev, rows, _ = cells.shape
    blocks = rows // lat_dev
    cells = cells.reshape(comp_dev, blocks, lat_dev, LANES).transpose(0, 2, 1, 3)
    return cells.reshape(comp_dev, lat_dev, blocks * LANES)


def total(spans):
    return sum(length for _, length in spans)


def laid(spans):
    at = 0
    for start, length in spans:
        yield at, start, length
        at += length


def load(own, chunks, extra=None):
    spots = [(c, at, start, length) for c, spans in enumerate(chunks) for at, start, length in laid(spans)]
    rows = own.shape[1]
    ends = [total(spans) for spans in chunks]
    sizes = list(ends)
    operands = [own]
    if extra is not None:
        sizes[0] += 1
        sizes.append(1)
        operands.append(extra)

    def kernel(own_ref, *refs):
        sems = refs[-1]
        out_refs = refs[len(operands) - 1:-1]
        copies = [
            pltpu.make_async_copy(own_ref.at[pl.ds(start, length)], out_refs[c].at[pl.ds(at, length)], sems.at[m])
            for m, (c, at, start, length) in enumerate(spots)
        ]
        for one in copies:
            one.start()
        if extra is not None:
            maskf = refs[0][0].astype(jnp.float32)
            out_refs[0][ends[0]] = maskf
            out_refs[-1][0] = maskf
        for one in copies:
            one.wait()

    return pl.pallas_call(
        kernel,
        out_shape=[vmem((size, rows, LANES)) for size in sizes],
        in_specs=[whole(pltpu.HBM)] + [whole(pltpu.VMEM)] * (len(operands) - 1),
        out_specs=[whole(pltpu.VMEM)] * len(sizes),
        scratch_shapes=[pltpu.SemaphoreType.DMA((len(spots),))],
        compiler_params=limits(8),
        cost_estimate=cost(0, 2 * sum(ends) * rows * LANES * 4),
        name="load",
    )(far_from_core(own), *operands[1:])


def pack_first(own, mate, along_lat, place, spans):
    rows = own.shape[1]
    size = total(spans)

    def kernel(a_ref, place_ref, own_ref, mate_ref, out_ref):
        odd = place_ref[0] > 0
        for at, start, length in laid(spans):
            def one(i, carry):
                from_own = (a_ref[start + i] > 0) == odd
                out_ref[at + i] = jnp.where(from_own, own_ref[at + i], mate_ref[at + i])
                return carry

            lax.fori_loop(0, length, one, 0, unroll=8)
        out_ref[size] = own_ref[size]
        out_ref[size + 1] = mate_ref[size]

    return pl.pallas_call(
        kernel,
        out_shape=vmem((size + 2, rows, LANES)),
        in_specs=[whole(pltpu.SMEM)] * 2 + [whole(pltpu.VMEM)] * 2,
        out_specs=whole(pltpu.VMEM),
        compiler_params=limits(8),
        cost_estimate=cost(0, 3 * size * rows * LANES * 4),
        name="pack_first",
    )(along_lat, place, near_core(own), near_core(mate))


def pack_message(own, other, along_lat, place, spans):
    rows = own.shape[1]

    def kernel(a_ref, place_ref, own_ref, other_ref, out_ref, held_ref, sems):
        odd = place_ref[0] > 0
        copies = [
            pltpu.make_async_copy(own_ref.at[pl.ds(start, length)], held_ref.at[pl.ds(at, length)], sems.at[n])
            for n, (at, start, length) in enumerate(laid(spans))
        ]
        for one in copies:
            one.start()
        for n, (at, start, length) in enumerate(laid(spans)):
            copies[n].wait()

            def one(i, carry):
                from_own = (a_ref[start + i] > 0) == odd
                out_ref[at + i] = jnp.where(from_own, held_ref[at + i], other_ref[at + i])
                return carry

            lax.fori_loop(0, length, one, 0, unroll=8)

    shape = (total(spans), rows, LANES)
    return pl.pallas_call(
        kernel,
        out_shape=vmem(shape),
        in_specs=[whole(pltpu.SMEM)] * 2 + [whole(pltpu.HBM), whole(pltpu.VMEM)],
        out_specs=whole(pltpu.VMEM),
        scratch_shapes=[vmem(shape), pltpu.SemaphoreType.DMA((len(spans),))],
        compiler_params=limits(8),
        cost_estimate=cost(0, 3 * total(spans) * rows * LANES * 4),
        name="pack_message",
    )(along_lat, place, far_from_core(own), near_core(other))


def propagate(own, mate, side, hand, along_lat, along_lon, place, masks, spans, skip=0):
    rows = own.shape[1]
    half = rows // PAIR
    size = total(spans)
    count = len(spans)

    def kernel(a_ref, b_ref, place_ref, mask_ref, own_hbm, mate_hbm, side_ref, hand_ref, *refs):
        out_refs = refs[:count]
        own_ref, mate_ref, done_ref, sems, out_sems = refs[count:]
        odd = place_ref[0] > 0
        handed = place_ref[1] > 0
        lane = lax.broadcasted_iota(jnp.int32, (half, LANES), 1)
        sub = lax.broadcasted_iota(jnp.int32, (8, LANES), 0)
        arrivals = [
            [
                pltpu.make_async_copy(src.at[pl.ds(start, length)], dst.at[pl.ds(at, length)], sems.at[n, m])
                for m, (src, dst) in enumerate(((own_hbm, own_ref), (mate_hbm, mate_ref)))
            ]
            for n, (at, start, length) in enumerate(laid(spans))
        ]
        for pair in arrivals:
            for one in pair:
                one.start()
        leaving = [
            pltpu.make_async_copy(done_ref.at[pl.ds(at, length)], out_refs[n], out_sems.at[n])
            for n, (at, start, length) in enumerate(laid(spans))
        ]

        def run(far_ref, at, start, length):
            def row(ref, spot, which):
                return ref[spot, pl.ds(which, half, stride=PAIR), :]

            def prepare(i):
                k = start + i
                j = at + i
                a = a_ref[k]
                b = b_ref[k]
                south = a > 0
                near = south == odd
                west = b > 0
                fore = jnp.where(south, 0, 1)
                back = 1 - fore
                far = skip + j
                return dict(
                    j=j,
                    a=jnp.abs(a),
                    b=jnp.abs(b),
                    west=west,
                    fore=fore,
                    back=back,
                    turn=jnp.where(west, 1, LANES - 1),
                    step=jnp.where(west, 1, 7),
                    first=sub == jnp.where(west, 0, 7),
                    edge=lane == jnp.where(west, 0, LANES - 1),
                    fore_mask=row(mask_ref, 0, fore),
                    back_mask=row(mask_ref, 0, back),
                    halo_mask=row(mask_ref, jnp.where(near, 1, 2), back),
                    x=[
                        jnp.where(near, row(mate_ref, j, fore), row(far_ref, far, fore)),
                        jnp.where(near, row(mate_ref, j, back), row(far_ref, far, back)),
                        row(own_ref, j, fore),
                        row(own_ref, j, back),
                    ],
                )

            def beside(c, x):
                turned = pltpu.roll(x, c["turn"], 1)
                rolled = [pltpu.roll(turned[8 * t:8 * t + 8], c["step"], 0) for t in range(half // 8)]
                over = [
                    jnp.where(c["first"], jnp.where(c["west"], rolled[t - 1], rolled[(t + 1) % len(rolled)]), rolled[t])
                    for t in range(len(rolled))
                ]
                return jnp.where(c["edge"], jnp.concatenate(over, 0), turned)

            def moved(c, x, before, mask):
                return (x - c["a"] * (x - before) - c["b"] * (x - beside(c, x))) * mask

            def some(group, carry):
                comps = [prepare(group * GROUP + u) for u in range(GROUP)]
                y1 = [moved(c, c["x"][1], c["x"][0], c["halo_mask"]) for c in comps]
                y2 = [moved(c, c["x"][2], c["x"][1], c["fore_mask"]) for c in comps]
                y3 = [moved(c, c["x"][3], c["x"][2], c["back_mask"]) for c in comps]
                z2 = [moved(c, v, u, c["fore_mask"]) for c, v, u in zip(comps, y2, y1)]
                z3 = [moved(c, v, u, c["back_mask"]) for c, v, u in zip(comps, y3, y2)]
                for c, v, u in zip(comps, z2, z3):
                    done_ref[c["j"], pl.ds(c["fore"], half, stride=PAIR), :] = v
                    done_ref[c["j"], pl.ds(c["back"], half, stride=PAIR), :] = u
                return carry

            lax.fori_loop(0, length // GROUP, some, 0)

        for n, span in enumerate(laid(spans)):
            for one in arrivals[n]:
                one.wait()

            @pl.when(handed)
            def _():
                run(hand_ref, *span)

            @pl.when(jnp.logical_not(handed))
            def _():
                run(side_ref, *span)

            leaving[n].start()
        for one in leaving:
            one.wait()

    return pl.pallas_call(
        kernel,
        out_shape=[jax.ShapeDtypeStruct((length, rows, LANES), jnp.float32) for _, length in spans],
        in_specs=[whole(pltpu.SMEM)] * 3 + [whole(pltpu.VMEM)] + [whole(pltpu.HBM), whole(pl.ANY)]
        + [whole(pltpu.VMEM)] * 2,
        out_specs=[whole(pltpu.HBM)] * count,
        scratch_shapes=[vmem((size, rows, LANES))] * 3
        + [pltpu.SemaphoreType.DMA((count, 2)), pltpu.SemaphoreType.DMA((count,))],
        compiler_params=limits(8),
        cost_estimate=cost(40 * size * rows * LANES, 5 * size * rows * LANES * 4),
        name="propagate",
    )(
        along_lat, along_lon, place, near_core(masks),
        far_from_core(own), mate, near_core(side), near_core(hand),
    )


def quadruplets(window, parts, places, local, strength, shifts, first, freqs, into):
    rows = parts[0].shape[1]
    count = len(parts)

    def kernel(strength_ref, shift_ref, first_ref, *refs):
        part_refs = refs[:count]
        held_ref, out_ref, done, sems, part_sems = refs[-5:]
        arrivals = [
            pltpu.make_async_copy(part_refs[n], held_ref.at[pl.ds(place, parts[n].shape[0])], part_sems.at[n])
            for n, place in enumerate(places)
        ]
        for one in arrivals:
            one.start()
        for one in arrivals:
            one.wait()
        base = first_ref[0]
        turns = [shift_ref[1, q] for q in range(NQ)]
        copies = []
        for n, f in enumerate(freqs):
            bases = [(f + reach + shift_ref[0, q]) * ND for q in range(NQ)]

            def some(group, carry):
                made = []
                for u in range(GROUP):
                    d = group * GROUP + u
                    energy = held_ref[(f + reach) * ND + d]
                    summed = jnp.zeros_like(energy)
                    for q in range(NQ):
                        partner = held_ref[bases[q] + jnp.bitwise_and(d + turns[q], ND - 1)]
                        summed = summed + partner * (partner - energy)
                    made.append(energy + strength_ref[base + f * ND + d] * energy * summed)
                for u, one in enumerate(made):
                    done[n * ND + group * GROUP + u] = one
                return carry

            lax.fori_loop(0, ND // GROUP, some, 0)
            copies.append(
                pltpu.make_async_copy(done.at[pl.ds(n * ND, ND)], out_ref.at[pl.ds(f * ND, ND)], sems.at[n])
            )
            copies[-1].start()
        for one in copies:
            one.wait()

    operands = [strength, shifts, first] + parts
    in_specs = [whole(pltpu.SMEM)] * 3 + [whole(pl.ANY)] * count
    aliases = {}
    if window is not None:
        aliases = {len(operands): 0, len(operands) + 1: 1}
        operands += [near_core(window), into]
        in_specs += [whole(pltpu.VMEM), whole(pl.ANY)]
    return pl.pallas_call(
        kernel,
        out_shape=[
            vmem(((local + 2 * reach) * ND, rows, LANES)),
            jax.ShapeDtypeStruct((local * ND, rows, LANES), jnp.float32),
        ],
        in_specs=in_specs,
        out_specs=[whole(pltpu.VMEM), whole(pl.ANY)],
        scratch_shapes=[
            pltpu.VMEM((len(freqs) * ND, rows, LANES), jnp.float32),
            pltpu.SemaphoreType.DMA((len(freqs),)),
            pltpu.SemaphoreType.DMA((count,)),
        ],
        input_output_aliases=aliases,
        compiler_params=limits(8),
        cost_estimate=cost(15 * len(freqs) * ND * rows * LANES, 6 * len(freqs) * ND * rows * LANES * 4),
        name="quadruplets",
    )(*operands)


def halo_plan(spectrum, courant_lat, courant_lon, sea_mask, strength, quad_shift):
    comp_dev, lat_dev, _ = spectrum.shape
    local = comp_dev // ND
    lat_count = lax.axis_size("lat")
    comp_count = lax.axis_size("comp")
    at = lax.axis_index("lat")
    first = (lax.axis_index("comp") * comp_dev)[None].astype(jnp.int32)
    mates = [(i, i ^ 1) for i in range(lat_count)]
    corners = range(3, lat_count - 1, 4)
    sides = [(i, i + 1) for i in range(1, lat_count, 4)] + [(i + 1, i) for i in range(1, lat_count, 4)]
    relays = [(i - 2, i + 1) for i in corners] + [(i + 3, i) for i in corners]
    aheads = [(i, i + 3) for i in corners] + [(i + 1, i - 2) for i in corners]
    hands = [(i + 2, i + 1) for i in corners] + [(i - 1, i) for i in corners]
    handed = (at % 4 == 0) | (at % 4 == 3)
    place = jnp.stack([at % 2, jnp.where(handed, 1, 0)]).astype(jnp.int32)
    z_up = [(i, i + 1) for i in range(comp_count - 1)]
    z_down = [(i + 1, i) for i in range(comp_count - 1)]

    own = tiled(spectrum)
    mask = tiled(sea_mask[None])

    edge = reach * ND
    cuts = [edge * cut // 16 for cut in CUTS]
    chunks = [[(low, high - low), (comp_dev - high, high - low)] for low, high in zip(cuts, cuts[1:])]
    middle = [(edge, comp_dev - 2 * edge)]
    lots = chunks[:-1] + [chunks[-1] + middle]
    head, part, maskf = load(own, lots[:2], mask)
    mate_head = lax.ppermute(head, "lat", mates)
    ahead = [None, lax.ppermute(part, "lat", aheads)]
    sides_in = [lax.ppermute(pack_first(head, mate_head, courant_lat, place, chunks[0]), "lat", sides)]
    hands_in = [lax.ppermute(sides_in[0], "lat", relays)]
    rest = load(own, lots[2:])
    ahead += [lax.ppermute(part, "lat", aheads) for part in rest]
    mate = lax.ppermute(own, "lat", mates)
    for n, spans in enumerate(lots):
        if n:
            message = pack_message(own, ahead[n], courant_lat, place, spans)
            sides_in.append(lax.ppermute(message, "lat", sides))
            hands_in.append(lax.ppermute(sides_in[n], "lat", hands))
    size = total(chunks[0])
    far_mask = jnp.where(handed, hands_in[0][size + 1:], sides_in[0][size:size + 1])
    masks = jnp.concatenate([maskf, mate_head[size:], far_mask])
    parts = []
    places = []
    last = []
    for n, spans in enumerate(chunks):
        low, high = propagate(
            own, far_from_core(mate) if n else mate, sides_in[n], hands_in[n],
            courant_lat, courant_lon, place, masks, spans,
        )
        parts += [low, high]
        places += [edge + start for start, _ in spans]
        last = [lax.ppermute(high, "comp", z_up), lax.ppermute(low, "comp", z_down)]
        last_places = [edge + spans[1][0] - comp_dev, edge + comp_dev + spans[0][0]]
        if n < len(chunks) - 1:
            parts += last
            places += last_places
    parts += propagate(
        own, far_from_core(mate), sides_in[-1], hands_in[-1],
        courant_lat, courant_lon, place, masks, middle, skip=total(chunks[-1]),
    )
    places += [edge + start for start, _ in middle]
    shifts = quad_shift.T
    late = -(-chunks[-1][0][1] // ND)
    rims = list(range(late)) + list(range(local - late, local))
    window, inner = quadruplets(
        None, parts, places, local, strength, shifts, first, list(range(late, local - late)), None
    )
    window, result = quadruplets(window, last, last_places, local, strength, shifts, first, rims, inner)
    return untiled(result, lat_dev)


def fits(comp_dev, lat_count, lat_dev, lon_count):
    local, left = divmod(comp_dev, ND)
    return left == 0 and 0 < local - 2 * reach <= 1 and lat_count % 4 == 0 and lat_dev == 2 and lon_count % LANES == 0


def per_device(spectrum, courant_lat, courant_lon, sea_mask, strength, quad_shift):
    comp_dev, lat_dev, lon_count = spectrum.shape
    if fits(comp_dev, lax.axis_size("lat"), lat_dev, lon_count):
        return halo_plan(spectrum, courant_lat, courant_lon, sea_mask, strength, quad_shift)
    return gathered_plan(spectrum, courant_lat, courant_lon, sea_mask, strength, quad_shift)


def solution(mesh):
    return jax.shard_map(
        per_device,
        mesh=mesh,
        in_specs=(P("comp", "lat", None), P("comp"), P("comp"), P("lat", None), P(), P()),
        out_specs=P("comp", "lat", None),
        check_vma=False,
    )
```

```python
import jax
import jax.numpy as jnp
from jax import lax
from jax.sharding import PartitionSpec as P
from jax.experimental import pallas as pl
from jax.experimental.pallas import tpu as pltpu

NF = 36
ND = 32
NQ = 4


reach = 4


def extended(cells, sides, width):
    for axis, dim in sides:
        count = lax.axis_size(axis)
        ends = count - 1
        head = lax.slice_in_dim(cells, 0, width, axis=dim)
        tail = lax.slice_in_dim(cells, cells.shape[dim] - width, cells.shape[dim], axis=dim)
        cells = jnp.concatenate(
            [
                lax.ppermute(tail, axis, [(i, (i + 1) % count) for i in range(ends)]),
                cells,
                lax.ppermute(head, axis, [((i + 1) % count, i) for i in range(ends)]),
            ],
            axis=dim,
        )
    return cells


def upwind(field, along_lat, along_lon, maskf):
    padded = extended(field, (("lat", 1),), 1)
    south = padded[:, :-2, :]
    north = padded[:, 2:, :]
    west = jnp.roll(field, 1, axis=2)
    east = jnp.roll(field, -1, axis=2)
    plus_a = jnp.maximum(along_lat, 0.0)
    minus_a = jnp.minimum(along_lat, 0.0)
    plus_b = jnp.maximum(along_lon, 0.0)
    minus_b = jnp.minimum(along_lon, 0.0)
    moved = field - plus_a * (field - south) - minus_a * (north - field)
    moved = moved - plus_b * (field - west) - minus_b * (east - field)
    return moved * maskf


def interact(energy, strength, quad_shift):
    rest = energy.shape[1:]
    grid = energy.reshape((NF, ND) + rest)
    widths = ((reach, reach),) + ((0, 0),) * (grid.ndim - 1)
    padded = jnp.pad(grid, widths)
    total = jnp.zeros(grid.shape, jnp.float32)
    for index in range(NQ):
        offset_f = quad_shift[index, 0]
        offset_d = quad_shift[index, 1]
        partner = lax.dynamic_slice_in_dim(padded, reach + offset_f, NF, 0)
        partner = jnp.roll(partner, -offset_d, axis=1)
        total = total + partner * (partner - grid)
    coeff = strength.reshape((NF, ND) + (1,) * len(rest))
    return (coeff * grid * total).reshape(energy.shape)


def gathered_plan(spectrum, courant_lat, courant_lon, sea_mask, strength, quad_shift):
    maskf = sea_mask.astype(jnp.float32)[None]
    along_lat = courant_lat[:, None, None]
    along_lon = courant_lon[:, None, None]
    field = upwind(spectrum, along_lat, along_lon, maskf)
    field = upwind(field, along_lat, along_lon, maskf)
    comp_dev, lat_dev, lon_count = field.shape
    point_count = lat_dev * lon_count
    flat = field.reshape(comp_dev, point_count)
    sea_most = 3 * point_count // 4
    land_first = 1 - sea_mask.reshape(point_count)
    ordering = jnp.argsort(land_first, stable=True)
    chosen = ordering[:sea_most]
    packed = jnp.take(flat, chosen, axis=1)
    spectra = lax.all_to_all(packed, "comp", split_axis=1, concat_axis=0, tiled=True)
    updated = spectra + interact(spectra, strength, quad_shift)
    returned = lax.all_to_all(updated, "comp", split_axis=0, concat_axis=1, tiled=True)
    result = jnp.zeros((comp_dev, point_count), jnp.float32).at[:, chosen].set(returned)
    return result.reshape(comp_dev, lat_dev, lon_count)


LANES = 128
PAIR = 2
GROUP = 8
CUTS = (0, 4, 9, 13, 16)


def vmem(shape):
    return pltpu.VMEM(shape, jnp.float32)


def near_core(cells):
    return pltpu.with_memory_space_constraint(cells, pltpu.VMEM)


def far_from_core(cells):
    return pltpu.with_memory_space_constraint(cells, pltpu.HBM)


def whole(space):
    return pl.BlockSpec(memory_space=space)


def limits(mib):
    return pltpu.CompilerParams(vmem_limit_bytes=mib * 2**20)


def cost(flops, count):
    return pl.CostEstimate(flops=flops, bytes_accessed=count, transcendentals=0)


def tiled(cells):
    comp_dev, lat_dev, lon_count = cells.shape
    blocks = lon_count // LANES
    cells = cells.reshape(comp_dev, lat_dev, blocks, LANES).transpose(0, 2, 1, 3)
    return cells.reshape(comp_dev, blocks * lat_dev, LANES)


def untiled(cells, lat_dev):
    comp_dev, rows, _ = cells.shape
    blocks = rows // lat_dev
    cells = cells.reshape(comp_dev, blocks, lat_dev, LANES).transpose(0, 2, 1, 3)
    return cells.reshape(comp_dev, lat_dev, blocks * LANES)


def total(spans):
    return sum(length for _, length in spans)


def laid(spans):
    at = 0
    for start, length in spans:
        yield at, start, length
        at += length


def load(own, chunks, extra=None):
    spots = [(c, at, start, length) for c, spans in enumerate(chunks) for at, start, length in laid(spans)]
    rows = own.shape[1]
    ends = [total(spans) for spans in chunks]
    sizes = list(ends)
    operands = [own]
    if extra is not None:
        sizes[0] += 1
        sizes.append(1)
        operands.append(extra)

    def kernel(own_ref, *refs):
        sems = refs[-1]
        out_refs = refs[len(operands) - 1:-1]
        copies = [
            pltpu.make_async_copy(own_ref.at[pl.ds(start, length)], out_refs[c].at[pl.ds(at, length)], sems.at[m])
            for m, (c, at, start, length) in enumerate(spots)
        ]
        for one in copies:
            one.start()
        if extra is not None:
            maskf = refs[0][0].astype(jnp.float32)
            out_refs[0][ends[0]] = maskf
            out_refs[-1][0] = maskf
        for one in copies:
            one.wait()

    return pl.pallas_call(
        kernel,
        out_shape=[vmem((size, rows, LANES)) for size in sizes],
        in_specs=[whole(pltpu.HBM)] + [whole(pltpu.VMEM)] * (len(operands) - 1),
        out_specs=[whole(pltpu.VMEM)] * len(sizes),
        scratch_shapes=[pltpu.SemaphoreType.DMA((len(spots),))],
        compiler_params=limits(8),
        cost_estimate=cost(0, 2 * sum(ends) * rows * LANES * 4),
        name="load",
    )(far_from_core(own), *operands[1:])


def pack_first(own, mate, along_lat, place, spans):
    rows = own.shape[1]
    size = total(spans)

    def kernel(a_ref, place_ref, own_ref, mate_ref, out_ref):
        odd = place_ref[0] > 0
        for at, start, length in laid(spans):
            def one(i, carry):
                from_own = (a_ref[start + i] > 0) == odd
                out_ref[at + i] = jnp.where(from_own, own_ref[at + i], mate_ref[at + i])
                return carry

            lax.fori_loop(0, length, one, 0, unroll=8)
        out_ref[size] = own_ref[size]
        out_ref[size + 1] = mate_ref[size]

    return pl.pallas_call(
        kernel,
        out_shape=vmem((size + 2, rows, LANES)),
        in_specs=[whole(pltpu.SMEM)] * 2 + [whole(pltpu.VMEM)] * 2,
        out_specs=whole(pltpu.VMEM),
        compiler_params=limits(8),
        cost_estimate=cost(0, 3 * size * rows * LANES * 4),
        name="pack_first",
    )(along_lat, place, near_core(own), near_core(mate))


def pack_message(own, other, along_lat, place, spans):
    rows = own.shape[1]

    def kernel(a_ref, place_ref, own_ref, other_ref, out_ref, held_ref, sems):
        odd = place_ref[0] > 0
        copies = [
            pltpu.make_async_copy(own_ref.at[pl.ds(start, length)], held_ref.at[pl.ds(at, length)], sems.at[n])
            for n, (at, start, length) in enumerate(laid(spans))
        ]
        for one in copies:
            one.start()
        for n, (at, start, length) in enumerate(laid(spans)):
            copies[n].wait()

            def one(i, carry):
                from_own = (a_ref[start + i] > 0) == odd
                out_ref[at + i] = jnp.where(from_own, held_ref[at + i], other_ref[at + i])
                return carry

            lax.fori_loop(0, length, one, 0, unroll=8)

    shape = (total(spans), rows, LANES)
    return pl.pallas_call(
        kernel,
        out_shape=vmem(shape),
        in_specs=[whole(pltpu.SMEM)] * 2 + [whole(pltpu.HBM), whole(pltpu.VMEM)],
        out_specs=whole(pltpu.VMEM),
        scratch_shapes=[vmem(shape), pltpu.SemaphoreType.DMA((len(spans),))],
        compiler_params=limits(8),
        cost_estimate=cost(0, 3 * total(spans) * rows * LANES * 4),
        name="pack_message",
    )(along_lat, place, far_from_core(own), near_core(other))


def propagate(own, mate, side, hand, along_lat, along_lon, place, masks, spans, skip=0):
    rows = own.shape[1]
    half = rows // PAIR
    size = total(spans)
    count = len(spans)

    def kernel(a_ref, b_ref, place_ref, mask_ref, own_hbm, mate_hbm, side_ref, hand_ref, *refs):
        out_refs = refs[:count]
        own_ref, mate_ref, done_ref, sems, out_sems = refs[count:]
        odd = place_ref[0] > 0
        handed = place_ref[1] > 0
        lane = lax.broadcasted_iota(jnp.int32, (half, LANES), 1)
        sub = lax.broadcasted_iota(jnp.int32, (8, LANES), 0)
        arrivals = [
            [
                pltpu.make_async_copy(src.at[pl.ds(start, length)], dst.at[pl.ds(at, length)], sems.at[n, m])
                for m, (src, dst) in enumerate(((own_hbm, own_ref), (mate_hbm, mate_ref)))
            ]
            for n, (at, start, length) in enumerate(laid(spans))
        ]
        for pair in arrivals:
            for one in pair:
                one.start()
        leaving = [
            pltpu.make_async_copy(done_ref.at[pl.ds(at, length)], out_refs[n], out_sems.at[n])
            for n, (at, start, length) in enumerate(laid(spans))
        ]

        def run(far_ref, at, start, length):
            def row(ref, spot, which):
                return ref[spot, pl.ds(which, half, stride=PAIR), :]

            def prepare(i):
                k = start + i
                j = at + i
                a = a_ref[k]
                b = b_ref[k]
                south = a > 0
                near = south == odd
                west = b > 0
                fore = jnp.where(south, 0, 1)
                back = 1 - fore
                far = skip + j
                return dict(
                    j=j,
                    a=jnp.abs(a),
                    b=jnp.abs(b),
                    keep=1.0 - jnp.abs(a) - jnp.abs(b),
                    west=west,
                    fore=fore,
                    back=back,
                    turn=jnp.where(west, 1, LANES - 1),
                    step=jnp.where(west, 1, 7),
                    first=sub == jnp.where(west, 0, 7),
                    edge=lane == jnp.where(west, 0, LANES - 1),
                    fore_mask=row(mask_ref, 0, fore),
                    back_mask=row(mask_ref, 0, back),
                    halo_mask=row(mask_ref, jnp.where(near, 1, 2), back),
                    x=[
                        jnp.where(near, row(mate_ref, j, fore), row(far_ref, far, fore)),
                        jnp.where(near, row(mate_ref, j, back), row(far_ref, far, back)),
                        row(own_ref, j, fore),
                        row(own_ref, j, back),
                    ],
                )

            def across(c, ahead, behind):
                return ahead if ahead is behind else jnp.where(c["west"], ahead, behind)

            def beside(c, x):
                turned = pltpu.roll(x, c["turn"], 1)
                rolled = [pltpu.roll(turned[8 * t:8 * t + 8], c["step"], 0) for t in range(half // 8)]
                over = [
                    jnp.where(c["first"], across(c, rolled[t - 1], rolled[(t + 1) % len(rolled)]), rolled[t])
                    for t in range(len(rolled))
                ]
                return jnp.where(c["edge"], jnp.concatenate(over, 0), turned)

            def moved(c, x, before, mask):
                return (c["keep"] * x + c["a"] * before + c["b"] * beside(c, x)) * mask

            def early(i):
                c = prepare(i)
                y1 = moved(c, c["x"][1], c["x"][0], c["halo_mask"])
                y2 = moved(c, c["x"][2], c["x"][1], c["fore_mask"])
                y3 = moved(c, c["x"][3], c["x"][2], c["back_mask"])
                return c, y1, y2, y3

            def late(c, y1, y2, y3):
                done_ref[c["j"], pl.ds(c["fore"], half, stride=PAIR), :] = moved(c, y2, y1, c["fore_mask"])
                done_ref[c["j"], pl.ds(c["back"], half, stride=PAIR), :] = moved(c, y3, y2, c["back_mask"])

            def some(group, carry):
                held = early(group * GROUP)
                for u in range(1, GROUP):
                    following = early(group * GROUP + u)
                    late(*held)
                    held = following
                late(*held)
                return carry

            lax.fori_loop(0, length // GROUP, some, 0)

        for n, span in enumerate(laid(spans)):
            for one in arrivals[n]:
                one.wait()

            @pl.when(handed)
            def _():
                run(hand_ref, *span)

            @pl.when(jnp.logical_not(handed))
            def _():
                run(side_ref, *span)

            leaving[n].start()
        for one in leaving:
            one.wait()

    return pl.pallas_call(
        kernel,
        out_shape=[jax.ShapeDtypeStruct((length, rows, LANES), jnp.float32) for _, length in spans],
        in_specs=[whole(pltpu.SMEM)] * 3 + [whole(pltpu.VMEM)] + [whole(pltpu.HBM), whole(pl.ANY)]
        + [whole(pltpu.VMEM)] * 2,
        out_specs=[whole(pltpu.HBM)] * count,
        scratch_shapes=[vmem((size, rows, LANES))] * 3
        + [pltpu.SemaphoreType.DMA((count, 2)), pltpu.SemaphoreType.DMA((count,))],
        compiler_params=limits(8),
        cost_estimate=cost(40 * size * rows * LANES, 5 * size * rows * LANES * 4),
        name="propagate",
    )(
        along_lat, along_lon, place, near_core(masks),
        far_from_core(own), mate, near_core(side), near_core(hand),
    )


def quadruplets(window, parts, places, local, strength, shifts, first, freqs, into):
    rows = parts[0].shape[1]
    count = len(parts)

    def kernel(strength_ref, shift_ref, first_ref, *refs):
        part_refs = refs[:count]
        held_ref, out_ref, done, sems, part_sems = refs[-5:]
        arrivals = [
            pltpu.make_async_copy(part_refs[n], held_ref.at[pl.ds(place, parts[n].shape[0])], part_sems.at[n])
            for n, place in enumerate(places)
        ]
        for one in arrivals:
            one.start()
        for one in arrivals:
            one.wait()
        base = first_ref[0]
        turns = [shift_ref[1, q] for q in range(NQ)]
        copies = []
        for n, f in enumerate(freqs):
            bases = [(f + reach + shift_ref[0, q]) * ND for q in range(NQ)]

            def some(group, carry):
                made = []
                for u in range(GROUP):
                    d = group * GROUP + u
                    energy = held_ref[(f + reach) * ND + d]
                    summed = jnp.zeros_like(energy)
                    for q in range(NQ):
                        partner = held_ref[bases[q] + jnp.bitwise_and(d + turns[q], ND - 1)]
                        summed = summed + partner * (partner - energy)
                    made.append(energy + strength_ref[base + f * ND + d] * energy * summed)
                for u, one in enumerate(made):
                    done[n * ND + group * GROUP + u] = one
                return carry

            lax.fori_loop(0, ND // GROUP, some, 0)
            copies.append(
                pltpu.make_async_copy(done.at[pl.ds(n * ND, ND)], out_ref.at[pl.ds(f * ND, ND)], sems.at[n])
            )
            copies[-1].start()
        for one in copies:
            one.wait()

    operands = [strength, shifts, first] + parts
    in_specs = [whole(pltpu.SMEM)] * 3 + [whole(pl.ANY)] * count
    aliases = {}
    if window is not None:
        aliases = {len(operands): 0, len(operands) + 1: 1}
        operands += [near_core(window), into]
        in_specs += [whole(pltpu.VMEM), whole(pl.ANY)]
    return pl.pallas_call(
        kernel,
        out_shape=[
            vmem(((local + 2 * reach) * ND, rows, LANES)),
            jax.ShapeDtypeStruct((local * ND, rows, LANES), jnp.float32),
        ],
        in_specs=in_specs,
        out_specs=[whole(pltpu.VMEM), whole(pl.ANY)],
        scratch_shapes=[
            pltpu.VMEM((len(freqs) * ND, rows, LANES), jnp.float32),
            pltpu.SemaphoreType.DMA((len(freqs),)),
            pltpu.SemaphoreType.DMA((count,)),
        ],
        input_output_aliases=aliases,
        compiler_params=limits(8),
        cost_estimate=cost(15 * len(freqs) * ND * rows * LANES, 6 * len(freqs) * ND * rows * LANES * 4),
        name="quadruplets",
    )(*operands)


def halo_plan(spectrum, courant_lat, courant_lon, sea_mask, strength, quad_shift):
    comp_dev, lat_dev, _ = spectrum.shape
    local = comp_dev // ND
    lat_count = lax.axis_size("lat")
    comp_count = lax.axis_size("comp")
    at = lax.axis_index("lat")
    first = (lax.axis_index("comp") * comp_dev)[None].astype(jnp.int32)
    mates = [(i, i ^ 1) for i in range(lat_count)]
    corners = range(3, lat_count - 1, 4)
    sides = [(i, i + 1) for i in range(1, lat_count, 4)] + [(i + 1, i) for i in range(1, lat_count, 4)]
    relays = [(i - 2, i + 1) for i in corners] + [(i + 3, i) for i in corners]
    aheads = [(i, i + 3) for i in corners] + [(i + 1, i - 2) for i in corners]
    hands = [(i + 2, i + 1) for i in corners] + [(i - 1, i) for i in corners]
    handed = (at % 4 == 0) | (at % 4 == 3)
    place = jnp.stack([at % 2, jnp.where(handed, 1, 0)]).astype(jnp.int32)
    z_up = [(i, i + 1) for i in range(comp_count - 1)]
    z_down = [(i + 1, i) for i in range(comp_count - 1)]

    own = tiled(spectrum)
    mask = tiled(sea_mask[None])

    edge = reach * ND
    cuts = [edge * cut // 16 for cut in CUTS]
    chunks = [[(low, high - low), (comp_dev - high, high - low)] for low, high in zip(cuts, cuts[1:])]
    middle = [(edge, comp_dev - 2 * edge)]
    lots = chunks[:-1] + [chunks[-1] + middle]
    head, part, maskf = load(own, lots[:2], mask)
    mate_head = lax.ppermute(head, "lat", mates)
    ahead = [None, lax.ppermute(part, "lat", aheads)]
    sides_in = [lax.ppermute(pack_first(head, mate_head, courant_lat, place, chunks[0]), "lat", sides)]
    hands_in = [lax.ppermute(sides_in[0], "lat", relays)]
    rest = load(own, lots[2:])
    ahead += [lax.ppermute(part, "lat", aheads) for part in rest]
    mate = lax.ppermute(own, "lat", mates)
    for n, spans in enumerate(lots):
        if n:
            message = pack_message(own, ahead[n], courant_lat, place, spans)
            sides_in.append(lax.ppermute(message, "lat", sides))
            hands_in.append(lax.ppermute(sides_in[n], "lat", hands))
    size = total(chunks[0])
    far_mask = jnp.where(handed, hands_in[0][size + 1:], sides_in[0][size:size + 1])
    masks = jnp.concatenate([maskf, mate_head[size:], far_mask])
    parts = []
    places = []
    last = []
    for n, spans in enumerate(chunks):
        low, high = propagate(
            own, far_from_core(mate) if n else mate, sides_in[n], hands_in[n],
            courant_lat, courant_lon, place, masks, spans,
        )
        parts += [low, high]
        places += [edge + start for start, _ in spans]
        last = [lax.ppermute(high, "comp", z_up), lax.ppermute(low, "comp", z_down)]
        last_places = [edge + spans[1][0] - comp_dev, edge + comp_dev + spans[0][0]]
        if n < len(chunks) - 1:
            parts += last
            places += last_places
    parts += propagate(
        own, far_from_core(mate), sides_in[-1], hands_in[-1],
        courant_lat, courant_lon, place, masks, middle, skip=total(chunks[-1]),
    )
    places += [edge + start for start, _ in middle]
    shifts = quad_shift.T
    late = -(-chunks[-1][0][1] // ND)
    rims = list(range(late)) + list(range(local - late, local))
    window, inner = quadruplets(
        None, parts, places, local, strength, shifts, first, list(range(late, local - late)), None
    )
    window, result = quadruplets(window, last, last_places, local, strength, shifts, first, rims, inner)
    return untiled(result, lat_dev)


def fits(comp_dev, lat_count, lat_dev, lon_count):
    local, left = divmod(comp_dev, ND)
    return left == 0 and 0 < local - 2 * reach <= 1 and lat_count % 4 == 0 and lat_dev == 2 and lon_count % LANES == 0


def per_device(spectrum, courant_lat, courant_lon, sea_mask, strength, quad_shift):
    comp_dev, lat_dev, lon_count = spectrum.shape
    if fits(comp_dev, lax.axis_size("lat"), lat_dev, lon_count):
        return halo_plan(spectrum, courant_lat, courant_lon, sea_mask, strength, quad_shift)
    return gathered_plan(spectrum, courant_lat, courant_lon, sea_mask, strength, quad_shift)


def solution(mesh):
    return jax.shard_map(
        per_device,
        mesh=mesh,
        in_specs=(P("comp", "lat", None), P("comp"), P("comp"), P("lat", None), P(), P()),
        out_specs=P("comp", "lat", None),
        check_vma=False,
    )
```

```python
import jax
import jax.numpy as jnp
from jax import lax
from jax.sharding import PartitionSpec as P
from jax.experimental import pallas as pl
from jax.experimental.pallas import tpu as pltpu

NF = 36
ND = 32
NQ = 4


reach = 4


def extended(cells, sides, width):
    for axis, dim in sides:
        count = lax.axis_size(axis)
        ends = count - 1
        head = lax.slice_in_dim(cells, 0, width, axis=dim)
        tail = lax.slice_in_dim(cells, cells.shape[dim] - width, cells.shape[dim], axis=dim)
        cells = jnp.concatenate(
            [
                lax.ppermute(tail, axis, [(i, (i + 1) % count) for i in range(ends)]),
                cells,
                lax.ppermute(head, axis, [((i + 1) % count, i) for i in range(ends)]),
            ],
            axis=dim,
        )
    return cells


def upwind(field, along_lat, along_lon, maskf):
    padded = extended(field, (("lat", 1),), 1)
    south = padded[:, :-2, :]
    north = padded[:, 2:, :]
    west = jnp.roll(field, 1, axis=2)
    east = jnp.roll(field, -1, axis=2)
    plus_a = jnp.maximum(along_lat, 0.0)
    minus_a = jnp.minimum(along_lat, 0.0)
    plus_b = jnp.maximum(along_lon, 0.0)
    minus_b = jnp.minimum(along_lon, 0.0)
    moved = field - plus_a * (field - south) - minus_a * (north - field)
    moved = moved - plus_b * (field - west) - minus_b * (east - field)
    return moved * maskf


def interact(energy, strength, quad_shift):
    rest = energy.shape[1:]
    grid = energy.reshape((NF, ND) + rest)
    widths = ((reach, reach),) + ((0, 0),) * (grid.ndim - 1)
    padded = jnp.pad(grid, widths)
    total = jnp.zeros(grid.shape, jnp.float32)
    for index in range(NQ):
        offset_f = quad_shift[index, 0]
        offset_d = quad_shift[index, 1]
        partner = lax.dynamic_slice_in_dim(padded, reach + offset_f, NF, 0)
        partner = jnp.roll(partner, -offset_d, axis=1)
        total = total + partner * (partner - grid)
    coeff = strength.reshape((NF, ND) + (1,) * len(rest))
    return (coeff * grid * total).reshape(energy.shape)


def gathered_plan(spectrum, courant_lat, courant_lon, sea_mask, strength, quad_shift):
    maskf = sea_mask.astype(jnp.float32)[None]
    along_lat = courant_lat[:, None, None]
    along_lon = courant_lon[:, None, None]
    field = upwind(spectrum, along_lat, along_lon, maskf)
    field = upwind(field, along_lat, along_lon, maskf)
    comp_dev, lat_dev, lon_count = field.shape
    point_count = lat_dev * lon_count
    flat = field.reshape(comp_dev, point_count)
    sea_most = 3 * point_count // 4
    land_first = 1 - sea_mask.reshape(point_count)
    ordering = jnp.argsort(land_first, stable=True)
    chosen = ordering[:sea_most]
    packed = jnp.take(flat, chosen, axis=1)
    spectra = lax.all_to_all(packed, "comp", split_axis=1, concat_axis=0, tiled=True)
    updated = spectra + interact(spectra, strength, quad_shift)
    returned = lax.all_to_all(updated, "comp", split_axis=0, concat_axis=1, tiled=True)
    result = jnp.zeros((comp_dev, point_count), jnp.float32).at[:, chosen].set(returned)
    return result.reshape(comp_dev, lat_dev, lon_count)


LANES = 128
PAIR = 2
GROUP = 8
CUTS = (0, 4, 9, 13, 16)


def vmem(shape):
    return pltpu.VMEM(shape, jnp.float32)


def near_core(cells):
    return pltpu.with_memory_space_constraint(cells, pltpu.VMEM)


def far_from_core(cells):
    return pltpu.with_memory_space_constraint(cells, pltpu.HBM)


def whole(space):
    return pl.BlockSpec(memory_space=space)


def limits(mib):
    return pltpu.CompilerParams(vmem_limit_bytes=mib * 2**20)


def cost(flops, count):
    return pl.CostEstimate(flops=flops, bytes_accessed=count, transcendentals=0)


def tiled(cells):
    comp_dev, lat_dev, lon_count = cells.shape
    blocks = lon_count // LANES
    cells = cells.reshape(comp_dev, lat_dev, blocks, LANES).transpose(0, 2, 1, 3)
    return cells.reshape(comp_dev, blocks * lat_dev, LANES)


def untiled(cells, lat_dev):
    comp_dev, rows, _ = cells.shape
    blocks = rows // lat_dev
    cells = cells.reshape(comp_dev, blocks, lat_dev, LANES).transpose(0, 2, 1, 3)
    return cells.reshape(comp_dev, lat_dev, blocks * LANES)


def total(spans):
    return sum(length for _, length in spans)


def laid(spans):
    at = 0
    for start, length in spans:
        yield at, start, length
        at += length


def load(own, chunks, extra=None):
    spots = [(c, at, start, length) for c, spans in enumerate(chunks) for at, start, length in laid(spans)]
    rows = own.shape[1]
    ends = [total(spans) for spans in chunks]
    sizes = list(ends)
    operands = [own]
    if extra is not None:
        sizes[0] += 1
        sizes.append(1)
        operands.append(extra)

    def kernel(own_ref, *refs):
        sems = refs[-1]
        out_refs = refs[len(operands) - 1:-1]
        copies = [
            pltpu.make_async_copy(own_ref.at[pl.ds(start, length)], out_refs[c].at[pl.ds(at, length)], sems.at[m])
            for m, (c, at, start, length) in enumerate(spots)
        ]
        for one in copies:
            one.start()
        if extra is not None:
            maskf = refs[0][0].astype(jnp.float32)
            out_refs[0][ends[0]] = maskf
            out_refs[-1][0] = maskf
        for one in copies:
            one.wait()

    return pl.pallas_call(
        kernel,
        out_shape=[vmem((size, rows, LANES)) for size in sizes],
        in_specs=[whole(pltpu.HBM)] + [whole(pltpu.VMEM)] * (len(operands) - 1),
        out_specs=[whole(pltpu.VMEM)] * len(sizes),
        scratch_shapes=[pltpu.SemaphoreType.DMA((len(spots),))],
        compiler_params=limits(8),
        cost_estimate=cost(0, 2 * sum(ends) * rows * LANES * 4),
        name="load",
    )(far_from_core(own), *operands[1:])


def pack_first(own, mate, along_lat, place, spans):
    rows = own.shape[1]
    size = total(spans)

    def kernel(a_ref, place_ref, own_ref, mate_ref, out_ref):
        odd = place_ref[0] > 0
        for at, start, length in laid(spans):
            def one(i, carry):
                from_own = (a_ref[start + i] > 0) == odd
                out_ref[at + i] = jnp.where(from_own, own_ref[at + i], mate_ref[at + i])
                return carry

            lax.fori_loop(0, length, one, 0, unroll=8)
        out_ref[size] = own_ref[size]
        out_ref[size + 1] = mate_ref[size]

    return pl.pallas_call(
        kernel,
        out_shape=vmem((size + 2, rows, LANES)),
        in_specs=[whole(pltpu.SMEM)] * 2 + [whole(pltpu.VMEM)] * 2,
        out_specs=whole(pltpu.VMEM),
        compiler_params=limits(8),
        cost_estimate=cost(0, 3 * size * rows * LANES * 4),
        name="pack_first",
    )(along_lat, place, near_core(own), near_core(mate))


def pack_message(own, other, along_lat, place, spans):
    rows = own.shape[1]

    def kernel(a_ref, place_ref, own_ref, other_ref, out_ref, held_ref, sems):
        odd = place_ref[0] > 0
        copies = [
            pltpu.make_async_copy(own_ref.at[pl.ds(start, length)], held_ref.at[pl.ds(at, length)], sems.at[n])
            for n, (at, start, length) in enumerate(laid(spans))
        ]
        for one in copies:
            one.start()
        for n, (at, start, length) in enumerate(laid(spans)):
            copies[n].wait()

            def one(i, carry):
                from_own = (a_ref[start + i] > 0) == odd
                out_ref[at + i] = jnp.where(from_own, held_ref[at + i], other_ref[at + i])
                return carry

            lax.fori_loop(0, length, one, 0, unroll=8)

    shape = (total(spans), rows, LANES)
    return pl.pallas_call(
        kernel,
        out_shape=vmem(shape),
        in_specs=[whole(pltpu.SMEM)] * 2 + [whole(pltpu.HBM), whole(pltpu.VMEM)],
        out_specs=whole(pltpu.VMEM),
        scratch_shapes=[vmem(shape), pltpu.SemaphoreType.DMA((len(spans),))],
        compiler_params=limits(8),
        cost_estimate=cost(0, 3 * total(spans) * rows * LANES * 4),
        name="pack_message",
    )(along_lat, place, far_from_core(own), near_core(other))


def propagate(own, mate, side, hand, along_lat, along_lon, place, masks, spans, skip=0):
    rows = own.shape[1]
    half = rows // PAIR
    size = total(spans)
    count = len(spans)

    def kernel(a_ref, b_ref, place_ref, mask_ref, own_hbm, mate_hbm, side_ref, hand_ref, *refs):
        out_refs = refs[:count]
        own_ref, mate_ref, done_ref, sems, out_sems = refs[count:]
        odd = place_ref[0] > 0
        handed = place_ref[1] > 0
        lane = lax.broadcasted_iota(jnp.int32, (half, LANES), 1)
        sub = lax.broadcasted_iota(jnp.int32, (8, LANES), 0)
        arrivals = [
            [
                pltpu.make_async_copy(src.at[pl.ds(start, length)], dst.at[pl.ds(at, length)], sems.at[n, m])
                for m, (src, dst) in enumerate(((own_hbm, own_ref), (mate_hbm, mate_ref)))
            ]
            for n, (at, start, length) in enumerate(laid(spans))
        ]
        for pair in arrivals:
            for one in pair:
                one.start()
        leaving = [
            pltpu.make_async_copy(done_ref.at[pl.ds(at, length)], out_refs[n], out_sems.at[n])
            for n, (at, start, length) in enumerate(laid(spans))
        ]

        def run(far_ref, at, start, length):
            def row(ref, spot, which):
                return ref[spot, pl.ds(which, half, stride=PAIR), :]

            def prepare(i):
                k = start + i
                j = at + i
                a = a_ref[k]
                b = b_ref[k]
                south = a > 0
                near = south == odd
                west = b > 0
                fore = jnp.where(south, 0, 1)
                back = 1 - fore
                far = skip + j
                return dict(
                    j=j,
                    a=jnp.abs(a),
                    b=jnp.abs(b),
                    keep=1.0 - jnp.abs(a) - jnp.abs(b),
                    west=west,
                    fore=fore,
                    back=back,
                    turn=jnp.where(west, 1, LANES - 1),
                    step=jnp.where(west, 1, 7),
                    first=sub == jnp.where(west, 0, 7),
                    edge=lane == jnp.where(west, 0, LANES - 1),
                    fore_mask=row(mask_ref, 0, fore),
                    back_mask=row(mask_ref, 0, back),
                    halo_mask=row(mask_ref, jnp.where(near, 1, 2), back),
                    x=[
                        jnp.where(near, row(mate_ref, j, fore), row(far_ref, far, fore)),
                        jnp.where(near, row(mate_ref, j, back), row(far_ref, far, back)),
                        row(own_ref, j, fore),
                        row(own_ref, j, back),
                    ],
                )

            def across(c, ahead, behind):
                return ahead if ahead is behind else jnp.where(c["west"], ahead, behind)

            def beside(c, x):
                turned = pltpu.roll(x, c["turn"], 1)
                rolled = [pltpu.roll(turned[8 * t:8 * t + 8], c["step"], 0) for t in range(half // 8)]
                over = [
                    jnp.where(c["first"], across(c, rolled[t - 1], rolled[(t + 1) % len(rolled)]), rolled[t])
                    for t in range(len(rolled))
                ]
                return jnp.where(c["edge"], jnp.concatenate(over, 0), turned)

            def moved(c, x, before, mask):
                return (c["keep"] * x + c["a"] * before + c["b"] * beside(c, x)) * mask

            def early(i):
                c = prepare(i)
                y1 = moved(c, c["x"][1], c["x"][0], c["halo_mask"])
                y2 = moved(c, c["x"][2], c["x"][1], c["fore_mask"])
                y3 = moved(c, c["x"][3], c["x"][2], c["back_mask"])
                return c, y1, y2, y3

            def late(c, y1, y2, y3):
                done_ref[c["j"], pl.ds(c["fore"], half, stride=PAIR), :] = moved(c, y2, y1, c["fore_mask"])
                done_ref[c["j"], pl.ds(c["back"], half, stride=PAIR), :] = moved(c, y3, y2, c["back_mask"])

            def some(group, carry):
                held = early(group * GROUP)
                for u in range(1, GROUP):
                    following = early(group * GROUP + u)
                    late(*held)
                    held = following
                late(*held)
                return carry

            lax.fori_loop(0, length // GROUP, some, 0)

        for n, span in enumerate(laid(spans)):
            for one in arrivals[n]:
                one.wait()

            @pl.when(handed)
            def _():
                run(hand_ref, *span)

            @pl.when(jnp.logical_not(handed))
            def _():
                run(side_ref, *span)

            leaving[n].start()
        for one in leaving:
            one.wait()

    return pl.pallas_call(
        kernel,
        out_shape=[jax.ShapeDtypeStruct((length, rows, LANES), jnp.float32) for _, length in spans],
        in_specs=[whole(pltpu.SMEM)] * 3 + [whole(pltpu.VMEM)] + [whole(pltpu.HBM), whole(pl.ANY)]
        + [whole(pltpu.VMEM)] * 2,
        out_specs=[whole(pltpu.HBM)] * count,
        scratch_shapes=[vmem((size, rows, LANES))] * 3
        + [pltpu.SemaphoreType.DMA((count, 2)), pltpu.SemaphoreType.DMA((count,))],
        compiler_params=limits(8),
        cost_estimate=cost(40 * size * rows * LANES, 5 * size * rows * LANES * 4),
        name="propagate",
    )(
        along_lat, along_lon, place, near_core(masks),
        far_from_core(own), mate, near_core(side), near_core(hand),
    )


def quadruplets(window, parts, places, local, strength, shifts, first, freqs, into):
    rows = parts[0].shape[1]
    count = len(parts)

    def kernel(strength_ref, shift_ref, first_ref, *refs):
        part_refs = refs[:count]
        held_ref, out_ref, done, sems, part_sems = refs[-5:]
        arrivals = [
            pltpu.make_async_copy(part_refs[n], held_ref.at[pl.ds(place, parts[n].shape[0])], part_sems.at[n])
            for n, place in enumerate(places)
        ]
        waiting = sorted(range(count), key=lambda n: places[n])
        for n in waiting:
            arrivals[n].start()
        base = first_ref[0]
        turns = [shift_ref[1, q] for q in range(NQ)]
        copies = []
        for n, f in enumerate(freqs):
            while waiting and places[waiting[0]] < (f + 2 * reach + 1) * ND:
                arrivals[waiting.pop(0)].wait()
            bases = [(f + reach + shift_ref[0, q]) * ND for q in range(NQ)]

            def some(group, carry):
                made = []
                for u in range(GROUP):
                    d = group * GROUP + u
                    energy = held_ref[(f + reach) * ND + d]
                    summed = jnp.zeros_like(energy)
                    for q in range(NQ):
                        partner = held_ref[bases[q] + jnp.bitwise_and(d + turns[q], ND - 1)]
                        summed = summed + partner * (partner - energy)
                    made.append(energy + strength_ref[base + f * ND + d] * energy * summed)
                for u, one in enumerate(made):
                    done[n * ND + group * GROUP + u] = one
                return carry

            lax.fori_loop(0, ND // GROUP, some, 0)
            copies.append(
                pltpu.make_async_copy(done.at[pl.ds(n * ND, ND)], out_ref.at[pl.ds(f * ND, ND)], sems.at[n])
            )
            copies[-1].start()
        for n in waiting:
            arrivals[n].wait()
        for one in copies:
            one.wait()

    operands = [strength, shifts, first] + parts
    in_specs = [whole(pltpu.SMEM)] * 3 + [whole(pl.ANY)] * count
    aliases = {}
    if window is not None:
        aliases = {len(operands): 0, len(operands) + 1: 1}
        operands += [near_core(window), into]
        in_specs += [whole(pltpu.VMEM), whole(pl.ANY)]
    return pl.pallas_call(
        kernel,
        out_shape=[
            vmem(((local + 2 * reach) * ND, rows, LANES)),
            jax.ShapeDtypeStruct((local * ND, rows, LANES), jnp.float32),
        ],
        in_specs=in_specs,
        out_specs=[whole(pltpu.VMEM), whole(pl.ANY)],
        scratch_shapes=[
            pltpu.VMEM((len(freqs) * ND, rows, LANES), jnp.float32),
            pltpu.SemaphoreType.DMA((len(freqs),)),
            pltpu.SemaphoreType.DMA((count,)),
        ],
        input_output_aliases=aliases,
        compiler_params=limits(8),
        cost_estimate=cost(15 * len(freqs) * ND * rows * LANES, 6 * len(freqs) * ND * rows * LANES * 4),
        name="quadruplets",
    )(*operands)


def halo_plan(spectrum, courant_lat, courant_lon, sea_mask, strength, quad_shift):
    comp_dev, lat_dev, _ = spectrum.shape
    local = comp_dev // ND
    lat_count = lax.axis_size("lat")
    comp_count = lax.axis_size("comp")
    at = lax.axis_index("lat")
    first = (lax.axis_index("comp") * comp_dev)[None].astype(jnp.int32)
    mates = [(i, i ^ 1) for i in range(lat_count)]
    corners = range(3, lat_count - 1, 4)
    sides = [(i, i + 1) for i in range(1, lat_count, 4)] + [(i + 1, i) for i in range(1, lat_count, 4)]
    relays = [(i - 2, i + 1) for i in corners] + [(i + 3, i) for i in corners]
    aheads = [(i, i + 3) for i in corners] + [(i + 1, i - 2) for i in corners]
    hands = [(i + 2, i + 1) for i in corners] + [(i - 1, i) for i in corners]
    handed = (at % 4 == 0) | (at % 4 == 3)
    place = jnp.stack([at % 2, jnp.where(handed, 1, 0)]).astype(jnp.int32)
    z_up = [(i, i + 1) for i in range(comp_count - 1)]
    z_down = [(i + 1, i) for i in range(comp_count - 1)]

    own = tiled(spectrum)
    mask = tiled(sea_mask[None])

    edge = reach * ND
    cuts = [edge * cut // 16 for cut in CUTS]
    chunks = [[(low, high - low), (comp_dev - high, high - low)] for low, high in zip(cuts, cuts[1:])]
    middle = [(edge, comp_dev - 2 * edge)]
    lots = chunks[:-1] + [chunks[-1] + middle]
    head, part, maskf = load(own, lots[:2], mask)
    mate_head = lax.ppermute(head, "lat", mates)
    ahead = [None, lax.ppermute(part, "lat", aheads)]
    sides_in = [lax.ppermute(pack_first(head, mate_head, courant_lat, place, chunks[0]), "lat", sides)]
    hands_in = [lax.ppermute(sides_in[0], "lat", relays)]
    rest = load(own, lots[2:])
    ahead += [lax.ppermute(part, "lat", aheads) for part in rest]
    mate = lax.ppermute(own, "lat", mates)
    for n, spans in enumerate(lots):
        if n:
            message = pack_message(own, ahead[n], courant_lat, place, spans)
            sides_in.append(lax.ppermute(message, "lat", sides))
            hands_in.append(lax.ppermute(sides_in[n], "lat", hands))
    size = total(chunks[0])
    far_mask = jnp.where(handed, hands_in[0][size + 1:], sides_in[0][size:size + 1])
    masks = jnp.concatenate([maskf, mate_head[size:], far_mask])
    parts = []
    places = []
    last = []
    for n, spans in enumerate(chunks):
        low, high = propagate(
            own, far_from_core(mate) if n else mate, sides_in[n], hands_in[n],
            courant_lat, courant_lon, place, masks, spans,
        )
        parts += [low, high]
        places += [edge + start for start, _ in spans]
        last = [lax.ppermute(high, "comp", z_up), lax.ppermute(low, "comp", z_down)]
        last_places = [edge + spans[1][0] - comp_dev, edge + comp_dev + spans[0][0]]
        if n < len(chunks) - 1:
            parts += last
            places += last_places
    parts += propagate(
        own, far_from_core(mate), sides_in[-1], hands_in[-1],
        courant_lat, courant_lon, place, masks, middle, skip=total(chunks[-1]),
    )
    places += [edge + start for start, _ in middle]
    shifts = quad_shift.T
    late = -(-chunks[-1][0][1] // ND)
    rims = list(range(late)) + list(range(local - late, local))
    window, inner = quadruplets(
        None, parts, places, local, strength, shifts, first, list(range(late, local - late)), None
    )
    window, result = quadruplets(window, last, last_places, local, strength, shifts, first, rims, inner)
    return untiled(result, lat_dev)


def fits(comp_dev, lat_count, lat_dev, lon_count):
    local, left = divmod(comp_dev, ND)
    return left == 0 and 0 < local - 2 * reach <= 1 and lat_count % 4 == 0 and lat_dev == 2 and lon_count % LANES == 0


def per_device(spectrum, courant_lat, courant_lon, sea_mask, strength, quad_shift):
    comp_dev, lat_dev, lon_count = spectrum.shape
    if fits(comp_dev, lax.axis_size("lat"), lat_dev, lon_count):
        return halo_plan(spectrum, courant_lat, courant_lon, sea_mask, strength, quad_shift)
    return gathered_plan(spectrum, courant_lat, courant_lon, sea_mask, strength, quad_shift)


def solution(mesh):
    return jax.shard_map(
        per_device,
        mesh=mesh,
        in_specs=(P("comp", "lat", None), P("comp"), P("comp"), P("lat", None), P(), P()),
        out_specs=P("comp", "lat", None),
        check_vma=False,
    )
```
